32 devices in a mesh: tm: 8 (over z, x), chan: 4 (over y, core).
Axes of the slice: x: 2, y: 2, z: 4, core: 2. Of those that a mesh axis runs over, the one named last changes fastest.
Arguments:
- inputs: bfloat16 [2048, 2048], P('tm'), may hold values from -6 to 6
- cotangent: bfloat16 [2048, 2048], P('tm'), may hold values from -6 to 6
- in_proj: bfloat16 [2048, 4096], P(None, 'chan'), may hold values from -0.125 to 0.125
- out_proj: bfloat16 [4096, 2048], P('chan'), may hold values from -0.09375 to 0.09375
- decays: float32 [4096], P('chan'), may hold values from 0 to 1, as said below
- input_scale: float32 [4096], P('chan'), may hold values from 0 to 1.5, as said below
- retain: float32 [2048], P('tm'), may hold values from 0.5 to 1, as said below
Outputs:
- in_proj_grad: float32 [2048, 4096], P('tm', 'chan')
- out_proj_grad: float32 [2048, 4096], P('tm', 'chan')
- decay_grad: float32 [4096], P('chan')
- input_grad: bfloat16 [2048, 2048], P('tm', 'chan')
The draws below stay inside these ranges and needn't reach their ends.
Inputs may be any that keep to these rules, and one draw needn't show every extreme that they name: `decays`: each decay lies strictly between 0 and 1. `input_scale`: positive. `retain`: most steps have factor 1.
All inputs are finite; a program needn't handle non-finite values.
Results may differ from the reference program's by a relative error of at most 0.0049.
Values sent between devices are 32-bit elements; how exact they have to be, the bound alone decides.
No kernel may reach another device: no remote copies, remote signals or barrier semaphores. Data moves between devices by JAX's collectives and lax.ppermute only.
A program may use at most 128 MiB of HBM per device.

```python
import math
import jax
import jax.numpy as jnp
from jax import lax

D = 2048
S = 4096
TOK_DEV = 256
TOKENS = 2048


def channel_rates(key, slow_share):
    pick_key, slow_key, fast_key = jax.random.split(jax.random.fold_in(key, 7), 3)
    slow = jnp.exp(jax.random.uniform(slow_key, (S,), jnp.float32, math.log(0.2 / TOKENS), math.log(2.0 / TOKENS)))
    fast = jnp.exp(jax.random.uniform(fast_key, (S,), jnp.float32, math.log(2.0 / TOKENS), math.log(1.0 / 30.0)))
    return jnp.where(jax.random.uniform(pick_key, (S,), jnp.float32) < slow_share, slow, fast)


def draw_decays(key, part):
    rates = channel_rates(key, 0.5)
    return jnp.exp(-rates).astype(jnp.float32)


def draw_input_scale(key, part):
    rates = channel_rates(key, 0.5)
    spread = jax.random.uniform(jax.random.fold_in(key, 11), (S,), jnp.float32, 0.7, 1.4)
    return (jnp.sqrt(-jnp.expm1(-2.0 * rates)) * spread).astype(jnp.float32)


def draw_retain(key, part):
    first_key, second_key = jax.random.split(jax.random.fold_in(key, 5))
    hits = jax.random.uniform(first_key, (TOKENS,), jnp.float32) < 8.0 / TOKENS
    levels = jax.random.uniform(second_key, (TOKENS,), jnp.float32, 0.5, 0.8)
    return jnp.where(hits, levels, 1.0).astype(jnp.float32)


def raised(entries, rng, source, target, parts, factor):
    def block_of(dim):
        return (jnp.arange(entries.shape[dim]) // (entries.shape[dim] // parts)).reshape((-1,) + (1,) * (entries.ndim - 1 - dim))

    near = jax.random.permutation(rng, parts)[block_of(target)]
    second = (block_of(target) + parts // 2) % parts
    return jnp.where((block_of(source) == near) | (block_of(source) == second), factor * entries, entries)


def shard_levels(own_key, shape, pieces, smallest, largest):
    loudness, own = 1.0, jax.random.fold_in(own_key, 6)
    for axis_at, blocks in pieces:
        heights = jnp.exp(jax.random.uniform(jax.random.fold_in(own, axis_at), (blocks,), jnp.float32, smallest / len(pieces), largest / len(pieces)))
        loudness = loudness * jnp.repeat(heights, shape[axis_at] // blocks).reshape([-1 if axis == axis_at else 1 for axis in range(len(shape))])
    return loudness


def normal_values(own_key, extent, scale, limit, shards=(), kind=jnp.bfloat16):
    array = scale * jax.random.normal(own_key, extent, jnp.float32)
    if shards:
        array = array * shard_levels(own_key, extent, shards, -0.22, 0.18)
    return jnp.clip(array, -limit, limit).astype(kind)


def noise_with(rng, shape, scale, most, cuts, heavy, dtype=jnp.bfloat16):
    array = scale * jax.random.normal(rng, shape, jnp.float32)
    if cuts:
        array = array * shard_levels(rng, shape, cuts, -0.22, 0.18)
    return jnp.clip(raised(array, jax.random.fold_in(rng, 3), *heavy), -most, most).astype(dtype)


def setup_inputs(seed: int = 0) -> dict:
    key_list = jax.random.split(jax.random.key(seed), 8)
    return {
        "inputs": noise_with(key_list[0], (TOKENS, D), 1.0, 6.0, ((0, 8),), (0, 1, 8, 2.0)),
        "cotangent": noise_with(key_list[1], (TOKENS, D), 1.0, 6.0, ((0, 8),), (0, 1, 8, 2.0)),
        "in_proj": normal_values(key_list[2], (D, S), D ** -0.5, 0.125, ((1, 4),)),
        "out_proj": normal_values(key_list[3], (S, D), S ** -0.5, 0.09375, ((0, 4),)),
        "decays": draw_decays(jax.random.fold_in(key_list[7], 71), 0),
        "input_scale": draw_input_scale(jax.random.fold_in(key_list[7], 71), 0),
        "retain": draw_retain(jax.random.fold_in(key_list[7], 71), 0),
    }


def reference(inputs, cotangent, in_proj, out_proj, decays, input_scale, retain):
    blocks = TOKENS // TOK_DEV
    scaling = 1.0 / math.sqrt(TOKENS)
    in_blocks = inputs.reshape(blocks, TOK_DEV, D)
    cot_blocks = cotangent.reshape(blocks, TOK_DEV, D)
    keep_blocks = retain.reshape(blocks, TOK_DEV)

    def advance(hidden_state, entry_pair):
        driven, factor = entry_pair
        hidden_state = decays * factor * hidden_state + driven
        return (hidden_state, hidden_state)

    def forward_block(carried, block_pair):
        tok_rows, kept_part = block_pair
        driving = jnp.dot(tok_rows, in_proj, preferred_element_type=jnp.float32) * input_scale
        final_state, _ = lax.scan(advance, carried, (driving, kept_part))
        return (final_state, carried)
    _, starts = lax.scan(forward_block, jnp.zeros((S,), jnp.float32), (in_blocks, keep_blocks))

    def retreat(carry_mu, entry_pair):
        state_cot, factor = entry_pair
        adjoint = state_cot + carry_mu
        return (decays * factor * adjoint, adjoint)

    def backward_block(carried, block_items):
        carry_mu, grad_in, grad_out, grad_decay = carried
        tok_rows, cot_rows, kept_part, start_state = block_items
        driving = jnp.dot(tok_rows, in_proj, preferred_element_type=jnp.float32) * input_scale
        _, states = lax.scan(advance, start_state, (driving, kept_part))
        previous = jnp.concatenate([start_state[None, :], states[:-1]], axis=0)
        state_cot = jnp.dot(cot_rows, out_proj.T, preferred_element_type=jnp.float32) * scaling
        first_mu, adjoint = lax.scan(retreat, carry_mu, (state_cot, kept_part), reverse=True)
        grad_decay = grad_decay + lax.optimization_barrier(jnp.sum(kept_part[:, None] * adjoint * previous, axis=0))
        scaled = (input_scale * adjoint).astype(jnp.bfloat16)
        state_low = states.astype(jnp.bfloat16)
        grad_in = grad_in + jnp.dot(tok_rows.T, scaled, preferred_element_type=jnp.float32)
        grad_out = grad_out + jnp.dot(cot_rows.T, state_low, preferred_element_type=jnp.float32) * scaling
        row_grad = jnp.dot(scaled, in_proj.T, preferred_element_type=jnp.float32).astype(jnp.bfloat16)
        return ((first_mu, grad_in, grad_out, grad_decay), row_grad)
    initial = (jnp.zeros((S,), jnp.float32), jnp.zeros((D, S), jnp.float32), jnp.zeros((D, S), jnp.float32), jnp.zeros((S,), jnp.float32))
    finals, row_grads = lax.scan(backward_block, initial, (in_blocks, cot_blocks, keep_blocks, starts), reverse=True)
    return (finals[1], finals[2], finals[3], row_grads.reshape(TOKENS, D))
```

```python
import functools
import math

import jax
import jax.numpy as jnp
from jax import lax
from jax.experimental import pallas as pl
from jax.experimental.pallas import tpu as pltpu
from jax.sharding import PartitionSpec as P

F32 = jnp.float32
BF16 = jnp.bfloat16
SEG = 8
VMEM_LIMIT = 48 * 1024 * 1024


def swap(x, axis, bit):
    n = lax.axis_size(axis)
    return lax.ppermute(x, axis, [(k, k ^ bit) for k in range(n)])


def nn(a, b):
    return lax.dot_general(a, b, (((1,), (0,)), ((), ())), preferred_element_type=F32)


def nt(a, b):
    return lax.dot_general(a, b, (((1,), (1,)), ((), ())), preferred_element_type=F32)


def tn(a, b):
    return lax.dot_general(a, b, (((0,), (0,)), ((), ())), preferred_element_type=F32)


def tiles(row, width):
    return [row[:, 128 * l : 128 * (l + 1)] for l in range(width // 128)]


def put(dst, value):
    for l in range(dst.shape[0]):
        dst[l] = value[:, 128 * l : 128 * (l + 1)]


def joined(src):
    return jnp.concatenate([src[l] for l in range(src.shape[0])], axis=1)


def scan_ends(src, retain_ref, decays, reverse):
    count, steps = src.shape[0], src.shape[1] // SEG

    def lap(k, carry):
        j = steps - 1 - k if reverse else k
        rows = pl.ds(j, SEG, stride=steps)
        kept = retain_ref[rows, :]
        out = []
        for l in range(count):
            end, rate = carry[l]
            factor = kept * decays[l]
            value = src[l, rows, :]
            end = factor * (value + end) if reverse else factor * end + value
            out.append((end, factor * rate))
        return tuple(out)

    start = tuple((jnp.zeros((SEG, 128), F32), jnp.ones((SEG, 128), F32)) for _ in range(count))
    ends = lax.fori_loop(0, steps, lap, start, unroll=4)
    return jnp.concatenate([e[0] for e in ends], axis=1), jnp.concatenate([e[1] for e in ends], axis=1)


def seg_starts(end, rate, entering, reverse):
    now = entering
    starts = [None] * SEG
    for k in range(SEG):
        s = SEG - 1 - k if reverse else k
        starts[s] = now
        now = end[s : s + 1] + rate[s : s + 1] * now
    return jnp.concatenate(starts, axis=0), now


def summary_kernel(x_ref, c_ref, w_ref, v_ref, scale_ref, decay_ref, retain_ref, out_ref, drive, scot, *, scaling):
    width = decay_ref.shape[1]
    decays = tiles(jnp.broadcast_to(decay_ref[...], (SEG, width)), width)
    put(drive, nn(x_ref[...], w_ref[...]) * scale_ref[...])
    put(scot, nt(c_ref[...], v_ref[...]) * scaling)
    zero = jnp.zeros((1, width), F32)
    end, rate = scan_ends(drive, retain_ref, decays, False)
    _, forward = seg_starts(end, rate, zero, False)
    back, _ = scan_ends(scot, retain_ref, decays, True)
    _, backward = seg_starts(back, rate, zero, True)
    total = rate[0:1]
    for s in range(1, SEG):
        total = total * rate[s : s + 1]
    out_ref[...] = jnp.concatenate([total, forward, backward, zero], axis=0)


def summary(x, c, in_proj, out_proj, scale, decays, retain_wide, scaling, chunk):
    rows, depth = x.shape
    channels = in_proj.shape[1]
    return pl.pallas_call(
        functools.partial(summary_kernel, scaling=scaling),
        out_shape=jax.ShapeDtypeStruct((4, channels), F32),
        grid=(channels // chunk,),
        in_specs=[
            pl.BlockSpec((rows, depth), lambda j: (0, 0)),
            pl.BlockSpec((rows, depth), lambda j: (0, 0)),
            pl.BlockSpec((depth, chunk), lambda j: (0, j)),
            pl.BlockSpec((chunk, depth), lambda j: (j, 0)),
            pl.BlockSpec((1, chunk), lambda j: (0, j)),
            pl.BlockSpec((1, chunk), lambda j: (0, j)),
            pl.BlockSpec((rows, 128), lambda j: (0, 0)),
        ],
        out_specs=pl.BlockSpec((4, chunk), lambda j: (0, j)),
        scratch_shapes=[pltpu.VMEM((chunk // 128, rows, 128), F32)] * 2,
        compiler_params=pltpu.CompilerParams(vmem_limit_bytes=VMEM_LIMIT),
        cost_estimate=pl.CostEstimate(flops=4 * rows * depth * channels, transcendentals=0, bytes_accessed=4 * depth * channels),
        name="summary",
    )(x, c, in_proj, out_proj, scale, decays, retain_wide)


def carries_kernel(sum_ref, fwd_ref, bwd_ref):
    blocks = sum_ref.shape[0]
    now = jnp.zeros_like(fwd_ref[0:1, :])
    for b in range(blocks):
        fwd_ref[b : b + 1, :] = now
        row = sum_ref[b]
        now = row[1:2] + row[0:1] * now
    now = jnp.zeros_like(now)
    for b in range(blocks - 1, -1, -1):
        bwd_ref[b : b + 1, :] = now
        row = sum_ref[b]
        now = row[2:3] + row[0:1] * now


def carries(table):
    shape = jax.ShapeDtypeStruct((table.shape[0], table.shape[2]), F32)
    return pl.pallas_call(carries_kernel, out_shape=(shape, shape), name="carries")(table)


def collect(idx_ref, pieces, out_ref):
    @pl.when(pl.program_id(0) == 0)
    def _():
        if len(pieces) == 1:
            out_ref[...] = pieces[0][...].astype(BF16)
        else:
            for k, piece in enumerate(pieces):
                rows = piece.shape[0]
                at = pl.multiple_of(idx_ref[1 + k] * rows, rows)
                out_ref[pl.ds(at, rows), :] = piece[...].astype(BF16)


def forward_kernel(idx_ref, *refs, given):
    pieces = refs[:given]
    w_ref, scale_ref, decay_ref, retain_ref, enter_ref = refs[given : given + 5]
    x_ref, prev_ref, low_ref, drive, state = refs[given + 5 :]
    collect(idx_ref, pieces, x_ref)
    width = decay_ref.shape[1]
    count = drive.shape[0]
    steps = drive.shape[1] // SEG
    decays = tiles(jnp.broadcast_to(decay_ref[...], (SEG, width)), width)
    put(drive, nn(x_ref[...], w_ref[...]) * scale_ref[...])
    end, rate = scan_ends(drive, retain_ref, decays, False)
    start, _ = seg_starts(end, rate, enter_ref[pl.ds(idx_ref[0], 1), :], False)

    def lap(j, before):
        rows = pl.ds(j, SEG, stride=steps)
        kept = retain_ref[rows, :]
        out = []
        for l in range(count):
            after = kept * decays[l] * before[l] + drive[l, rows, :]
            prev_ref[l, rows, :] = before[l]
            state[l, rows, :] = after
            out.append(after)
        return tuple(out)

    lax.fori_loop(0, steps, lap, tuple(tiles(start, width)), unroll=4)
    low_ref[...] = joined(state).astype(BF16)


def backward_kernel(idx_ref, *refs, given, scaling):
    pieces = refs[:given]
    v_ref, scale_ref, decay_ref, retain_ref, enter_ref, prev_ref = refs[given : given + 6]
    x_ref, scaled_ref, grad_ref, scot, adjoint = refs[given + 6 :]
    collect(idx_ref, pieces, x_ref)
    width = decay_ref.shape[1]
    count = scot.shape[0]
    steps = scot.shape[1] // SEG
    decays = tiles(jnp.broadcast_to(decay_ref[...], (SEG, width)), width)
    put(scot, nt(x_ref[...], v_ref[...]) * scaling)
    end, rate = scan_ends(scot, retain_ref, decays, True)
    start, _ = seg_starts(end, rate, enter_ref[pl.ds(idx_ref[0], 1), :], True)

    def lap(k, carry):
        rows = pl.ds(steps - 1 - k, SEG, stride=steps)
        kept = retain_ref[rows, :]
        out = []
        for l in range(count):
            follow, grad = carry[l]
            here = scot[l, rows, :] + follow
            adjoint[l, rows, :] = here
            part = kept * here
            out.append((part * decays[l], grad + part * prev_ref[l, rows, :]))
        return tuple(out)

    begin = tuple((t, jnp.zeros((SEG, 128), F32)) for t in tiles(start, width))
    done = lax.fori_loop(0, steps, lap, begin, unroll=4)
    scaled_ref[...] = (joined(adjoint) * scale_ref[...]).astype(BF16)
    grad_ref[...] = jnp.sum(jnp.concatenate([d[1] for d in done], axis=1), axis=0, keepdims=True)


def block_call(kernel, idx, pieces, weight, across, scale, decays, retain_wide, enter, prev, chunk, name):
    channels = scale.shape[1]
    depth = pieces[0].shape[1]
    rows = sum(p.shape[0] for p in pieces)
    blocks = enter.shape[0]
    specs = [pl.BlockSpec(p.shape, lambda j, i: (0, 0)) for p in pieces]
    specs.append(
        pl.BlockSpec((depth, chunk), lambda j, i: (0, j)) if across else pl.BlockSpec((chunk, depth), lambda j, i: (j, 0))
    )
    specs += [
        pl.BlockSpec((1, chunk), lambda j, i: (0, j)),
        pl.BlockSpec((1, chunk), lambda j, i: (0, j)),
        pl.BlockSpec((rows, 128), lambda j, i: (i[0], 0)),
        pl.BlockSpec((blocks, chunk), lambda j, i: (0, j)),
    ]
    operands = [*pieces, weight, scale, decays, retain_wide, enter]
    tile = pl.BlockSpec((rows, chunk), lambda j, i: (0, j))
    outs = [(jax.ShapeDtypeStruct((rows, depth), BF16), pl.BlockSpec((rows, depth), lambda j, i: (0, 0)))]
    deep = pl.BlockSpec((chunk // 128, rows, 128), lambda j, i: (j, 0, 0))
    if prev is None:
        outs.append((jax.ShapeDtypeStruct((channels // 128, rows, 128), F32), deep))
        outs.append((jax.ShapeDtypeStruct((rows, channels), BF16), tile))
    else:
        specs.append(deep)
        operands.append(prev)
        outs.append((jax.ShapeDtypeStruct((rows, channels), BF16), tile))
        outs.append((jax.ShapeDtypeStruct((1, channels), F32), pl.BlockSpec((1, chunk), lambda j, i: (0, j))))
    return pl.pallas_call(
        functools.partial(kernel, given=len(pieces)),
        out_shape=tuple(o[0] for o in outs),
        grid_spec=pltpu.PrefetchScalarGridSpec(
            num_scalar_prefetch=1,
            grid=(channels // chunk,),
            in_specs=specs,
            out_specs=tuple(o[1] for o in outs),
            scratch_shapes=[pltpu.VMEM((chunk // 128, rows, 128), F32)] * 2,
        ),
        compiler_params=pltpu.CompilerParams(vmem_limit_bytes=VMEM_LIMIT),
        cost_estimate=pl.CostEstimate(
            flops=2 * rows * depth * channels, transcendentals=0, bytes_accessed=2 * depth * channels + 8 * rows * channels
        ),
        name=name,
    )(idx, *operands)


def grad_kernel(idx_ref, *refs, factor):
    half = (len(refs) - 1) // 2
    total = tn(refs[0][...], refs[half][...])
    for k in range(1, half):
        total += tn(refs[k][...], refs[half + k][...])
    refs[-1][...] = total * factor if factor is not None else total


def grad_rows(at, features, values, rows_out, factor, chunk, name):
    channels = values[0].shape[1]
    rows = values[0].shape[0]
    if rows_out % 128:
        total = sum(
            tn(lax.dynamic_slice_in_dim(x, at * rows_out, rows_out, axis=1), v) for x, v in zip(features, values, strict=True)
        )
        return total * factor if factor is not None else total
    return pl.pallas_call(
        functools.partial(grad_kernel, factor=factor),
        out_shape=jax.ShapeDtypeStruct((rows_out, channels), F32),
        grid_spec=pltpu.PrefetchScalarGridSpec(
            num_scalar_prefetch=1,
            grid=(channels // chunk,),
            in_specs=[pl.BlockSpec((rows, rows_out), lambda j, i: (0, i[0]))] * len(features)
            + [pl.BlockSpec((rows, chunk), lambda j, i: (0, j))] * len(values),
            out_specs=pl.BlockSpec((rows_out, chunk), lambda j, i: (0, j)),
        ),
        compiler_params=pltpu.CompilerParams(vmem_limit_bytes=VMEM_LIMIT),
        cost_estimate=pl.CostEstimate(
            flops=2 * len(values) * rows * rows_out * channels, transcendentals=0, bytes_accessed=8 * rows * channels
        ),
        name=name,
    )(jnp.reshape(at, (1,)).astype(jnp.int32), *features, *values)


def rowgrad_kernel(a_ref, w_ref, out_ref):
    out_ref[0] = nt(a_ref[...], w_ref[...])


def row_grad(scaled, in_proj, parts):
    rows, channels = scaled.shape
    depth = in_proj.shape[0]
    width = depth // parts
    return pl.pallas_call(
        rowgrad_kernel,
        out_shape=jax.ShapeDtypeStruct((parts, rows, width), F32),
        grid=(parts,),
        in_specs=[pl.BlockSpec((rows, channels), lambda j: (0, 0)), pl.BlockSpec((width, channels), lambda j: (j, 0))],
        out_specs=pl.BlockSpec((1, rows, width), lambda j: (j, 0, 0)),
        compiler_params=pltpu.CompilerParams(vmem_limit_bytes=VMEM_LIMIT),
        cost_estimate=pl.CostEstimate(flops=2 * rows * depth * channels, transcendentals=0, bytes_accessed=2 * depth * channels),
        name="row_grad",
    )(scaled, in_proj)


def gather_group(x, far, lane):
    rows = x.shape[0]
    half, quarter = rows // 2, rows // 4
    near = swap(lax.dynamic_slice_in_dim(x, (lane % 2) * half, half, axis=0).astype(F32), "tm", 1)
    away = swap(lax.dynamic_slice_in_dim(x, lane * quarter, quarter, axis=0).astype(F32), "tm", far)
    corner = swap(away, "tm", 1)
    near_rest = swap(near, "chan", 1)

    def spread(piece):
        across = swap(piece, "chan", 2)
        return [piece, swap(piece, "chan", 1), across, swap(across, "chan", 1)]

    return [near, near_rest], spread(away), spread(corner)


def per_device(inputs, cotangent, in_proj, out_proj, decays, input_scale, retain):
    rows, depth = inputs.shape
    channels = in_proj.shape[1]
    devices, lanes = lax.axis_size("tm"), lax.axis_size("chan")
    scaling = 1.0 / math.sqrt(rows * devices)
    me, lane = lax.axis_index("tm"), lax.axis_index("chan")
    far = devices // 2
    groups = devices // 4
    chunk = min(512, channels)
    scale = input_scale[None, :]
    decay_row = decays[None, :]

    in_pieces = gather_group(inputs, far, lane)
    cot_pieces = gather_group(cotangent, far, lane)

    own = summary(
        inputs, cotangent, in_proj, out_proj, scale, decay_row,
        jnp.broadcast_to(retain[:, None], (rows, 128)), scaling, chunk,
    )
    own = jnp.concatenate([own[:3], jnp.pad(retain, (0, channels - rows))[None, :]], axis=0)
    table = own[None]
    bit = 1
    while bit < devices:
        other = swap(table, "tm", bit)
        low = (me & bit) == 0
        table = jnp.where(low, jnp.concatenate([table, other]), jnp.concatenate([other, table]))
        bit *= 2
    enter_fwd, enter_bwd = carries(table)
    retain_wide = jnp.broadcast_to(table[:, 3, :rows].reshape(-1, 1), (devices * rows, 128))

    quarters = jnp.stack([lane, lane ^ 1, lane ^ 2, lane ^ 3])
    halves = jnp.stack([lane % 2, 1 - lane % 2, 0, 0])
    places = [jnp.zeros_like(halves), halves, quarters, quarters]
    blocks = [me, me ^ 1, me ^ far, me ^ far ^ 1]
    idx = [jnp.concatenate([b[None], p]).astype(jnp.int32) for b, p in zip(blocks, places, strict=True)]

    backward = functools.partial(backward_kernel, scaling=scaling)
    xs, prevs, lows = [], [], []
    for role, pieces in enumerate([[inputs], *in_pieces]):
        x, prev, low = block_call(
            forward_kernel, idx[role], pieces, in_proj, True, scale, decay_row, retain_wide, enter_fwd, None, chunk, "forward"
        )
        xs.append(x)
        prevs.append(prev)
        lows.append(low)
    cs, scaled, grads = [], [], []
    for role, pieces in enumerate([[cotangent], *cot_pieces]):
        c, s, g = block_call(
            backward, idx[role], pieces, out_proj, False, scale, decay_row, retain_wide, enter_bwd, prevs[role], chunk, "backward"
        )
        cs.append(c)
        scaled.append(s)
        grads.append(g)

    rows_out = depth // devices

    def reduced(features, values, factor, name):
        mine = grad_rows(me, features, values, rows_out, factor, chunk, name)
        for k in range(1, groups):
            mine += swap(grad_rows(me ^ (2 * k), features, values, rows_out, factor, chunk, name), "tm", 2 * k)
        return mine

    out_proj_grad = reduced(cs, lows, scaling, "out_grad")
    in_proj_grad = reduced(xs, scaled, None, "in_grad")

    decay_grad = (grads[0] + grads[1]) + (grads[2] + grads[3])
    bit = 2
    while bit < far:
        decay_grad += swap(decay_grad, "tm", bit)
        bit *= 2

    parts = row_grad(scaled[0], in_proj, lanes)
    bit = 1
    while bit < lanes:
        parts = parts.reshape(-1, 2, *parts.shape[1:])
        side = (lane // bit) % 2
        keep = lax.dynamic_index_in_dim(parts, side, axis=1, keepdims=False)
        give = lax.dynamic_index_in_dim(parts, 1 - side, axis=1, keepdims=False)
        parts = keep + swap(give, "chan", bit)
        bit *= 2
    input_grad = parts[0].astype(BF16)
    return (in_proj_grad, out_proj_grad, decay_grad[0], input_grad)


def solution(mesh):
    return jax.shard_map(
        per_device,
        mesh=mesh,
        in_specs=(
            P("tm", None),
            P("tm", None),
            P(None, "chan"),
            P("chan", None),
            P("chan"),
            P("chan"),
            P("tm"),
        ),
        out_specs=(P("tm", "chan"), P("tm", "chan"), P("chan"), P("tm", "chan")),
        check_vma=False,
    )
```

```python
import functools
import math

import jax
import jax.numpy as jnp
from jax import lax
from jax.experimental import pallas as pl
from jax.experimental.pallas import tpu as pltpu
from jax.sharding import PartitionSpec as P

F32 = jnp.float32
BF16 = jnp.bfloat16
SEG = 8
VMEM_LIMIT = 8 * 1024 * 1024


def swap(x, axis, bit):
    n = lax.axis_size(axis)
    return lax.ppermute(x, axis, [(k, k ^ bit) for k in range(n)])


def nn(a, b):
    return lax.dot_general(a, b, (((1,), (0,)), ((), ())), preferred_element_type=F32)


def nt(a, b):
    return lax.dot_general(a, b, (((1,), (1,)), ((), ())), preferred_element_type=F32)


def tn(a, b):
    return lax.dot_general(a, b, (((0,), (0,)), ((), ())), preferred_element_type=F32)


def order(rows, transpose=False):
    steps = rows // SEG
    r = lax.broadcasted_iota(jnp.int32, (rows, rows), 1 if transpose else 0)
    t = lax.broadcasted_iota(jnp.int32, (rows, rows), 0 if transpose else 1)
    return ((r % SEG) * steps + r // SEG == t).astype(F32).astype(BF16)


VMEM = pl.BlockSpec(memory_space=pltpu.VMEM)
SMEM = pl.BlockSpec(memory_space=pltpu.SMEM)


def resident(kernel, out_shape, operands, name, scratch=(), scalars=1):
    outs = jax.tree.map(lambda _: VMEM, out_shape)
    return pl.pallas_call(
        kernel,
        out_shape=out_shape,
        in_specs=[SMEM] * scalars + [VMEM] * (len(operands) - scalars),
        out_specs=outs,
        scratch_shapes=scratch,
        compiler_params=pltpu.CompilerParams(vmem_limit_bytes=VMEM_LIMIT),
        cost_estimate=pl.CostEstimate(flops=0, transcendentals=0, bytes_accessed=0),
        name=name,
    )(*operands)


def prep_kernel(idx_ref, x_ref, p_ref, half_ref, quarter_ref, full):
    rows = x_ref.shape[0]
    full[...] = nn(order(rows), x_ref[...])
    p_ref[...] = full[...].astype(BF16)
    half, quarter = rows // 2, rows // 4
    half_ref[...] = full[pl.ds(pl.multiple_of(idx_ref[0] * half, half), half), :]
    quarter_ref[...] = full[pl.ds(pl.multiple_of(idx_ref[1] * quarter, quarter), quarter), :]


def prep(idx, x, name):
    rows, depth = x.shape
    shapes = (
        jax.ShapeDtypeStruct((rows, depth), BF16),
        jax.ShapeDtypeStruct((rows // 2, depth), F32),
        jax.ShapeDtypeStruct((rows // 4, depth), F32),
    )
    return resident(prep_kernel, shapes, (idx, x), name, [pltpu.VMEM((rows, depth), F32)])


def lanes_of(l):
    return slice(128 * l, 128 * (l + 1))


def scan_ends(src, retain_ref, base, decays, reverse):
    count, steps = src.shape[1] // 128, src.shape[0] // SEG

    def lap(k, carry):
        j = steps - 1 - k if reverse else k
        rows = pl.ds(pl.multiple_of(j * SEG, SEG), SEG)
        kept = retain_ref[pl.ds(pl.multiple_of(base + j * SEG, SEG), SEG), :]
        out = []
        for l in range(count):
            end, rate = carry[l]
            factor = kept * decays[l]
            value = src[rows, lanes_of(l)]
            end = factor * (value + end) if reverse else factor * end + value
            out.append((end, factor * rate))
        return tuple(out)

    start = tuple((jnp.zeros((SEG, 128), F32), jnp.ones((SEG, 128), F32)) for _ in range(count))
    ends = lax.fori_loop(0, steps, lap, start, unroll=4)
    return jnp.concatenate([e[0] for e in ends], axis=1), jnp.concatenate([e[1] for e in ends], axis=1)


def seg_starts(end, rate, entering, reverse):
    now = entering
    starts = [None] * SEG
    for k in range(SEG):
        s = SEG - 1 - k if reverse else k
        starts[s] = now
        now = end[s : s + 1] + rate[s : s + 1] * now
    return jnp.concatenate(starts, axis=0), now


def decay_tiles(decay_ref):
    width = decay_ref.shape[1]
    full = jnp.broadcast_to(decay_ref[...], (SEG, width))
    return [full[:, lanes_of(l)] for l in range(width // 128)]


def summary_kernel(x_ref, c_ref, w_ref, v_ref, scale_ref, decay_ref, retain_ref, out_ref, drive, scot, *, scaling):
    decays = decay_tiles(decay_ref)
    drive[...] = nn(x_ref[...], w_ref[...]) * scale_ref[...]
    scot[...] = nt(c_ref[...], v_ref[...]) * scaling
    zero = jnp.zeros(decay_ref.shape, F32)
    end, rate = scan_ends(drive, retain_ref, 0, decays, False)
    _, forward = seg_starts(end, rate, zero, False)
    back, _ = scan_ends(scot, retain_ref, 0, decays, True)
    _, backward = seg_starts(back, rate, zero, True)
    total = rate[0:1]
    for s in range(1, SEG):
        total = total * rate[s : s + 1]
    out_ref[...] = jnp.concatenate([total, forward, backward], axis=0)


def carries_kernel(sum_ref, fwd_ref, bwd_ref):
    blocks = sum_ref.shape[0]
    now = jnp.zeros_like(fwd_ref[0:1, :])
    for b in range(blocks):
        fwd_ref[b : b + 1, :] = now
        row = sum_ref[b]
        now = row[1:2] + row[0:1] * now
    now = jnp.zeros_like(now)
    for b in range(blocks - 1, -1, -1):
        bwd_ref[b : b + 1, :] = now
        row = sum_ref[b]
        now = row[2:3] + row[0:1] * now


def carries(table):
    shape = jax.ShapeDtypeStruct((table.shape[0], table.shape[2]), F32)
    return resident(carries_kernel, (shape, shape), (table,), "carries", scalars=0)


def collect(idx_ref, role, pieces, out_ref):
    for k, piece in enumerate(pieces):
        rows = piece.shape[0]
        at = pl.multiple_of(idx_ref[role, 1 + k] * rows, rows)
        out_ref[pl.ds(at, rows), :] = piece[...].astype(BF16)


def forward_kernel(idx_ref, *refs, given):
    total = sum(given)
    pieces = refs[:total]
    w_ref, scale_ref, decay_ref, retain_ref, enter_ref = refs[total : total + 5]
    outs = list(refs[total + 5 :])
    decays = decay_tiles(decay_ref)
    count = len(decays)
    drive = outs.pop()
    rows_all = drive.shape[0]
    steps = rows_all // SEG
    at_piece = 0
    for role, number in enumerate(given):
        mine = pieces[at_piece : at_piece + number]
        at_piece += number
        if number > 1:
            x_ref = outs.pop(0)
            collect(idx_ref, role, mine, x_ref)
        else:
            x_ref = mine[0]
        track_ref, low_ref = outs.pop(0), outs.pop(0)
        block = idx_ref[role, 0]
        base = block * rows_all
        drive[...] = nn(x_ref[...], w_ref[...]) * scale_ref[...]
        end, rate = scan_ends(drive, retain_ref, base, decays, False)
        start, _ = seg_starts(end, rate, enter_ref[pl.ds(block, 1), :], False)
        track_ref[0:SEG, :] = start

        def lap(j, before, base=base, track_ref=track_ref):
            at = pl.multiple_of(j * SEG, SEG)
            kept = retain_ref[pl.ds(pl.multiple_of(base + j * SEG, SEG), SEG), :]
            out = []
            for l in range(count):
                after = kept * decays[l] * before[l] + drive[pl.ds(at, SEG), lanes_of(l)]
                track_ref[pl.ds(pl.multiple_of(at + SEG, SEG), SEG), lanes_of(l)] = after
                out.append(after)
            return tuple(out)

        lax.fori_loop(0, steps, lap, tuple(start[:, lanes_of(l)] for l in range(count)), unroll=4)
        low_ref[...] = track_ref[SEG:, :].astype(BF16)


def backward_kernel(idx_ref, *refs, given, scaling):
    total = sum(given)
    roles = len(given)
    pieces = refs[:total]
    v_ref, scale_ref, decay_ref, retain_ref, enter_ref = refs[total : total + 5]
    tracks = refs[total + 5 : total + 5 + roles]
    outs = list(refs[total + 5 + roles :])
    decays = decay_tiles(decay_ref)
    count = len(decays)
    adjoint, scot = outs.pop(), outs.pop()
    rows_all = scot.shape[0]
    steps = rows_all // SEG
    at_piece = 0
    for role, number in enumerate(given):
        mine = pieces[at_piece : at_piece + number]
        at_piece += number
        if number > 1:
            x_ref = outs.pop(0)
            collect(idx_ref, role, mine, x_ref)
        else:
            x_ref = mine[0]
        scaled_ref, grad_ref = outs.pop(0), outs.pop(0)
        block = idx_ref[role, 0]
        base = block * rows_all
        scot[...] = nt(x_ref[...], v_ref[...]) * scaling
        end, rate = scan_ends(scot, retain_ref, base, decays, True)
        start, _ = seg_starts(end, rate, enter_ref[pl.ds(block, 1), :], True)

        def lap(k, carry, base=base, track_ref=tracks[role]):
            at = (steps - 1 - k) * SEG
            rows = pl.ds(pl.multiple_of(at, SEG), SEG)
            kept = retain_ref[pl.ds(pl.multiple_of(base + at, SEG), SEG), :]
            out = []
            for l in range(count):
                follow, grad = carry[l]
                here = scot[rows, lanes_of(l)] + follow
                adjoint[rows, lanes_of(l)] = here
                part = kept * here
                out.append((part * decays[l], grad + part * track_ref[rows, lanes_of(l)]))
            return tuple(out)

        begin = tuple((start[:, lanes_of(l)], jnp.zeros((SEG, 128), F32)) for l in range(count))
        done = lax.fori_loop(0, steps, lap, begin, unroll=4)
        scaled_ref[...] = (adjoint[...] * scale_ref[...]).astype(BF16)
        grad_ref[...] = jnp.sum(jnp.concatenate([d[1] for d in done], axis=1), axis=0, keepdims=True)


def block_call(kernel, idx, blocks, operands, backward, name):
    channels = operands[1].shape[1]
    rows, depth = sum(p.shape[0] for p in blocks[0]), blocks[0][0].shape[1]
    low = jax.ShapeDtypeStruct((rows, channels), BF16)
    shapes = []
    for pieces in blocks:
        shapes += [jax.ShapeDtypeStruct((rows, depth), BF16)] if len(pieces) > 1 else []
        if backward:
            shapes += [low, jax.ShapeDtypeStruct((1, channels), F32)]
        else:
            shapes += [jax.ShapeDtypeStruct((SEG + rows, channels), F32), low]
    out = list(resident(
        functools.partial(kernel, given=tuple(len(b) for b in blocks)), tuple(shapes),
        (idx, *[p for b in blocks for p in b], *operands), name,
        [pltpu.VMEM((rows, channels), F32)] * (2 if backward else 1),
    ))
    return [(out.pop(0) if len(b) > 1 else b[0], out.pop(0), out.pop(0)) for b in blocks]


def grad_kernel(idx_ref, *refs, factor):
    half = (len(refs) - 1) // 2
    width = refs[-1].shape[0]
    at = pl.ds(pl.multiple_of(idx_ref[0] * width, width), width)
    total = tn(refs[0][:, at], refs[half][...])
    for k in range(1, half):
        total += tn(refs[k][:, at], refs[half + k][...])
    refs[-1][...] = total * factor if factor is not None else total


def grad_rows(at, features, values, rows_out, factor, name):
    channels = values[0].shape[1]
    rows = values[0].shape[0]
    if rows_out % 128:
        total = sum(
            tn(lax.dynamic_slice_in_dim(x, at * rows_out, rows_out, axis=1), v) for x, v in zip(features, values, strict=True)
        )
        return total * factor if factor is not None else total
    return resident(
        functools.partial(grad_kernel, factor=factor), jax.ShapeDtypeStruct((rows_out, channels), F32),
        (jnp.reshape(at, (1,)).astype(jnp.int32), *features, *values), name,
    )


def row_grad_kernel(a_ref, w_ref, out_ref):
    parts, rows, width = out_ref.shape
    a = nn(order(rows, True), a_ref[...]).astype(BF16)
    for k in range(parts):
        out_ref[k] = nt(a, w_ref[width * k : width * (k + 1), :])


def row_grad(scaled, in_proj, parts):
    rows, channels = scaled.shape
    depth = in_proj.shape[0]
    return resident(
        row_grad_kernel, jax.ShapeDtypeStruct((parts, rows, depth // parts), F32), (scaled, in_proj), "row_grad",
        scalars=0,
    )


def after(x, *others):
    return lax.optimization_barrier((x, *others))[0]


def spread(piece):
    across = swap(piece, "chan", 2)
    return [piece, swap(piece, "chan", 1), across, swap(across, "chan", 1)]


def per_device(inputs, cotangent, in_proj, out_proj, decays, input_scale, retain):
    rows, depth = inputs.shape
    channels = in_proj.shape[1]
    devices, lanes = lax.axis_size("tm"), lax.axis_size("chan")
    scaling = 1.0 / math.sqrt(rows * devices)
    me, lane = lax.axis_index("tm"), lax.axis_index("chan")
    far = devices // 2
    groups = devices // 4
    steps = rows // SEG
    scale = input_scale[None, :]
    decay_row = decays[None, :]

    where = jnp.stack([lane % 2, lane]).astype(jnp.int32)
    x_own, x_half, x_quarter = prep(where, inputs, "prep_inputs")
    near_x = swap(x_half, "tm", 1)
    away_x = swap(x_quarter, "tm", far)
    c_own, c_half, c_quarter = prep(where, cotangent, "prep_cotangent")
    corner_x = swap(away_x, "tm", 1)
    x_pieces = [[near_x, swap(near_x, "chan", 1)], spread(away_x), spread(corner_x)]
    away_c = swap(after(c_quarter, away_x), "tm", far)
    near_c = swap(after(c_half, corner_x), "tm", 1)
    corner_c = swap(away_c, "tm", 1)
    c_pieces = [[near_c, swap(near_c, "chan", 1)], spread(away_c), spread(corner_c)]

    def ordered(r):
        return r.reshape(-1, SEG, steps).swapaxes(1, 2).reshape(-1, 1)

    ends = resident(
        functools.partial(summary_kernel, scaling=scaling), jax.ShapeDtypeStruct((3, channels), F32),
        (x_own, c_own, in_proj, out_proj, scale, decay_row, jnp.broadcast_to(ordered(retain), (rows, 128))), "summary",
        [pltpu.VMEM((rows, channels), F32)] * 2, scalars=0,
    )
    table = jnp.concatenate([after(ends, away_x, near_x), jnp.pad(retain, (0, channels - rows))[None, :]], axis=0)[None]
    bit = 1
    while bit < devices:
        other = swap(table, "tm", bit)
        low = (me & bit) == 0
        table = jnp.where(low, jnp.concatenate([table, other]), jnp.concatenate([other, table]))
        bit *= 2
    enter_fwd, enter_bwd = carries(table)
    retain_wide = jnp.broadcast_to(ordered(table[:, 3, :rows]), (devices * rows, 128))

    quarters = jnp.stack([lane, lane ^ 1, lane ^ 2, lane ^ 3])
    halves = jnp.stack([lane % 2, 1 - lane % 2, 0, 0])
    places = [jnp.zeros_like(halves), halves, quarters, quarters]
    blocks = [me, me ^ 1, me ^ far, me ^ far ^ 1]
    idx = [jnp.concatenate([b[None], p]).astype(jnp.int32) for b, p in zip(blocks, places, strict=True)]

    own, others = jnp.stack(idx[:1]), jnp.stack(idx[1:])
    shared = (in_proj, scale, decay_row, retain_wide, enter_fwd)
    forward = block_call(forward_kernel, own, [[x_own]], shared, False, "forward_own")
    forward += block_call(forward_kernel, others, x_pieces, shared, False, "forward_group")
    xs, tracks, lows = zip(*forward, strict=True)
    shared = (out_proj, scale, decay_row, retain_wide, enter_bwd)
    kernel = functools.partial(backward_kernel, scaling=scaling)
    backward = block_call(kernel, own, [[c_own]], (*shared, tracks[0]), True, "backward_own")
    backward += block_call(kernel, others[:2], c_pieces[:2], (*shared, *tracks[1:3]), True, "backward_near")
    backward += block_call(kernel, others[2:], c_pieces[2:], (*shared, *tracks[3:]), True, "backward_far")
    cs, scaled, grads = zip(*backward, strict=True)

    rows_out = depth // devices

    def reduced(features, values, factor, name):
        given = [swap(grad_rows(me ^ (2 * k), features, values, rows_out, factor, name), "tm", 2 * k) for k in range(1, groups)]
        mine = grad_rows(me, features, values, rows_out, factor, name)
        for part in given:
            mine += part
        return mine

    out_proj_grad = reduced(cs, lows, scaling, "out_grad")
    in_proj_grad = reduced(xs, scaled, None, "in_grad")

    decay_grad = (grads[0] + grads[1]) + (grads[2] + grads[3])
    bit = 2
    while bit < far:
        decay_grad += swap(decay_grad, "tm", bit)
        bit *= 2

    parts = row_grad(scaled[0], in_proj, lanes)
    bit = 1
    while bit < lanes:
        parts = parts.reshape(-1, 2, *parts.shape[1:])
        side = (lane // bit) % 2
        keep = lax.dynamic_index_in_dim(parts, side, axis=1, keepdims=False)
        give = lax.dynamic_index_in_dim(parts, 1 - side, axis=1, keepdims=False)
        parts = keep + swap(give, "chan", bit)
        bit *= 2
    input_grad = parts[0].astype(BF16)
    return (in_proj_grad, out_proj_grad, decay_grad[0], input_grad)


def solution(mesh):
    return jax.shard_map(
        per_device,
        mesh=mesh,
        in_specs=(
            P("tm", None),
            P("tm", None),
            P(None, "chan"),
            P("chan", None),
            P("chan"),
            P("chan"),
            P("tm"),
        ),
        out_specs=(P("tm", "chan"), P("tm", "chan"), P("chan"), P("tm", "chan")),
        check_vma=False,
    )
```

```python
import functools
import math

import jax
import jax.numpy as jnp
from jax import lax
from jax.experimental import pallas as pl
from jax.experimental.pallas import tpu as pltpu
from jax.sharding import PartitionSpec as P

F32 = jnp.float32
BF16 = jnp.bfloat16
SEG = 8
VMEM_LIMIT = 12 * 1024 * 1024


def swap(x, axis, bit):
    n = lax.axis_size(axis)
    return lax.ppermute(x, axis, [(k, k ^ bit) for k in range(n)])


def nn(a, b):
    return lax.dot_general(a, b, (((1,), (0,)), ((), ())), preferred_element_type=F32)


def nt(a, b):
    return lax.dot_general(a, b, (((1,), (1,)), ((), ())), preferred_element_type=F32)


def tn(a, b):
    return lax.dot_general(a, b, (((0,), (0,)), ((), ())), preferred_element_type=F32)


def order(rows, transpose=False):
    steps = rows // SEG
    r = lax.broadcasted_iota(jnp.int32, (rows, rows), 1 if transpose else 0)
    t = lax.broadcasted_iota(jnp.int32, (rows, rows), 0 if transpose else 1)
    return ((r % SEG) * steps + r // SEG == t).astype(F32).astype(BF16)


VMEM = pl.BlockSpec(memory_space=pltpu.VMEM)
SMEM = pl.BlockSpec(memory_space=pltpu.SMEM)


ANY = pl.BlockSpec(memory_space=pltpu.HBM)


def resident(kernel, out_shape, operands, name, scratch=(), scalars=1, anywhere=0, out_specs=None):
    return pl.pallas_call(
        kernel,
        out_shape=out_shape,
        in_specs=[SMEM] * scalars + [VMEM] * (len(operands) - scalars - anywhere) + [ANY] * anywhere,
        out_specs=jax.tree.map(lambda _: VMEM, out_shape) if out_specs is None else out_specs,
        scratch_shapes=scratch,
        compiler_params=pltpu.CompilerParams(vmem_limit_bytes=VMEM_LIMIT),
        cost_estimate=pl.CostEstimate(flops=0, transcendentals=0, bytes_accessed=0),
        name=name,
    )(*operands)


def prep_kernel(idx_ref, x_ref, p_ref, *refs, parts):
    full = refs[-1]
    rows, depth = x_ref.shape
    full[...] = nn(order(rows), x_ref[...])
    p_ref[...] = full[...].astype(BF16)
    half, quarter, width = rows // 2, rows // 4, depth // parts
    for k in range(parts):
        near = pl.ds(pl.multiple_of(idx_ref[2 + k] * width, width), width)
        away = pl.ds(pl.multiple_of(idx_ref[2 + parts - 1 - k] * width, width), width)
        refs[2 * k][...] = full[pl.ds(pl.multiple_of(idx_ref[0] * half, half), half), near]
        refs[2 * k + 1][...] = full[pl.ds(pl.multiple_of(idx_ref[1] * quarter, quarter), quarter), away]


def prep(idx, x, parts, name):
    rows, depth = x.shape
    shapes = [jax.ShapeDtypeStruct((rows, depth), BF16)]
    for _ in range(parts):
        shapes.append(jax.ShapeDtypeStruct((rows // 2, depth // parts), F32))
        shapes.append(jax.ShapeDtypeStruct((rows // 4, depth // parts), F32))
    kernel = functools.partial(prep_kernel, parts=parts)
    return resident(kernel, tuple(shapes), (idx, x), name, [pltpu.VMEM((rows, depth), F32)])


def pack_kernel(*refs):
    *pieces, out_ref, sems = refs
    copies, at = [], 0
    for k, ref in enumerate(pieces):
        copies.append(pltpu.make_async_copy(ref, out_ref.at[pl.ds(at, ref.shape[0]), :], sems.at[k]))
        at += ref.shape[0]
    for copy in copies:
        copy.start()
    for copy in copies:
        copy.wait()


def pack(pieces, name):
    shape = jax.ShapeDtypeStruct((sum(p.shape[0] for p in pieces), pieces[0].shape[1]), F32)
    return resident(pack_kernel, shape, tuple(pieces), name, [pltpu.SemaphoreType.DMA((len(pieces),))], scalars=0, anywhere=len(pieces))


def lanes_of(l):
    return slice(128 * l, 128 * (l + 1))


def scan_ends(src, retain_ref, base, decays, reverse):
    count, steps = src.shape[1] // 128, src.shape[0] // SEG

    def lap(k, carry):
        j = steps - 1 - k if reverse else k
        rows = pl.ds(pl.multiple_of(j * SEG, SEG), SEG)
        kept = retain_ref[pl.ds(pl.multiple_of(base + j * SEG, SEG), SEG), :]
        out = []
        for l in range(count):
            end, rate = carry[l]
            factor = kept * decays[l]
            value = src[rows, lanes_of(l)]
            end = factor * (value + end) if reverse else factor * end + value
            out.append((end, factor * rate))
        return tuple(out)

    start = tuple((jnp.zeros((SEG, 128), F32), jnp.ones((SEG, 128), F32)) for _ in range(count))
    ends = lax.fori_loop(0, steps, lap, start, unroll=4)
    return jnp.concatenate([e[0] for e in ends], axis=1), jnp.concatenate([e[1] for e in ends], axis=1)


def seg_starts(end, rate, entering, reverse):
    now = entering
    starts = [None] * SEG
    for k in range(SEG):
        s = SEG - 1 - k if reverse else k
        starts[s] = now
        now = end[s : s + 1] + rate[s : s + 1] * now
    return jnp.concatenate(starts, axis=0), now


def decay_tiles(decay_ref):
    width = decay_ref.shape[1]
    full = jnp.broadcast_to(decay_ref[...], (SEG, width))
    return [full[:, lanes_of(l)] for l in range(width // 128)]


def summary_kernel(x_ref, c_ref, w_ref, v_ref, scale_ref, decay_ref, retain_ref, out_ref, drive, scot, *, scaling):
    decays = decay_tiles(decay_ref)
    drive[...] = nn(x_ref[...], w_ref[...]) * scale_ref[...]
    scot[...] = nt(c_ref[...], v_ref[...]) * scaling
    zero = jnp.zeros(decay_ref.shape, F32)
    end, rate = scan_ends(drive, retain_ref, 0, decays, False)
    _, forward = seg_starts(end, rate, zero, False)
    back, _ = scan_ends(scot, retain_ref, 0, decays, True)
    _, backward = seg_starts(back, rate, zero, True)
    total = rate[0:1]
    for s in range(1, SEG):
        total = total * rate[s : s + 1]
    out_ref[...] = jnp.concatenate([total, forward, backward], axis=0)


def carries_kernel(idx_ref, sum_ref, fwd_ref, bwd_ref, retain_ref):
    blocks = sum_ref.shape[0]
    far = blocks // 2

    def row(b):
        away = idx_ref[0] ^ b
        top = away // far
        low = (away % 2) ^ top
        middle = ((away // 2) % (far // 2)) ^ low
        return sum_ref[middle + (far // 2) * low + far * top]

    now = jnp.zeros_like(fwd_ref[0:1, :])
    for b in range(blocks):
        fwd_ref[b : b + 1, :] = now
        ends = row(b)
        retain_ref[b : b + 1, :] = ends[3:4]
        now = ends[1:2] + ends[0:1] * now
    now = jnp.zeros_like(now)
    for b in range(blocks - 1, -1, -1):
        bwd_ref[b : b + 1, :] = now
        ends = row(b)
        now = ends[2:3] + ends[0:1] * now


def carries(me, table):
    shape = jax.ShapeDtypeStruct((table.shape[0], table.shape[2]), F32)
    return resident(carries_kernel, (shape,) * 3, (me, table), "carries")


def reach(devices):
    return [1 << k for k in range(1, devices.bit_length() - 2)] + [3, devices // 2 + 1]


def collect_kernel(idx_ref, *refs, layout):
    count = len(layout)
    outs = refs[count : count + 3]
    held, sems = refs[count + 3], refs[count + 4]
    copies, at = [], 0
    for k, ref in enumerate(refs[:count]):
        copies.append(pltpu.make_async_copy(ref, held.at[pl.ds(at, ref.shape[0]), :], sems.at[k]))
        at += ref.shape[0]
    for copy in copies:
        copy.start()
    start = 0
    for copy, parts in zip(copies, layout, strict=True):
        copy.wait()
        for role, slot, rows in parts:
            at = pl.multiple_of(idx_ref[slot] * rows, rows)
            outs[role][pl.ds(at, rows), :] = held[start : start + rows, :].astype(BF16)
            start += rows


def collected(place, pieces, name):
    rows = sum(part[2] for _, parts in pieces for part in parts)
    depth = pieces[0][0].shape[1]
    shape = jax.ShapeDtypeStruct((rows // 3, depth), BF16)
    kernel = functools.partial(collect_kernel, layout=[parts for _, parts in pieces])
    scratch = [pltpu.VMEM((rows, depth), F32), pltpu.SemaphoreType.DMA((len(pieces),))]
    return list(resident(kernel, (shape,) * 3, (place, *[array for array, _ in pieces]), name, scratch, anywhere=len(pieces)))


def forward_kernel(idx_ref, *refs, roles):
    xs = refs[:roles]
    w_ref, scale_ref, decay_ref, retain_ref, enter_ref = refs[roles : roles + 5]
    outs = refs[roles + 5 : -3]
    drive, held, sems = refs[-3:]
    copies = []
    decays = decay_tiles(decay_ref)
    count = len(decays)
    rows_all = drive.shape[0]
    steps = rows_all // SEG
    for role in range(roles):
        track_ref, low_ref = held.at[role], outs[2 * role + 1]
        block = idx_ref[role]
        base = block * rows_all
        drive[...] = nn(xs[role][...], w_ref[...]) * scale_ref[...]
        end, rate = scan_ends(drive, retain_ref, base, decays, False)
        start, _ = seg_starts(end, rate, enter_ref[pl.ds(block, 1), :], False)
        track_ref[0:SEG, :] = start

        def lap(j, before, base=base, track_ref=track_ref):
            at = pl.multiple_of(j * SEG, SEG)
            kept = retain_ref[pl.ds(pl.multiple_of(base + j * SEG, SEG), SEG), :]
            out = []
            for l in range(count):
                now = kept * decays[l] * before[l] + drive[pl.ds(at, SEG), lanes_of(l)]
                track_ref[pl.ds(pl.multiple_of(at + SEG, SEG), SEG), lanes_of(l)] = now
                out.append(now)
            return tuple(out)

        lax.fori_loop(0, steps, lap, tuple(start[:, lanes_of(l)] for l in range(count)), unroll=4)
        copies.append(pltpu.make_async_copy(track_ref, outs[2 * role], sems.at[role]))
        copies[-1].start()
        low_ref[...] = track_ref[SEG:, :].astype(BF16)
    for copy in copies:
        copy.wait()


def backward_kernel(idx_ref, side_ref, *refs, roles, parts, scaling):
    cs = refs[: roles * parts]
    v_ref, scale_ref, decay_ref, retain_ref, enter_ref = refs[roles * parts : roles * parts + 5]
    tracks = refs[roles * parts + 5 : roles * parts + 5 + roles]
    outs = refs[roles * parts + 5 + roles : -4]
    scot, adjoint, held, sems = refs[-4:]
    copies = [pltpu.make_async_copy(track, held.at[k], sems.at[k]) for k, track in enumerate(tracks)]
    for copy in copies:
        copy.start()
    decays = decay_tiles(decay_ref)
    count = len(decays)
    rows_all = scot.shape[0]
    steps = rows_all // SEG
    width = v_ref.shape[1] // parts
    for role in range(roles):
        scaled_ref, grad_ref = outs[2 * role : 2 * role + 2]
        block = idx_ref[role]
        base = block * rows_all
        if parts == 1:
            scot[...] = nt(cs[role][...], v_ref[...]) * scaling
        else:
            total = None
            for k in range(parts):
                cols = pl.ds(pl.multiple_of(side_ref[k] * width, width), width)
                part = nt(cs[parts * role + k][...], v_ref[:, cols])
                total = part if total is None else total + part
            scot[...] = total * scaling
        end, rate = scan_ends(scot, retain_ref, base, decays, True)
        start, _ = seg_starts(end, rate, enter_ref[pl.ds(block, 1), :], True)

        copies[role].wait()

        def lap(k, carry, base=base, track_ref=held.at[role]):
            at = (steps - 1 - k) * SEG
            rows = pl.ds(pl.multiple_of(at, SEG), SEG)
            kept = retain_ref[pl.ds(pl.multiple_of(base + at, SEG), SEG), :]
            out = []
            for l in range(count):
                follow, grad = carry[l]
                here = scot[rows, lanes_of(l)] + follow
                adjoint[rows, lanes_of(l)] = here
                part = kept * here
                out.append((part * decays[l], grad + part * track_ref[rows, lanes_of(l)]))
            return tuple(out)

        begin = tuple((start[:, lanes_of(l)], jnp.zeros((SEG, 128), F32)) for l in range(count))
        done = lax.fori_loop(0, steps, lap, begin, unroll=4)
        scaled_ref[...] = (adjoint[...] * scale_ref[...]).astype(BF16)
        grad_ref[...] = jnp.sum(jnp.concatenate([d[1] for d in done], axis=1), axis=0, keepdims=True)


def forward_call(blocks, xs, operands, name):
    channels = operands[1].shape[1]
    rows, roles = xs[0].shape[0], len(xs)
    shapes = (jax.ShapeDtypeStruct((SEG + rows, channels), F32), jax.ShapeDtypeStruct((rows, channels), BF16)) * roles
    out = resident(
        functools.partial(forward_kernel, roles=roles), shapes, (blocks, *xs, *operands), name,
        [
            pltpu.VMEM((rows, channels), F32),
            pltpu.VMEM((roles, SEG + rows, channels), F32),
            pltpu.SemaphoreType.DMA((roles,)),
        ],
        out_specs=(ANY, VMEM) * roles,
    )
    return list(out[::2]), list(out[1::2])


def backward_call(blocks, sides, cs, operands, tracks, scaling, name):
    channels = operands[1].shape[1]
    rows, roles = cs[0][0].shape[0], len(cs)
    kernel = functools.partial(backward_kernel, roles=roles, parts=len(cs[0]), scaling=scaling)
    shapes = (jax.ShapeDtypeStruct((rows, channels), BF16), jax.ShapeDtypeStruct((1, channels), F32)) * roles
    out = resident(
        kernel, shapes, (blocks, sides, *[part for c in cs for part in c], *operands, *tracks), name,
        [pltpu.VMEM((rows, channels), F32)] * 2
        + [pltpu.VMEM((roles, *tracks[0].shape), F32), pltpu.SemaphoreType.DMA((roles,))],
        scalars=2, anywhere=roles,
    )
    return list(out[::2]), list(out[1::2])


def grad_kernel(idx_ref, *refs, factor):
    half = (len(refs) - 1) // 2
    width = refs[-1].shape[0]
    at = pl.ds(pl.multiple_of(idx_ref[0] * width, width), width)
    total = tn(refs[0][:, at], refs[half][...])
    for k in range(1, half):
        total += tn(refs[k][:, at], refs[half + k][...])
    refs[-1][...] = total * factor if factor is not None else total


def grad_rows(at, features, values, rows_out, factor, name):
    channels = values[0].shape[1]
    rows = values[0].shape[0]
    if rows_out % 128:
        total = sum(
            tn(lax.dynamic_slice_in_dim(x, at * rows_out, rows_out, axis=1), v) for x, v in zip(features, values, strict=True)
        )
        return total * factor if factor is not None else total
    return resident(
        functools.partial(grad_kernel, factor=factor), jax.ShapeDtypeStruct((rows_out, channels), F32),
        (jnp.reshape(at, (1,)).astype(jnp.int32), *features, *values), name,
    )


def row_grad_kernel(a_ref, w_ref, out_ref):
    parts, rows, width = out_ref.shape
    a = nn(order(rows, True), a_ref[...]).astype(BF16)
    for k in range(parts):
        out_ref[k] = nt(a, w_ref[width * k : width * (k + 1), :])


def row_grad(scaled, in_proj, parts):
    rows, channels = scaled.shape
    depth = in_proj.shape[0]
    return resident(
        row_grad_kernel, jax.ShapeDtypeStruct((parts, rows, depth // parts), F32), (scaled, in_proj), "row_grad",
        scalars=0,
    )


def after(x, *others):
    return lax.optimization_barrier((x, *others))[0]


class Order:
    def __init__(self):
        self.last = None

    def behind(self, x):
        return x if self.last is None else lax.optimization_barrier((x, self.last))[0]

    def step(self, *results):
        held = results if self.last is None else (*results, self.last)
        results = lax.optimization_barrier(held)[: len(results)]
        self.last = results[0]
        return results[0] if len(results) == 1 else results

    def send(self, x, axis, bit):
        return swap(self.behind(x), axis, bit)


def per_device(inputs, cotangent, in_proj, out_proj, decays, input_scale, retain):
    rows, depth = inputs.shape
    channels = in_proj.shape[1]
    devices, lanes = lax.axis_size("tm"), lax.axis_size("chan")
    scaling = 1.0 / math.sqrt(rows * devices)
    me, lane = lax.axis_index("tm"), lax.axis_index("chan")
    far = devices // 2
    groups = devices // 4
    steps = rows // SEG
    scale = input_scale[None, :]
    decay_row = decays[None, :]
    side = me // far

    half, quarter = rows // 2, rows // 4
    rows_out = depth // devices
    core = lane % 2
    place = [core, 1 - core, lane, lane ^ 2, lane ^ 1, lane ^ 3, 2 * core, 2 * core + 1, 2 - 2 * core, 3 - 2 * core]
    place = jnp.stack(place).astype(jnp.int32)
    blocks = jnp.stack([me, me ^ 1, me ^ far, me ^ far ^ 1]).astype(jnp.int32)
    sides = jnp.stack([side, 1 - side]).astype(jnp.int32)
    mine_near, mine_1, mine_2, mine_3, mine_4 = (
        [(0, 0, half)], [(1, 2, quarter)], [(1, 3, quarter)], [(2, 2, quarter)], [(2, 3, quarter)],
    )
    their_near, their_1, their_2, their_3, their_4 = (
        [(0, 1, half)], [(1, 4, quarter)], [(1, 5, quarter)], [(2, 4, quarter)], [(2, 5, quarter)],
    )

    def ordered(r):
        return r.reshape(-1, SEG, steps).swapaxes(1, 2).reshape(-1, 1)

    line = Order()
    where = jnp.stack([lane % 2, lane, side * 0]).astype(jnp.int32)
    x_own, x_half, x_quarter = line.step(*prep(where, inputs, 1, "prep_inputs"))
    near_x = line.send(x_half, "tm", 1)
    away_x = line.send(x_quarter, "tm", far)
    where = jnp.stack([lane % 2, lane, side, 1 - side]).astype(jnp.int32)
    c_own, c_half_a, c_quarter_a, c_half_b, c_quarter_b = prep(where, line.behind(cotangent), 2, "prep_cotangent")
    ends = resident(
        functools.partial(summary_kernel, scaling=scaling), jax.ShapeDtypeStruct((3, channels), F32),
        (x_own, c_own, in_proj, out_proj, scale, decay_row, jnp.broadcast_to(ordered(retain), (rows, 128))), "summary",
        [pltpu.VMEM((rows, channels), F32)] * 2, scalars=0,
    )
    table = jnp.concatenate([ends, jnp.pad(retain, (0, channels - rows))[None, :]], axis=0)[None]
    for bit in reach(devices)[:-1]:
        table = jnp.concatenate([table, line.send(table, "tm", bit)])
    near_x, away_x, table = line.step(near_x, away_x, table)

    corner_x = line.send(away_x, "tm", 1)
    side_x = line.send(away_x, "chan", 2)
    away_a = line.send(c_quarter_a, "tm", far)
    table = jnp.concatenate([table, line.send(table, "tm", reach(devices)[-1])])
    enter_fwd, enter_bwd, retain_all = carries(me[None].astype(jnp.int32), table)
    corner_x, side_x, away_a, enter_fwd = line.step(corner_x, side_x, away_a, enter_fwd)

    near_a = line.send(c_half_a, "tm", 1)
    corner_a = line.send(away_a, "tm", 1)
    corner_side_x = line.send(corner_x, "chan", 2)
    away_b = line.send(c_quarter_b, "tm", far)
    retain_wide = jnp.broadcast_to(ordered(retain_all[:, :rows]), (devices * rows, 128))
    forward = (in_proj, scale, decay_row, retain_wide, enter_fwd)
    backward = (out_proj, scale, decay_row, retain_wide, enter_bwd)
    tracks, lows = forward_call(blocks[:1], [x_own], forward, "forward_own")
    scaled, grads = backward_call(blocks[:1], sides, [[c_own]], backward, tracks, scaling, "backward_own")
    parts = row_grad(scaled[0], in_proj, lanes)
    other_x = line.send(pack([near_x, away_x, side_x, corner_x], "pack_x"), "chan", 1)
    corner_side_x, corner_a, near_a, away_b, parts, other_x = line.step(corner_side_x, corner_a, near_a, away_b, parts, other_x)

    corner_b = line.send(away_b, "tm", 1)
    corner_side_a = line.send(corner_a, "chan", 2)
    side_a = line.send(away_a, "chan", 2)
    near_b1 = line.send(c_half_b[:quarter], "tm", 1)
    last_x = line.send(corner_side_x, "chan", 1)
    side_b = line.send(away_b, "chan", 2)
    xs = [x_own] + collected(place, [
        (near_x, mine_near), (away_x, mine_1), (side_x, mine_2), (corner_x, mine_3), (corner_side_x, mine_4),
        (other_x, their_near + their_1 + their_2 + their_3), (last_x, their_4),
    ], "collect_x")
    more, more_low = forward_call(blocks[1:], xs[1:], forward, "forward_group")
    tracks, lows = tracks + more, lows + more_low
    corner_side_a, side_a, side_b, corner_b, near_b1, lows[1] = line.step(corner_side_a, side_a, side_b, corner_b, near_b1, lows[1])

    corner_side_b = line.send(corner_b, "chan", 2)
    near_b2 = line.send(c_half_b[quarter:], "tm", 1)
    other_a = line.send(pack([near_a, away_a, side_a, corner_a, corner_side_a], "pack_a"), "chan", 1)
    own_a = lax.dynamic_slice_in_dim(c_own, side * (depth // 2), depth // 2, axis=1)
    ca = [own_a] + collected(place, [
        (near_a, mine_near), (away_a, mine_1), (side_a, mine_2), (corner_a, mine_3), (corner_side_a, mine_4),
        (other_a, their_near + their_1 + their_2 + their_3 + their_4),
    ], "collect_a")

    def shares(features, values, block, factor, name):
        return [grad_rows(block ^ (2 * k), features, values, rows_out, factor, name) for k in range(1, groups)]

    out_given = shares(ca, lows, me % far, scaling, "out_grad")
    out_given[0], corner_side_b, near_b2 = line.step(out_given[0], corner_side_b, near_b2)

    out_got = [line.send(part, "tm", 2 * (k + 1)) for k, part in enumerate(out_given)]
    other_b = line.send(pack([away_b, side_b, corner_b, corner_side_b, near_b1, near_b2], "pack_b"), "chan", 1)
    cb = collected(place, [
        (near_b1, [(0, 6, quarter)]), (near_b2, [(0, 7, quarter)]),
        (away_b, mine_1), (side_b, mine_2), (corner_b, mine_3), (corner_side_b, mine_4),
        (other_b, their_1 + their_2 + their_3 + their_4 + [(0, 8, quarter), (0, 9, quarter)]),
    ], "collect_b")
    cs = [list(pair) for pair in zip(ca[1:], cb, strict=True)]
    more, more_grads = backward_call(blocks[1:], sides, cs, backward, tracks[1:], scaling, "backward_group")
    scaled, grads = scaled + more, grads + more_grads
    in_given = shares(xs, scaled, me, None, "in_grad")
    in_given[0] = line.step(in_given[0])
    in_got = [line.send(part, "tm", 2 * (k + 1)) for k, part in enumerate(in_given)]
    out_got[0] = line.step(out_got[0])
    decay_grad = (grads[0] + grads[1]) + (grads[2] + grads[3])
    bit = 2
    while bit < far:
        decay_grad += line.send(decay_grad, "tm", bit)
        bit *= 2
    bit = 1
    while bit < lanes:
        parts = parts.reshape(-1, 2, *parts.shape[1:])
        turn = (lane // bit) % 2
        keep = lax.dynamic_index_in_dim(parts, turn, axis=1, keepdims=False)
        give = lax.dynamic_index_in_dim(parts, 1 - turn, axis=1, keepdims=False)
        parts = keep + line.send(give, "chan", bit)
        bit *= 2
    input_grad = parts[0].astype(BF16)
    in_got[0] = after(in_got[0], input_grad)

    out_proj_grad = sum(out_got, grad_rows(me % far, [line.behind(ca[0]), *ca[1:]], lows, rows_out, scaling, "out_grad"))
    in_proj_grad = sum(in_got, grad_rows(me, [line.behind(xs[0]), *xs[1:]], scaled, rows_out, None, "in_grad"))
    return (in_proj_grad, out_proj_grad, decay_grad[0], input_grad)


def solution(mesh):
    return jax.shard_map(
        per_device,
        mesh=mesh,
        in_specs=(
            P("tm", None),
            P("tm", None),
            P(None, "chan"),
            P("chan", None),
            P("chan"),
            P("chan"),
            P("tm"),
        ),
        out_specs=(P("tm", "chan"), P("tm", "chan"), P("chan"), P("tm", "chan")),
        check_vma=False,
    )
```

```python
import functools
import math

import jax
import jax.numpy as jnp
from jax import lax
from jax.experimental import pallas as pl
from jax.experimental.pallas import tpu as pltpu
from jax.sharding import PartitionSpec as P

F32 = jnp.float32
BF16 = jnp.bfloat16
SEG = 8
VMEM_LIMIT = 12 * 1024 * 1024


def swap(x, axis, bit):
    n = lax.axis_size(axis)
    return lax.ppermute(x, axis, [(k, k ^ bit) for k in range(n)])


def nn(a, b):
    return lax.dot_general(a, b, (((1,), (0,)), ((), ())), preferred_element_type=F32)


def nt(a, b):
    return lax.dot_general(a, b, (((1,), (1,)), ((), ())), preferred_element_type=F32)


def tn(a, b):
    return lax.dot_general(a, b, (((0,), (0,)), ((), ())), preferred_element_type=F32)


def order(rows, transpose=False):
    steps = rows // SEG
    r = lax.broadcasted_iota(jnp.int32, (rows, rows), 1 if transpose else 0)
    t = lax.broadcasted_iota(jnp.int32, (rows, rows), 0 if transpose else 1)
    return ((r % SEG) * steps + r // SEG == t).astype(F32).astype(BF16)


VMEM = pl.BlockSpec(memory_space=pltpu.VMEM)
SMEM = pl.BlockSpec(memory_space=pltpu.SMEM)


ANY = pl.BlockSpec(memory_space=pl.ANY)


def resident(kernel, out_shape, operands, name, scratch=(), scalars=1, anywhere=0):
    return pl.pallas_call(
        kernel,
        out_shape=out_shape,
        in_specs=[SMEM] * scalars + [VMEM] * (len(operands) - scalars - anywhere) + [ANY] * anywhere,
        out_specs=jax.tree.map(lambda _: VMEM, out_shape),
        scratch_shapes=scratch,
        compiler_params=pltpu.CompilerParams(vmem_limit_bytes=VMEM_LIMIT),
        cost_estimate=pl.CostEstimate(flops=0, transcendentals=0, bytes_accessed=0),
        name=name,
    )(*operands)


def ordered_rows(x_ref, p_ref, full):
    full[...] = nn(order(x_ref.shape[0]), x_ref[...])
    p_ref[...] = full[...].astype(BF16)


def prep_inputs_kernel(idx_ref, x_ref, p_ref, half_ref, quarter_ref, full):
    ordered_rows(x_ref, p_ref, full)
    half, quarter = half_ref.shape[0], quarter_ref.shape[0]
    half_ref[...] = full[pl.ds(pl.multiple_of(idx_ref[0] * half, half), half), :]
    quarter_ref[...] = full[pl.ds(pl.multiple_of(idx_ref[1] * quarter, quarter), quarter), :]


def prep_cotangent_kernel(idx_ref, x_ref, p_ref, first_a_ref, first_b_ref, second_ref, away_a_ref, away_b_ref, full):
    ordered_rows(x_ref, p_ref, full)
    quarter, width = first_a_ref.shape
    cols = [pl.ds(pl.multiple_of(idx_ref[2 + k] * width, width), width) for k in range(2)]
    first = pl.ds(pl.multiple_of(idx_ref[0] * 2 * quarter, quarter), quarter)
    second = pl.ds(pl.multiple_of(idx_ref[0] * 2 * quarter + quarter, quarter), quarter)
    away = pl.ds(pl.multiple_of(idx_ref[1] * quarter, quarter), quarter)
    first_a_ref[...] = full[first, cols[0]]
    first_b_ref[...] = full[first, cols[1]]
    second_ref[:, :width] = full[second, cols[0]]
    second_ref[:, width:] = full[second, cols[1]]
    away_a_ref[...] = full[away, cols[1]]
    away_b_ref[...] = full[away, cols[0]]


def prep(kernel, idx, x, shapes, name):
    rows, depth = x.shape
    shapes = (jax.ShapeDtypeStruct((rows, depth), BF16), *[jax.ShapeDtypeStruct(shape, F32) for shape in shapes])
    return resident(kernel, shapes, (idx, x), name, [pltpu.VMEM((rows, depth), F32)])


def pack_kernel(*refs):
    *pieces, out_ref, sems = refs
    copies, at = [], 0
    for k, ref in enumerate(pieces):
        copies.append(pltpu.make_async_copy(ref, out_ref.at[pl.ds(at, ref.shape[0]), :], sems.at[k]))
        at += ref.shape[0]
    for copy in copies:
        copy.start()
    for copy in copies:
        copy.wait()


def pack(pieces, name):
    shape = jax.ShapeDtypeStruct((sum(p.shape[0] for p in pieces), pieces[0].shape[1]), F32)
    return resident(pack_kernel, shape, tuple(pieces), name, [pltpu.SemaphoreType.DMA((len(pieces),))], scalars=0, anywhere=len(pieces))


def lanes_of(l):
    return slice(128 * l, 128 * (l + 1))


def scan_ends(src, retain_ref, base, decays, reverse):
    count, steps = src.shape[1] // 128, src.shape[0] // SEG

    def lap(k, carry):
        j = steps - 1 - k if reverse else k
        rows = pl.ds(pl.multiple_of(j * SEG, SEG), SEG)
        kept = retain_ref[pl.ds(pl.multiple_of(base + j * SEG, SEG), SEG), :]
        out = []
        for l in range(count):
            end, rate = carry[l]
            factor = kept * decays[l]
            value = src[rows, lanes_of(l)]
            end = factor * (value + end) if reverse else factor * end + value
            out.append((end, factor * rate))
        return tuple(out)

    start = tuple((jnp.zeros((SEG, 128), F32), jnp.ones((SEG, 128), F32)) for _ in range(count))
    ends = lax.fori_loop(0, steps, lap, start, unroll=4)
    return jnp.concatenate([e[0] for e in ends], axis=1), jnp.concatenate([e[1] for e in ends], axis=1)


def seg_starts(end, rate, entering, reverse):
    now = entering
    starts = [None] * SEG
    for k in range(SEG):
        s = SEG - 1 - k if reverse else k
        starts[s] = now
        now = end[s : s + 1] + rate[s : s + 1] * now
    return jnp.concatenate(starts, axis=0), now


def decay_tiles(decay_ref):
    width = decay_ref.shape[1]
    full = jnp.broadcast_to(decay_ref[...], (SEG, width))
    return [full[:, lanes_of(l)] for l in range(width // 128)]


def summary_kernel(x_ref, c_ref, w_ref, v_ref, scale_ref, decay_ref, retain_ref, out_ref, drive, scot, *, scaling):
    decays = decay_tiles(decay_ref)
    drive[...] = nn(x_ref[...], w_ref[...]) * scale_ref[...]
    scot[...] = nt(c_ref[...], v_ref[...]) * scaling
    zero = jnp.zeros(decay_ref.shape, F32)
    end, rate = scan_ends(drive, retain_ref, 0, decays, False)
    _, forward = seg_starts(end, rate, zero, False)
    back, _ = scan_ends(scot, retain_ref, 0, decays, True)
    _, backward = seg_starts(back, rate, zero, True)
    total = rate[0:1]
    for s in range(1, SEG):
        total = total * rate[s : s + 1]
    out_ref[...] = jnp.concatenate([total, forward, backward], axis=0)


def carries_kernel(idx_ref, sum_ref, fwd_ref, bwd_ref, retain_ref):
    blocks = sum_ref.shape[0]
    far = blocks // 2

    def row(b):
        away = idx_ref[0] ^ b
        top = away // far
        low = (away % 2) ^ top
        middle = ((away // 2) % (far // 2)) ^ low
        return sum_ref[middle + (far // 2) * low + far * top]

    now = jnp.zeros_like(fwd_ref[0:1, :])
    for b in range(blocks):
        fwd_ref[b : b + 1, :] = now
        ends = row(b)
        retain_ref[b : b + 1, :] = ends[3:4]
        now = ends[1:2] + ends[0:1] * now
    now = jnp.zeros_like(now)
    for b in range(blocks - 1, -1, -1):
        bwd_ref[b : b + 1, :] = now
        ends = row(b)
        now = ends[2:3] + ends[0:1] * now


def carries(me, table):
    shape = jax.ShapeDtypeStruct((table.shape[0], table.shape[2]), F32)
    return resident(carries_kernel, (shape,) * 3, (me, table), "carries")


def reach(devices):
    return [1 << k for k in range(1, devices.bit_length() - 2)] + [3, devices // 2 + 1]


def collect_kernel(idx_ref, *refs, layout):
    count = len(layout)
    outs = refs[count : count + 3]
    held, sems = refs[count + 3], refs[count + 4]
    copies, at = [], 0
    for k, ref in enumerate(refs[:count]):
        copies.append(pltpu.make_async_copy(ref, held.at[pl.ds(at, ref.shape[0]), :], sems.at[k]))
        at += ref.shape[0]
    for copy in copies:
        copy.start()
    start = 0
    for copy, parts in zip(copies, layout, strict=True):
        copy.wait()
        for role, slot, rows in parts:
            at = pl.multiple_of(idx_ref[slot] * rows, rows)
            outs[role][pl.ds(at, rows), :] = held[start : start + rows, :].astype(BF16)
            start += rows


def collected(place, pieces, name):
    rows = sum(part[2] for _, parts in pieces for part in parts)
    depth = pieces[0][0].shape[1]
    shape = jax.ShapeDtypeStruct((rows // 3, depth), BF16)
    kernel = functools.partial(collect_kernel, layout=[parts for _, parts in pieces])
    scratch = [pltpu.VMEM((rows, depth), F32), pltpu.SemaphoreType.DMA((len(pieces),))]
    return list(resident(kernel, (shape,) * 3, (place, *[array for array, _ in pieces]), name, scratch, anywhere=len(pieces)))


def forward_kernel(idx_ref, *refs, roles):
    xs = refs[:roles]
    w_ref, scale_ref, decay_ref, retain_ref, enter_ref = refs[roles : roles + 5]
    outs = refs[roles + 5 : -2]
    drive, state = refs[-2:]
    decays = decay_tiles(decay_ref)
    count = len(decays)
    rows_all = drive.shape[0]
    steps = rows_all // SEG
    for role in range(roles):
        start_ref, low_ref = outs[2 * role : 2 * role + 2]
        block = idx_ref[role]
        base = block * rows_all
        drive[...] = nn(xs[role][...], w_ref[...]) * scale_ref[...]
        end, rate = scan_ends(drive, retain_ref, base, decays, False)
        start, _ = seg_starts(end, rate, enter_ref[pl.ds(block, 1), :], False)
        start_ref[...] = start

        def lap(j, before, base=base):
            at = pl.multiple_of(j * SEG, SEG)
            kept = retain_ref[pl.ds(pl.multiple_of(base + j * SEG, SEG), SEG), :]
            out = []
            for l in range(count):
                now = kept * decays[l] * before[l] + drive[pl.ds(at, SEG), lanes_of(l)]
                state[pl.ds(at, SEG), lanes_of(l)] = now
                out.append(now)
            return tuple(out)

        lax.fori_loop(0, steps, lap, tuple(start[:, lanes_of(l)] for l in range(count)), unroll=4)
        low_ref[...] = state[...].astype(BF16)


def backward_kernel(idx_ref, side_ref, *refs, roles, parts, scaling):
    cs = refs[: roles * parts]
    v_ref, scale_ref, decay_ref, retain_ref, enter_ref = refs[roles * parts : roles * parts + 5]
    entering = refs[roles * parts + 5 : roles * parts + 5 + 2 * roles]
    outs = refs[roles * parts + 5 + 2 * roles : -3]
    scot, adjoint, track = refs[-3:]
    decays = decay_tiles(decay_ref)
    count = len(decays)
    rows_all = scot.shape[0]
    steps = rows_all // SEG
    width = v_ref.shape[1] // parts
    for role in range(roles):
        scaled_ref, grad_ref = outs[2 * role : 2 * role + 2]
        block = idx_ref[role]
        base = block * rows_all
        if parts == 1:
            scot[...] = nt(cs[role][...], v_ref[...]) * scaling
        else:
            total = None
            for k in range(parts):
                cols = pl.ds(pl.multiple_of(side_ref[k] * width, width), width)
                part = nt(cs[parts * role + k][...], v_ref[:, cols])
                total = part if total is None else total + part
            scot[...] = total * scaling
        end, rate = scan_ends(scot, retain_ref, base, decays, True)
        start, _ = seg_starts(end, rate, enter_ref[pl.ds(block, 1), :], True)

        start_ref, low_ref = entering[2 * role : 2 * role + 2]
        track[0:SEG, :] = start_ref[...]
        track[SEG:, :] = low_ref[...].astype(F32)

        def lap(k, carry, base=base):
            at = (steps - 1 - k) * SEG
            rows = pl.ds(pl.multiple_of(at, SEG), SEG)
            kept = retain_ref[pl.ds(pl.multiple_of(base + at, SEG), SEG), :]
            out = []
            for l in range(count):
                follow, grad = carry[l]
                here = scot[rows, lanes_of(l)] + follow
                adjoint[rows, lanes_of(l)] = here
                part = kept * here
                out.append((part * decays[l], grad + part * track[rows, lanes_of(l)]))
            return tuple(out)

        begin = tuple((start[:, lanes_of(l)], jnp.zeros((SEG, 128), F32)) for l in range(count))
        done = lax.fori_loop(0, steps, lap, begin, unroll=4)
        scaled_ref[...] = (adjoint[...] * scale_ref[...]).astype(BF16)
        grad_ref[...] = jnp.sum(jnp.concatenate([d[1] for d in done], axis=1), axis=0, keepdims=True)


def forward_call(blocks, xs, operands, name):
    channels = operands[1].shape[1]
    rows, roles = xs[0].shape[0], len(xs)
    shapes = (jax.ShapeDtypeStruct((SEG, channels), F32), jax.ShapeDtypeStruct((rows, channels), BF16)) * roles
    out = resident(
        functools.partial(forward_kernel, roles=roles), shapes, (blocks, *xs, *operands), name,
        [pltpu.VMEM((rows, channels), F32)] * 2,
    )
    return list(out[::2]), list(out[1::2])


def backward_call(blocks, sides, cs, operands, starts, lows, scaling, name):
    channels = operands[1].shape[1]
    rows, roles = cs[0][0].shape[0], len(cs)
    kernel = functools.partial(backward_kernel, roles=roles, parts=len(cs[0]), scaling=scaling)
    shapes = (jax.ShapeDtypeStruct((rows, channels), BF16), jax.ShapeDtypeStruct((1, channels), F32)) * roles
    out = resident(
        kernel, shapes, (blocks, sides, *[part for c in cs for part in c], *operands, *[r for pair in zip(starts, lows, strict=True) for r in pair]), name,
        [pltpu.VMEM((rows, channels), F32)] * 2 + [pltpu.VMEM((SEG + rows, channels), F32)], scalars=2,
    )
    return list(out[::2]), list(out[1::2])


def grad_kernel(idx_ref, *refs, count, factor):
    features, values, sums, out_ref = refs[:count], refs[count : 2 * count], refs[2 * count : -1], refs[-1]
    width = out_ref.shape[0] - (SEG if sums else 0)
    at = pl.ds(pl.multiple_of(idx_ref[0] * width, width), width)
    total = tn(features[0][:, at], values[0][...])
    for k in range(1, count):
        total += tn(features[k][:, at], values[k][...])
    out_ref[0:width, :] = total * factor if factor is not None else total
    if sums:
        row = (sums[0][...] + sums[1][...]) + (sums[2][...] + sums[3][...])
        out_ref[width:, :] = jnp.broadcast_to(row, (SEG, row.shape[1]))


def grad_rows(at, features, values, rows_out, factor, name, sums=()):
    channels = values[0].shape[1]
    if rows_out % 128:
        total = sum(
            tn(lax.dynamic_slice_in_dim(x, at * rows_out, rows_out, axis=1), v) for x, v in zip(features, values, strict=True)
        )
        total = total * factor if factor is not None else total
        if sums:
            row = (sums[0] + sums[1]) + (sums[2] + sums[3])
            total = jnp.concatenate([total, jnp.broadcast_to(row, (SEG, channels))], axis=0)
        return total
    return resident(
        functools.partial(grad_kernel, count=len(values), factor=factor),
        jax.ShapeDtypeStruct((rows_out + (SEG if sums else 0), channels), F32),
        (jnp.reshape(at, (1,)).astype(jnp.int32), *features, *values, *sums), name,
    )


def row_grad_kernel(a_ref, w_ref, out_ref):
    parts, rows, width = out_ref.shape
    a = nn(order(rows, True), a_ref[...]).astype(BF16)
    for k in range(parts):
        out_ref[k] = nt(a, w_ref[width * k : width * (k + 1), :])


def row_grad(scaled, in_proj, parts):
    rows, channels = scaled.shape
    depth = in_proj.shape[0]
    return resident(
        row_grad_kernel, jax.ShapeDtypeStruct((parts, rows, depth // parts), F32), (scaled, in_proj), "row_grad",
        scalars=0,
    )


def after(x, *others):
    return lax.optimization_barrier((x, *others))[0]


class Order:
    def __init__(self):
        self.last = None

    def behind(self, x):
        return x if self.last is None else lax.optimization_barrier((x, self.last))[0]

    def step(self, *results):
        held = results if self.last is None else (*results, self.last)
        results = lax.optimization_barrier(held)[: len(results)]
        self.last = results[0]
        return results[0] if len(results) == 1 else results

    def send(self, x, axis, bit):
        return swap(self.behind(x), axis, bit)


def per_device(inputs, cotangent, in_proj, out_proj, decays, input_scale, retain):
    rows, depth = inputs.shape
    channels = in_proj.shape[1]
    devices, lanes = lax.axis_size("tm"), lax.axis_size("chan")
    scaling = 1.0 / math.sqrt(rows * devices)
    me, lane = lax.axis_index("tm"), lax.axis_index("chan")
    far = devices // 2
    groups = devices // 4
    steps = rows // SEG
    scale = input_scale[None, :]
    decay_row = decays[None, :]
    side = me // far

    half, quarter = rows // 2, rows // 4
    rows_out = depth // devices
    core = lane % 2
    place = [core, 1 - core, lane, lane ^ 2, lane ^ 1, lane ^ 3, 2 * core, 2 * core + 1, 2 - 2 * core, 3 - 2 * core]
    place = jnp.stack(place).astype(jnp.int32)
    blocks = jnp.stack([me, me ^ 1, me ^ far, me ^ far ^ 1]).astype(jnp.int32)
    sides = jnp.stack([side, 1 - side]).astype(jnp.int32)
    mine_near, mine_1, mine_2, mine_3, mine_4 = (
        [(0, 0, half)], [(1, 2, quarter)], [(1, 3, quarter)], [(2, 2, quarter)], [(2, 3, quarter)],
    )
    their_near, their_1, their_2, their_3, their_4 = (
        [(0, 1, half)], [(1, 4, quarter)], [(1, 5, quarter)], [(2, 4, quarter)], [(2, 5, quarter)],
    )

    def ordered(r):
        return r.reshape(-1, SEG, steps).swapaxes(1, 2).reshape(-1, 1)

    line = Order()
    where = jnp.stack([lane % 2, lane, side * 0]).astype(jnp.int32)
    x_own, x_half, x_quarter = line.step(
        *prep(prep_inputs_kernel, where, inputs, [(half, depth), (quarter, depth)], "prep_inputs")
    )
    near_x = line.send(x_half, "tm", 1)
    away_x = line.send(x_quarter, "tm", far)
    where = jnp.stack([lane % 2, lane, side, 1 - side]).astype(jnp.int32)
    part = (quarter, depth // 2)
    c_own, c_first_a, c_first_b, c_second, c_quarter_a, c_quarter_b = prep(
        prep_cotangent_kernel, where, line.behind(cotangent), [part, part, (quarter, depth), part, part], "prep_cotangent"
    )
    ends = resident(
        functools.partial(summary_kernel, scaling=scaling), jax.ShapeDtypeStruct((3, channels), F32),
        (x_own, c_own, in_proj, out_proj, scale, decay_row, jnp.broadcast_to(ordered(retain), (rows, 128))), "summary",
        [pltpu.VMEM((rows, channels), F32)] * 2, scalars=0,
    )
    table = jnp.concatenate([ends, jnp.pad(retain, (0, channels - rows))[None, :]], axis=0)[None]
    if groups == 2:
        table = jnp.concatenate([table] + [line.send(table, "tm", bit) for bit in (2, 3, 1)])
    else:
        for bit in reach(devices)[:-1]:
            table = jnp.concatenate([table, line.send(table, "tm", bit)])
    near_x, away_x, table = line.step(near_x, away_x, table)

    corner_x = line.send(away_x, "tm", 1)
    side_x = line.send(away_x, "chan", 2)
    away_a = line.send(c_quarter_a, "tm", far)
    table = jnp.concatenate([table, line.send(table, "tm", reach(devices)[-1])])
    enter_fwd, enter_bwd, retain_all = carries(me[None].astype(jnp.int32), table)
    corner_x, side_x, away_a, enter_fwd = line.step(corner_x, side_x, away_a, enter_fwd)

    near_a1 = line.send(c_first_a, "tm", 1)
    corner_a = line.send(away_a, "tm", 1)
    corner_side_x = line.send(corner_x, "chan", 2)
    away_b = line.send(c_quarter_b, "tm", far)
    retain_wide = jnp.broadcast_to(ordered(retain_all[:, :rows]), (devices * rows, 128))
    forward = (in_proj, scale, decay_row, retain_wide, enter_fwd)
    backward = (out_proj, scale, decay_row, retain_wide, enter_bwd)
    starts, lows = forward_call(blocks[:1], [x_own], forward, "forward_own")
    scaled, grads = backward_call(blocks[:1], sides, [[c_own]], backward, starts, lows, scaling, "backward_own")
    parts = row_grad(scaled[0], in_proj, lanes)
    other_x = line.send(pack([near_x, away_x, side_x, corner_x], "pack_x"), "chan", 1)
    corner_side_x, corner_a, near_a1, away_b, parts, other_x = line.step(corner_side_x, corner_a, near_a1, away_b, parts, other_x)

    corner_b = line.send(away_b, "tm", 1)
    corner_side_a = line.send(corner_a, "chan", 2)
    side_a = line.send(away_a, "chan", 2)
    near_2 = line.send(c_second, "tm", 1)
    last_x = line.send(corner_side_x, "chan", 1)
    side_b = line.send(away_b, "chan", 2)
    xs = [x_own] + collected(place, [
        (near_x, mine_near), (away_x, mine_1), (side_x, mine_2), (corner_x, mine_3), (corner_side_x, mine_4),
        (other_x, their_near + their_1 + their_2 + their_3), (last_x, their_4),
    ], "collect_x")
    more, more_low = forward_call(blocks[1:], xs[1:], forward, "forward_group")
    starts, lows = starts + more, lows + more_low
    corner_side_a, side_a, side_b, corner_b, near_2, lows[1] = line.step(corner_side_a, side_a, side_b, corner_b, near_2, lows[1])
    near_a2, near_b2 = near_2[:, : depth // 2], near_2[:, depth // 2 :]

    corner_side_b = line.send(corner_b, "chan", 2)
    near_b1 = line.send(c_first_b, "tm", 1)
    other_a = line.send(pack([near_a1, near_a2, away_a, side_a, corner_a, corner_side_a], "pack_a"), "chan", 1)
    own_a = lax.dynamic_slice_in_dim(c_own, side * (depth // 2), depth // 2, axis=1)
    ca = [own_a] + collected(place, [
        (near_a1, [(0, 6, quarter)]), (near_a2, [(0, 7, quarter)]),
        (away_a, mine_1), (side_a, mine_2), (corner_a, mine_3), (corner_side_a, mine_4),
        (other_a, [(0, 8, quarter), (0, 9, quarter)] + their_1 + their_2 + their_3 + their_4),
    ], "collect_a")

    def shares(features, values, block, factor, name, sums=()):
        return [grad_rows(block ^ (2 * k), features, values, rows_out, factor, name, sums) for k in range(1, groups)]

    out_given = shares(ca, lows, me % far, scaling, "out_grad")
    out_given[0], corner_side_b, near_b1 = line.step(out_given[0], corner_side_b, near_b1)

    out_got = [line.send(part, "tm", 2 * (k + 1)) for k, part in enumerate(out_given)]
    near_b1_other = line.send(near_b1, "chan", 1)
    near_b2_other = line.send(near_b2, "chan", 1)
    away_b_other = line.send(away_b, "chan", 1)
    other_b = line.send(pack([side_b, corner_b, corner_side_b], "pack_b"), "chan", 1)
    cb = collected(place, [
        (near_b1, [(0, 6, quarter)]), (near_b2, [(0, 7, quarter)]),
        (away_b, mine_1), (side_b, mine_2), (corner_b, mine_3), (corner_side_b, mine_4),
        (near_b1_other, [(0, 8, quarter)]), (near_b2_other, [(0, 9, quarter)]), (away_b_other, their_1),
        (other_b, their_2 + their_3 + their_4),
    ], "collect_b")
    cs = [list(pair) for pair in zip(ca[1:], cb, strict=True)]
    more, more_grads = backward_call(blocks[1:], sides, cs, backward, starts[1:], lows[1:], scaling, "backward_group")
    scaled, grads = scaled + more, grads + more_grads
    in_given = shares(xs, scaled, me, None, "in_grad", grads)
    in_given[0] = line.step(in_given[0])
    in_got = [line.send(part, "tm", 2 * (k + 1)) for k, part in enumerate(in_given)]
    out_got[0] = line.step(out_got[0])
    bit = 1
    while bit < lanes:
        parts = parts.reshape(-1, 2, *parts.shape[1:])
        turn = (lane // bit) % 2
        keep = lax.dynamic_index_in_dim(parts, turn, axis=1, keepdims=False)
        give = lax.dynamic_index_in_dim(parts, 1 - turn, axis=1, keepdims=False)
        parts = keep + line.send(give, "chan", bit)
        bit *= 2
    input_grad = parts[0].astype(BF16)
    in_got[0] = after(in_got[0], input_grad)

    out_proj_grad = sum(out_got, grad_rows(me % far, [line.behind(ca[0]), *ca[1:]], lows, rows_out, scaling, "out_grad"))
    in_mine = grad_rows(me, [line.behind(xs[0]), *xs[1:]], scaled, rows_out, None, "in_grad", grads)
    in_proj_grad = sum((part[:rows_out] for part in in_got), in_mine[:rows_out])
    decay_grad = sum((part[rows_out] for part in in_got), in_mine[rows_out])
    if groups > 2:
        decay_grad = in_mine[rows_out]
        bit = 2
        while bit < far:
            decay_grad += swap(decay_grad, "tm", bit)
            bit *= 2
    return (in_proj_grad, out_proj_grad, decay_grad, input_grad)


def solution(mesh):
    return jax.shard_map(
        per_device,
        mesh=mesh,
        in_specs=(
            P("tm", None),
            P("tm", None),
            P(None, "chan"),
            P("chan", None),
            P("chan"),
            P("chan"),
            P("tm"),
        ),
        out_specs=(P("tm", "chan"), P("tm", "chan"), P("chan"), P("tm", "chan")),
        check_vma=False,
    )
```

```python
import functools
import math

import jax
import jax.numpy as jnp
from jax import lax
from jax.experimental import pallas as pl
from jax.experimental.pallas import tpu as pltpu
from jax.sharding import PartitionSpec as P

F32 = jnp.float32
BF16 = jnp.bfloat16
SEG = 8
CORE, LANE, SIDES, PLACES, BLOCKS, SELF, ROWS = 0, 1, 2, 4, 14, 18, 19
VMEM_LIMIT = 12 * 1024 * 1024


def swap(x, axis, bit):
    n = lax.axis_size(axis)
    return lax.ppermute(x, axis, [(k, k ^ bit) for k in range(n)])


def nn(a, b):
    return lax.dot_general(a, b, (((1,), (0,)), ((), ())), preferred_element_type=F32)


def nt(a, b):
    return lax.dot_general(a, b, (((1,), (1,)), ((), ())), preferred_element_type=F32)


def tn(a, b):
    return lax.dot_general(a, b, (((0,), (0,)), ((), ())), preferred_element_type=F32)


def order_of(rows, transpose=False):
    steps = rows // SEG
    r = lax.broadcasted_iota(jnp.int32, (rows, rows), 1 if transpose else 0)
    t = lax.broadcasted_iota(jnp.int32, (rows, rows), 0 if transpose else 1)
    return (r % SEG) * steps + r // SEG == t


def order(rows, transpose=False):
    return order_of(rows, transpose).astype(F32).astype(BF16)


VMEM = pl.BlockSpec(memory_space=pltpu.VMEM)
SMEM = pl.BlockSpec(memory_space=pltpu.SMEM)


ANY = pl.BlockSpec(memory_space=pl.ANY)


def resident(kernel, out_shape, operands, name, scratch=(), scalars=1, anywhere=0):
    return pl.pallas_call(
        kernel,
        out_shape=out_shape,
        in_specs=[SMEM] * scalars + [VMEM] * (len(operands) - scalars - anywhere) + [ANY] * anywhere,
        out_specs=jax.tree.map(lambda _: VMEM, out_shape),
        scratch_shapes=scratch,
        compiler_params=pltpu.CompilerParams(vmem_limit_bytes=VMEM_LIMIT),
        cost_estimate=pl.CostEstimate(flops=0, transcendentals=0, bytes_accessed=0),
        name=name,
    )(*operands)


def ordered_rows(x_ref, p_ref, full):
    full[...] = nn(order(x_ref.shape[0]), x_ref[...])
    p_ref[...] = full[...].astype(BF16)


def prep_inputs_kernel(idx_ref, x_ref, p_ref, half_ref, quarter_ref, full):
    ordered_rows(x_ref, p_ref, full)
    half, quarter = half_ref.shape[0], quarter_ref.shape[0]
    half_ref[...] = full[pl.ds(pl.multiple_of(idx_ref[CORE] * half, half), half), :]
    quarter_ref[...] = full[pl.ds(pl.multiple_of(idx_ref[LANE] * quarter, quarter), quarter), :]


def prep_cotangent_kernel(idx_ref, x_ref, p_ref, own_a_ref, first_a_ref, first_b_ref, second_ref, away_a_ref, away_b_ref, full):
    ordered_rows(x_ref, p_ref, full)
    quarter, width = first_a_ref.shape
    cols = [pl.ds(pl.multiple_of(idx_ref[SIDES + k] * width, width), width) for k in range(2)]
    first = pl.ds(pl.multiple_of(idx_ref[CORE] * 2 * quarter, quarter), quarter)
    second = pl.ds(pl.multiple_of(idx_ref[CORE] * 2 * quarter + quarter, quarter), quarter)
    away = pl.ds(pl.multiple_of(idx_ref[LANE] * quarter, quarter), quarter)
    own_a_ref[...] = full[:, cols[0]].astype(BF16)
    first_a_ref[...] = full[first, cols[0]]
    first_b_ref[...] = full[first, cols[1]]
    second_ref[:, :width] = full[second, cols[0]]
    second_ref[:, width:] = full[second, cols[1]]
    away_a_ref[...] = full[away, cols[1]]
    away_b_ref[...] = full[away, cols[0]]


def prep(kernel, idx, x, shapes, name):
    rows, depth = x.shape
    shapes = [jax.ShapeDtypeStruct(shape, kind) for shape, kind in shapes]
    return resident(kernel, (jax.ShapeDtypeStruct((rows, depth), BF16), *shapes), (idx, x), name, [pltpu.VMEM((rows, depth), F32)])


def pack_kernel(*refs):
    *pieces, out_ref, sems = refs
    copies, at = [], 0
    for k, ref in enumerate(pieces):
        copies.append(pltpu.make_async_copy(ref, out_ref.at[pl.ds(at, ref.shape[0]), :], sems.at[k]))
        at += ref.shape[0]
    for copy in copies:
        copy.start()
    for copy in copies:
        copy.wait()


def pack(pieces, name):
    shape = jax.ShapeDtypeStruct((sum(p.shape[0] for p in pieces), pieces[0].shape[1]), F32)
    return resident(pack_kernel, shape, tuple(pieces), name, [pltpu.SemaphoreType.DMA((len(pieces),))], scalars=0, anywhere=len(pieces))


def lanes_of(l):
    return slice(128 * l, 128 * (l + 1))


def scan_ends(src, retain_ref, base, decays, reverse):
    count, steps = src.shape[1] // 128, src.shape[0] // SEG

    def lap(k, carry):
        j = steps - 1 - k if reverse else k
        rows = pl.ds(pl.multiple_of(j * SEG, SEG), SEG)
        kept = retain_ref[pl.ds(pl.multiple_of(base + j * SEG, SEG), SEG), :]
        out = []
        for l in range(count):
            end, rate = carry[l]
            factor = kept * decays[l]
            value = src[rows, lanes_of(l)]
            end = factor * (value + end) if reverse else factor * end + value
            out.append((end, factor * rate))
        return tuple(out)

    start = tuple((jnp.zeros((SEG, 128), F32), jnp.ones((SEG, 128), F32)) for _ in range(count))
    ends = lax.fori_loop(0, steps, lap, start, unroll=4)
    return jnp.concatenate([e[0] for e in ends], axis=1), jnp.concatenate([e[1] for e in ends], axis=1)


def seg_starts(end, rate, entering, reverse):
    now = entering
    starts = [None] * SEG
    for k in range(SEG):
        s = SEG - 1 - k if reverse else k
        starts[s] = now
        now = end[s : s + 1] + rate[s : s + 1] * now
    return jnp.concatenate(starts, axis=0), now


def decay_tiles(decay_ref):
    width = decay_ref.shape[1]
    full = jnp.broadcast_to(decay_ref[...], (SEG, width))
    return [full[:, lanes_of(l)] for l in range(width // 128)]


def spread_rows(row, out_ref, at):
    rows = row.shape[1]
    column = jnp.sum(jnp.where(order_of(rows), row, 0.0), axis=1, keepdims=True)
    out_ref[at : at + rows, :] = jnp.broadcast_to(column, (rows, 128))


def summary_kernel(x_ref, c_ref, w_ref, v_ref, scale_ref, decay_ref, kept_ref, out_ref, drive, scot, retain_ref, *, scaling):
    decays = decay_tiles(decay_ref)
    spread_rows(kept_ref[...], retain_ref, 0)
    drive[...] = nn(x_ref[...], w_ref[...]) * scale_ref[...]
    scot[...] = nt(c_ref[...], v_ref[...]) * scaling
    zero = jnp.zeros(decay_ref.shape, F32)
    end, rate = scan_ends(drive, retain_ref, 0, decays, False)
    _, forward = seg_starts(end, rate, zero, False)
    back, _ = scan_ends(scot, retain_ref, 0, decays, True)
    _, backward = seg_starts(back, rate, zero, True)
    total = rate[0:1]
    for s in range(1, SEG):
        total = total * rate[s : s + 1]
    rest = zero.shape[1] - kept_ref.shape[1]
    kept = jnp.concatenate([kept_ref[...], zero[:, :rest]], axis=1) if rest else kept_ref[...]
    out_ref[0] = jnp.concatenate([total, forward, backward, kept], axis=0)


def carries_kernel(idx_ref, sum_ref, fwd_ref, bwd_ref, retain_ref):
    blocks = sum_ref.shape[0]
    far = blocks // 2
    rows = retain_ref.shape[0] // 4

    def row(away):
        top = away // far
        low = (away % 2) ^ top
        middle = ((away // 2) % (far // 2)) ^ low
        return sum_ref[middle + (far // 2) * low + far * top]

    for role, away in enumerate((0, 1, far, far + 1)):
        spread_rows(row(away)[3:4, :rows], retain_ref, role * rows)
    now = jnp.zeros_like(fwd_ref[0:1, :])
    for b in range(blocks):
        fwd_ref[b : b + 1, :] = now
        ends = row(idx_ref[SELF] ^ b)
        now = ends[1:2] + ends[0:1] * now
    now = jnp.zeros_like(now)
    for b in range(blocks - 1, -1, -1):
        bwd_ref[b : b + 1, :] = now
        ends = row(idx_ref[SELF] ^ b)
        now = ends[2:3] + ends[0:1] * now


def carries(idx, table, rows):
    shape = jax.ShapeDtypeStruct((table.shape[0], table.shape[2]), F32)
    return resident(carries_kernel, (shape, shape, jax.ShapeDtypeStruct((4 * rows, 128), F32)), (idx, table), "carries")


def reach(devices):
    return [1 << k for k in range(1, devices.bit_length() - 2)] + [3, devices // 2 + 1]


def collect_kernel(idx_ref, *refs, layout):
    count = len(layout)
    outs = refs[count : count + 3]
    held, sems = refs[count + 3], refs[count + 4]
    copies, at = [], 0
    for k, ref in enumerate(refs[:count]):
        copies.append(pltpu.make_async_copy(ref, held.at[pl.ds(at, ref.shape[0]), :], sems.at[k]))
        at += ref.shape[0]
    for copy in copies:
        copy.start()
    start = 0
    for copy, parts in zip(copies, layout, strict=True):
        copy.wait()
        for role, slot, rows in parts:
            at = pl.multiple_of(idx_ref[PLACES + slot] * rows, rows)
            outs[role][pl.ds(at, rows), :] = held[start : start + rows, :].astype(BF16)
            start += rows


def collected(idx, pieces, name):
    rows = sum(part[2] for _, parts in pieces for part in parts)
    depth = pieces[0][0].shape[1]
    shape = jax.ShapeDtypeStruct((rows // 3, depth), BF16)
    kernel = functools.partial(collect_kernel, layout=[parts for _, parts in pieces])
    scratch = [pltpu.VMEM((rows, depth), F32), pltpu.SemaphoreType.DMA((len(pieces),))]
    return list(resident(kernel, (shape,) * 3, (idx, *[array for array, _ in pieces]), name, scratch, anywhere=len(pieces)))


def forward_kernel(idx_ref, *refs, roles, first):
    xs = refs[:roles]
    w_ref, scale_ref, decay_ref, retain_ref, enter_ref = refs[roles : roles + 5]
    outs = refs[roles + 5 : -2]
    drive, state = refs[-2:]
    decays = decay_tiles(decay_ref)
    count = len(decays)
    rows_all = drive.shape[0]
    steps = rows_all // SEG
    for role in range(roles):
        start_ref, low_ref = outs[2 * role : 2 * role + 2]
        block = idx_ref[BLOCKS + first + role]
        base = (first + role) * rows_all
        drive[...] = nn(xs[role][...], w_ref[...]) * scale_ref[...]
        end, rate = scan_ends(drive, retain_ref, base, decays, False)
        start, _ = seg_starts(end, rate, enter_ref[pl.ds(block, 1), :], False)
        start_ref[...] = start

        def lap(j, before, base=base):
            at = pl.multiple_of(j * SEG, SEG)
            kept = retain_ref[pl.ds(pl.multiple_of(base + j * SEG, SEG), SEG), :]
            out = []
            for l in range(count):
                now = kept * decays[l] * before[l] + drive[pl.ds(at, SEG), lanes_of(l)]
                state[pl.ds(at, SEG), lanes_of(l)] = now
                out.append(now)
            return tuple(out)

        lax.fori_loop(0, steps, lap, tuple(start[:, lanes_of(l)] for l in range(count)), unroll=4)
        low_ref[...] = state[...].astype(BF16)


def backward_kernel(idx_ref, *refs, roles, parts, scaling, first):
    cs = refs[: roles * parts]
    v_ref, scale_ref, decay_ref, retain_ref, enter_ref = refs[roles * parts : roles * parts + 5]
    entering = refs[roles * parts + 5 : roles * parts + 5 + 2 * roles]
    outs = refs[roles * parts + 5 + 2 * roles : -3]
    scot, adjoint, track = refs[-3:]
    decays = decay_tiles(decay_ref)
    count = len(decays)
    rows_all = scot.shape[0]
    steps = rows_all // SEG
    width = v_ref.shape[1] // parts
    for role in range(roles):
        scaled_ref, grad_ref = outs[2 * role : 2 * role + 2]
        block = idx_ref[BLOCKS + first + role]
        base = (first + role) * rows_all
        if parts == 1:
            scot[...] = nt(cs[role][...], v_ref[...]) * scaling
        else:
            total = None
            for k in range(parts):
                cols = pl.ds(pl.multiple_of(idx_ref[SIDES + k] * width, width), width)
                part = nt(cs[parts * role + k][...], v_ref[:, cols])
                total = part if total is None else total + part
            scot[...] = total * scaling
        end, rate = scan_ends(scot, retain_ref, base, decays, True)
        start, _ = seg_starts(end, rate, enter_ref[pl.ds(block, 1), :], True)

        start_ref, low_ref = entering[2 * role : 2 * role + 2]
        track[0:SEG, :] = start_ref[...]
        track[SEG:, :] = low_ref[...].astype(F32)

        def lap(k, carry, base=base):
            at = (steps - 1 - k) * SEG
            rows = pl.ds(pl.multiple_of(at, SEG), SEG)
            kept = retain_ref[pl.ds(pl.multiple_of(base + at, SEG), SEG), :]
            out = []
            for l in range(count):
                follow, grad = carry[l]
                here = scot[rows, lanes_of(l)] + follow
                adjoint[rows, lanes_of(l)] = here
                part = kept * here
                out.append((part * decays[l], grad + part * track[rows, lanes_of(l)]))
            return tuple(out)

        begin = tuple((start[:, lanes_of(l)], jnp.zeros((SEG, 128), F32)) for l in range(count))
        done = lax.fori_loop(0, steps, lap, begin, unroll=4)
        scaled_ref[...] = (adjoint[...] * scale_ref[...]).astype(BF16)
        grad_ref[...] = jnp.sum(jnp.concatenate([d[1] for d in done], axis=1), axis=0, keepdims=True)


def forward_call(idx, first, xs, operands, name):
    channels = operands[1].shape[1]
    rows, roles = xs[0].shape[0], len(xs)
    shapes = (jax.ShapeDtypeStruct((SEG, channels), F32), jax.ShapeDtypeStruct((rows, channels), BF16)) * roles
    out = resident(
        functools.partial(forward_kernel, roles=roles, first=first), shapes, (idx, *xs, *operands), name,
        [pltpu.VMEM((rows, channels), F32)] * 2,
    )
    return list(out[::2]), list(out[1::2])


def backward_call(idx, first, cs, operands, starts, lows, scaling, name):
    channels = operands[1].shape[1]
    rows, roles = cs[0][0].shape[0], len(cs)
    kernel = functools.partial(backward_kernel, roles=roles, parts=len(cs[0]), scaling=scaling, first=first)
    shapes = (jax.ShapeDtypeStruct((rows, channels), BF16), jax.ShapeDtypeStruct((1, channels), F32)) * roles
    out = resident(
        kernel, shapes, (idx, *[part for c in cs for part in c], *operands, *[r for pair in zip(starts, lows, strict=True) for r in pair]), name,
        [pltpu.VMEM((rows, channels), F32)] * 2 + [pltpu.VMEM((SEG + rows, channels), F32)],
    )
    return list(out[::2]), list(out[1::2])


def grad_kernel(idx_ref, *refs, count, factor, which):
    features, values, sums, out_ref = refs[:count], refs[count : 2 * count], refs[2 * count : -1], refs[-1]
    width = out_ref.shape[0] - (SEG if sums else 0)
    at = pl.ds(pl.multiple_of(idx_ref[which] * width, width), width)
    total = tn(features[0][:, at], values[0][...])
    for k in range(1, count):
        total += tn(features[k][:, at], values[k][...])
    out_ref[0:width, :] = total * factor if factor is not None else total
    if sums:
        row = (sums[0][...] + sums[1][...]) + (sums[2][...] + sums[3][...])
        out_ref[width:, :] = jnp.broadcast_to(row, (SEG, row.shape[1]))


def grad_rows(idx, which, features, values, rows_out, factor, name, sums=()):
    channels = values[0].shape[1]
    if rows_out % 128:
        total = sum(
            tn(lax.dynamic_slice_in_dim(x, idx[which] * rows_out, rows_out, axis=1), v) for x, v in zip(features, values, strict=True)
        )
        total = total * factor if factor is not None else total
        if sums:
            row = (sums[0] + sums[1]) + (sums[2] + sums[3])
            total = jnp.concatenate([total, jnp.broadcast_to(row, (SEG, channels))], axis=0)
        return total
    return resident(
        functools.partial(grad_kernel, count=len(values), factor=factor, which=which),
        jax.ShapeDtypeStruct((rows_out + (SEG if sums else 0), channels), F32),
        (idx, *features, *values, *sums), name,
    )


def row_grad_kernel(idx_ref, a_ref, w_ref, keep_ref, give_ref):
    count, rows, width = keep_ref.shape
    a = nn(order(rows, True), a_ref[...]).astype(BF16)
    for k in range(count):
        for ref, flip in ((keep_ref, 0), (give_ref, 1)):
            at = (idx_ref[LANE] ^ (2 * k) ^ flip) * width
            ref[k] = nt(a, w_ref[pl.ds(pl.multiple_of(at, width), width), :])


def row_grad(idx, scaled, in_proj, parts):
    rows, channels = scaled.shape
    shape = jax.ShapeDtypeStruct((parts // 2, rows, in_proj.shape[0] // parts), F32)
    return resident(row_grad_kernel, (shape, shape), (idx, scaled, in_proj), "row_grad")


def after(x, *others):
    return lax.optimization_barrier((x, *others))[0]


class Order:
    def __init__(self):
        self.last = None

    def behind(self, x):
        return x if self.last is None else lax.optimization_barrier((x, self.last))[0]

    def step(self, *results):
        held = results if self.last is None else (*results, self.last)
        results = lax.optimization_barrier(held)[: len(results)]
        self.last = results[0]
        return results[0] if len(results) == 1 else results

    def send(self, x, axis, bit):
        return swap(self.behind(x), axis, bit)


def per_device(inputs, cotangent, in_proj, out_proj, decays, input_scale, retain):
    rows, depth = inputs.shape
    channels = in_proj.shape[1]
    devices, lanes = lax.axis_size("tm"), lax.axis_size("chan")
    scaling = 1.0 / math.sqrt(rows * devices)
    me, lane = lax.axis_index("tm"), lax.axis_index("chan")
    far = devices // 2
    groups = devices // 4
    steps = rows // SEG
    scale = input_scale[None, :]
    decay_row = decays[None, :]
    side = me // far

    half, quarter = rows // 2, rows // 4
    rows_out = depth // devices
    core = lane % 2
    idx = [core, lane, side, 1 - side]
    idx += [core, 1 - core, lane, lane ^ 2, lane ^ 1, lane ^ 3, 2 * core, 2 * core + 1, 2 - 2 * core, 3 - 2 * core]
    idx += [me, me ^ 1, me ^ far, me ^ far ^ 1, me]
    idx += [me ^ (2 * k) for k in range(groups)] + [(me % far) ^ (2 * k) for k in range(groups)]
    idx, inputs, cotangent = lax.optimization_barrier((jnp.stack(idx).astype(jnp.int32), inputs, cotangent))
    mine_near, mine_1, mine_2, mine_3, mine_4 = (
        [(0, 0, half)], [(1, 2, quarter)], [(1, 3, quarter)], [(2, 2, quarter)], [(2, 3, quarter)],
    )
    their_near, their_1, their_2, their_3, their_4 = (
        [(0, 1, half)], [(1, 4, quarter)], [(1, 5, quarter)], [(2, 4, quarter)], [(2, 5, quarter)],
    )

    line = Order()
    x_own, x_half, x_quarter = line.step(
        *prep(prep_inputs_kernel, idx, inputs, [((half, depth), F32), ((quarter, depth), F32)], "prep_inputs")
    )
    near_x = line.send(x_half, "tm", 1)
    away_x = line.send(x_quarter, "tm", far)
    part = ((quarter, depth // 2), F32)
    c_own, own_a, c_first_a, c_first_b, c_second, c_quarter_a, c_quarter_b = prep(
        prep_cotangent_kernel, idx, line.behind(cotangent),
        [((rows, depth // 2), BF16), part, part, ((quarter, depth), F32), part, part], "prep_cotangent",
    )
    table = resident(
        functools.partial(summary_kernel, scaling=scaling), jax.ShapeDtypeStruct((1, 4, channels), F32),
        (x_own, c_own, in_proj, out_proj, scale, decay_row, retain[None, :]), "summary",
        [pltpu.VMEM((rows, channels), F32)] * 2 + [pltpu.VMEM((rows, 128), F32)], scalars=0,
    )
    if groups == 2:
        table = jnp.concatenate([table] + [line.send(table, "tm", bit) for bit in (2, 3, 1)])
    else:
        for bit in reach(devices)[:-1]:
            table = jnp.concatenate([table, line.send(table, "tm", bit)])
    near_x, away_x, table = line.step(near_x, away_x, table)

    corner_x = line.send(away_x, "tm", 1)
    side_x = line.send(away_x, "chan", 2)
    away_a = line.send(c_quarter_a, "tm", far)
    table = jnp.concatenate([table, line.send(table, "tm", reach(devices)[-1])])
    enter_fwd, enter_bwd, retain_wide = carries(idx, table, rows)
    corner_x, side_x, away_a, enter_fwd = line.step(corner_x, side_x, away_a, enter_fwd)

    near_a1 = line.send(c_first_a, "tm", 1)
    corner_a = line.send(away_a, "tm", 1)
    corner_side_x = line.send(corner_x, "chan", 2)
    away_b = line.send(c_quarter_b, "tm", far)
    forward = (in_proj, scale, decay_row, retain_wide, enter_fwd)
    backward = (out_proj, scale, decay_row, retain_wide, enter_bwd)
    starts, lows = forward_call(idx, 0, [x_own], forward, "forward_own")
    scaled, grads = backward_call(idx, 0, [[c_own]], backward, starts, lows, scaling, "backward_own")
    keep, give = row_grad(idx, scaled[0], in_proj, lanes)
    other_x = line.send(pack([near_x, away_x, side_x, corner_x], "pack_x"), "chan", 1)
    corner_side_x, corner_a, near_a1, away_b, give, other_x = line.step(corner_side_x, corner_a, near_a1, away_b, give, other_x)

    corner_b = line.send(away_b, "tm", 1)
    corner_side_a = line.send(corner_a, "chan", 2)
    side_a = line.send(away_a, "chan", 2)
    near_2 = line.send(c_second, "tm", 1)
    last_x = line.send(corner_side_x, "chan", 1)
    side_b = line.send(away_b, "chan", 2)
    xs = [x_own] + collected(idx, [
        (near_x, mine_near), (away_x, mine_1), (side_x, mine_2), (corner_x, mine_3), (corner_side_x, mine_4),
        (other_x, their_near + their_1 + their_2 + their_3), (last_x, their_4),
    ], "collect_x")
    more, more_low = forward_call(idx, 1, xs[1:], forward, "forward_group")
    starts, lows = starts + more, lows + more_low
    corner_side_a, side_a, side_b, corner_b, near_2, lows[1] = line.step(corner_side_a, side_a, side_b, corner_b, near_2, lows[1])
    near_a2, near_b2 = near_2[:, : depth // 2], near_2[:, depth // 2 :]

    corner_side_b = line.send(corner_b, "chan", 2)
    near_b1 = line.send(c_first_b, "tm", 1)
    other_a = line.send(pack([near_a1, near_a2, away_a, side_a, corner_a, corner_side_a], "pack_a"), "chan", 1)
    ca = [own_a] + collected(idx, [
        (near_a1, [(0, 6, quarter)]), (near_a2, [(0, 7, quarter)]),
        (away_a, mine_1), (side_a, mine_2), (corner_a, mine_3), (corner_side_a, mine_4),
        (other_a, [(0, 8, quarter), (0, 9, quarter)] + their_1 + their_2 + their_3 + their_4),
    ], "collect_a")

    def shares(first, features, values, factor, name, sums=()):
        return [grad_rows(idx, first + k, features, values, rows_out, factor, name, sums) for k in range(1, groups)]

    out_given = shares(ROWS + groups, ca, lows, scaling, "out_grad")
    out_given[0], corner_side_b, near_b1 = line.step(out_given[0], corner_side_b, near_b1)

    out_got = [line.send(part, "tm", 2 * (k + 1)) for k, part in enumerate(out_given)]
    near_b1_other = line.send(near_b1, "chan", 1)
    near_b2_other = line.send(near_b2, "chan", 1)
    away_b_other = line.send(away_b, "chan", 1)
    other_b = line.send(pack([side_b, corner_b, corner_side_b], "pack_b"), "chan", 1)
    cb = collected(idx, [
        (near_b1, [(0, 6, quarter)]), (near_b2, [(0, 7, quarter)]),
        (away_b, mine_1), (side_b, mine_2), (corner_b, mine_3), (corner_side_b, mine_4),
        (near_b1_other, [(0, 8, quarter)]), (near_b2_other, [(0, 9, quarter)]), (away_b_other, their_1),
        (other_b, their_2 + their_3 + their_4),
    ], "collect_b")
    cs = [list(pair) for pair in zip(ca[1:], cb, strict=True)]
    more, more_grads = backward_call(idx, 1, cs, backward, starts[1:], lows[1:], scaling, "backward_group")
    scaled, grads = scaled + more, grads + more_grads
    in_given = shares(ROWS, xs, scaled, None, "in_grad", grads)
    in_given[0] = line.step(in_given[0])
    in_got = [line.send(part, "tm", 2 * (k + 1)) for k, part in enumerate(in_given)]
    out_got[0] = line.step(out_got[0])
    parts = keep + line.send(give, "chan", 1)
    columns = parts[0] + line.send(parts[1], "chan", 2)
    input_grad = columns.astype(BF16)
    in_got[0] = after(in_got[0], input_grad)

    out_proj_grad = sum(out_got, grad_rows(idx, ROWS + groups, [line.behind(ca[0]), *ca[1:]], lows, rows_out, scaling, "out_grad"))
    in_mine = grad_rows(idx, ROWS, [line.behind(xs[0]), *xs[1:]], scaled, rows_out, None, "in_grad", grads)
    in_proj_grad = sum((part[:rows_out] for part in in_got), in_mine[:rows_out])
    decay_grad = sum((part[rows_out] for part in in_got), in_mine[rows_out])
    if groups > 2:
        decay_grad = in_mine[rows_out]
        bit = 2
        while bit < far:
            decay_grad += swap(decay_grad, "tm", bit)
            bit *= 2
    return (in_proj_grad, out_proj_grad, decay_grad, input_grad)


def solution(mesh):
    return jax.shard_map(
        per_device,
        mesh=mesh,
        in_specs=(
            P("tm", None),
            P("tm", None),
            P(None, "chan"),
            P("chan", None),
            P("chan"),
            P("chan"),
            P("tm"),
        ),
        out_specs=(P("tm", "chan"), P("tm", "chan"), P("chan"), P("tm", "chan")),
        check_vma=False,
    )
```

```python
import functools
import math

import jax
import jax.numpy as jnp
from jax import lax
from jax.experimental import pallas as pl
from jax.experimental.pallas import tpu as pltpu
from jax.sharding import PartitionSpec as P

F32 = jnp.float32
BF16 = jnp.bfloat16
SEG = 8
CORE, LANE, SIDES, PLACES, BLOCKS, SELF, ROWS = 0, 1, 2, 4, 14, 18, 19
VMEM_LIMIT = 12 * 1024 * 1024


def swap(x, axis, bit):
    n = lax.axis_size(axis)
    return lax.ppermute(x, axis, [(k, k ^ bit) for k in range(n)])


def nn(a, b):
    return lax.dot_general(a, b, (((1,), (0,)), ((), ())), preferred_element_type=F32)


def nt(a, b):
    return lax.dot_general(a, b, (((1,), (1,)), ((), ())), preferred_element_type=F32)


def tn(a, b):
    return lax.dot_general(a, b, (((0,), (0,)), ((), ())), preferred_element_type=F32)


def order_of(rows, transpose=False):
    steps = rows // SEG
    r = lax.broadcasted_iota(jnp.int32, (rows, rows), 1 if transpose else 0)
    t = lax.broadcasted_iota(jnp.int32, (rows, rows), 0 if transpose else 1)
    return (r % SEG) * steps + r // SEG == t


def order(rows, transpose=False):
    return order_of(rows, transpose).astype(F32).astype(BF16)


VMEM = pl.BlockSpec(memory_space=pltpu.VMEM)
SMEM = pl.BlockSpec(memory_space=pltpu.SMEM)


ANY = pl.BlockSpec(memory_space=pl.ANY)


def resident(kernel, out_shape, operands, name, scratch=(), scalars=1, anywhere=0):
    return pl.pallas_call(
        kernel,
        out_shape=out_shape,
        in_specs=[SMEM] * scalars + [VMEM] * (len(operands) - scalars - anywhere) + [ANY] * anywhere,
        out_specs=jax.tree.map(lambda _: VMEM, out_shape),
        scratch_shapes=scratch,
        compiler_params=pltpu.CompilerParams(vmem_limit_bytes=VMEM_LIMIT),
        cost_estimate=pl.CostEstimate(flops=0, transcendentals=0, bytes_accessed=0),
        name=name,
    )(*operands)


def ordered_rows(x_ref, p_ref, full):
    full[...] = nn(order(x_ref.shape[0]), x_ref[...])
    p_ref[...] = full[...].astype(BF16)


def prep_inputs_kernel(idx_ref, x_ref, p_ref, half_ref, quarter_ref, full):
    ordered_rows(x_ref, p_ref, full)
    half, quarter = half_ref.shape[0], quarter_ref.shape[0]
    half_ref[...] = full[pl.ds(pl.multiple_of(idx_ref[CORE] * half, half), half), :]
    quarter_ref[...] = full[pl.ds(pl.multiple_of(idx_ref[LANE] * quarter, quarter), quarter), :]


def prep_cotangent_kernel(idx_ref, x_ref, p_ref, own_a_ref, first_a_ref, first_b_ref, second_a_ref, second_b_ref, away_a_ref, away_b_ref, full):
    ordered_rows(x_ref, p_ref, full)
    quarter, width = first_a_ref.shape
    cols = [pl.ds(pl.multiple_of(idx_ref[SIDES + k] * width, width), width) for k in range(2)]
    first = pl.ds(pl.multiple_of(idx_ref[CORE] * 2 * quarter, quarter), quarter)
    second = pl.ds(pl.multiple_of(idx_ref[CORE] * 2 * quarter + quarter, quarter), quarter)
    away = pl.ds(pl.multiple_of(idx_ref[LANE] * quarter, quarter), quarter)
    own_a_ref[...] = full[:, cols[0]].astype(BF16)
    first_a_ref[...] = full[first, cols[0]]
    first_b_ref[...] = full[first, cols[1]]
    second_a_ref[...] = full[second, cols[0]]
    second_b_ref[...] = full[second, cols[1]]
    away_a_ref[...] = full[away, cols[1]]
    away_b_ref[...] = full[away, cols[0]]


def prep(kernel, idx, x, shapes, name):
    rows, depth = x.shape
    shapes = [jax.ShapeDtypeStruct(shape, kind) for shape, kind in shapes]
    return resident(kernel, (jax.ShapeDtypeStruct((rows, depth), BF16), *shapes), (idx, x), name, [pltpu.VMEM((rows, depth), F32)])


def pack_kernel(*refs):
    *pieces, out_ref, sems = refs
    copies, at = [], 0
    for k, ref in enumerate(pieces):
        copies.append(pltpu.make_async_copy(ref, out_ref.at[pl.ds(at, ref.shape[0]), :], sems.at[k]))
        at += ref.shape[0]
    for copy in copies:
        copy.start()
    for copy in copies:
        copy.wait()


def pack(pieces, name):
    shape = jax.ShapeDtypeStruct((sum(p.shape[0] for p in pieces), pieces[0].shape[1]), F32)
    return resident(pack_kernel, shape, tuple(pieces), name, [pltpu.SemaphoreType.DMA((len(pieces),))], scalars=0, anywhere=len(pieces))


def lanes_of(l):
    return slice(128 * l, 128 * (l + 1))


def scan_ends(src, retain_ref, base, decays, reverse):
    count, steps = src.shape[1] // 128, src.shape[0] // SEG

    def lap(k, carry):
        j = steps - 1 - k if reverse else k
        rows = pl.ds(pl.multiple_of(j * SEG, SEG), SEG)
        kept = retain_ref[pl.ds(pl.multiple_of(base + j * SEG, SEG), SEG), :]
        out = []
        for l in range(count):
            end, rate = carry[l]
            factor = kept * decays[l]
            value = src[rows, lanes_of(l)]
            end = factor * (value + end) if reverse else factor * end + value
            out.append((end, factor * rate))
        return tuple(out)

    start = tuple((jnp.zeros((SEG, 128), F32), jnp.ones((SEG, 128), F32)) for _ in range(count))
    ends = lax.fori_loop(0, steps, lap, start, unroll=4)
    return jnp.concatenate([e[0] for e in ends], axis=1), jnp.concatenate([e[1] for e in ends], axis=1)


def seg_starts(end, rate, entering, reverse):
    now = entering
    starts = [None] * SEG
    for k in range(SEG):
        s = SEG - 1 - k if reverse else k
        starts[s] = now
        now = end[s : s + 1] + rate[s : s + 1] * now
    return jnp.concatenate(starts, axis=0), now


def decay_tiles(decay_ref):
    width = decay_ref.shape[1]
    full = jnp.broadcast_to(decay_ref[...], (SEG, width))
    return [full[:, lanes_of(l)] for l in range(width // 128)]


def spread_rows(row, out_ref, at):
    rows = row.shape[1]
    column = jnp.sum(jnp.where(order_of(rows), row, 0.0), axis=1, keepdims=True)
    out_ref[at : at + rows, :] = jnp.broadcast_to(column, (rows, 128))


def summary_kernel(x_ref, c_ref, w_ref, v_ref, scale_ref, decay_ref, kept_ref, out_ref, drive, scot, retain_ref, *, scaling):
    decays = decay_tiles(decay_ref)
    spread_rows(kept_ref[...], retain_ref, 0)
    drive[...] = nn(x_ref[...], w_ref[...]) * scale_ref[...]
    scot[...] = nt(c_ref[...], v_ref[...]) * scaling
    zero = jnp.zeros(decay_ref.shape, F32)
    end, rate = scan_ends(drive, retain_ref, 0, decays, False)
    _, forward = seg_starts(end, rate, zero, False)
    back, _ = scan_ends(scot, retain_ref, 0, decays, True)
    _, backward = seg_starts(back, rate, zero, True)
    total = rate[0:1]
    for s in range(1, SEG):
        total = total * rate[s : s + 1]
    rest = zero.shape[1] - kept_ref.shape[1]
    kept = jnp.concatenate([kept_ref[...], zero[:, :rest]], axis=1) if rest else kept_ref[...]
    out_ref[0] = jnp.concatenate([total, forward, backward, kept], axis=0)


def carries_kernel(idx_ref, sum_ref, fwd_ref, bwd_ref, retain_ref):
    blocks = sum_ref.shape[0]
    far = blocks // 2
    rows = retain_ref.shape[0] // 4

    def row(away):
        top = away // far
        low = (away % 2) ^ top
        middle = ((away // 2) % (far // 2)) ^ low
        return sum_ref[middle + (far // 2) * low + far * top]

    for role, away in enumerate((0, 1, far, far + 1)):
        spread_rows(row(away)[3:4, :rows], retain_ref, role * rows)
    now = jnp.zeros_like(fwd_ref[0:1, :])
    for b in range(blocks):
        fwd_ref[b : b + 1, :] = now
        ends = row(idx_ref[SELF] ^ b)
        now = ends[1:2] + ends[0:1] * now
    now = jnp.zeros_like(now)
    for b in range(blocks - 1, -1, -1):
        bwd_ref[b : b + 1, :] = now
        ends = row(idx_ref[SELF] ^ b)
        now = ends[2:3] + ends[0:1] * now


def carries(idx, table, rows):
    shape = jax.ShapeDtypeStruct((table.shape[0], table.shape[2]), F32)
    return resident(carries_kernel, (shape, shape, jax.ShapeDtypeStruct((4 * rows, 128), F32)), (idx, table), "carries")


def reach(devices):
    return [1 << k for k in range(1, devices.bit_length() - 2)] + [3, devices // 2 + 1]


def collect_kernel(idx_ref, *refs, layout):
    count = len(layout)
    outs = refs[count : count + 3]
    held, sems = refs[count + 3], refs[count + 4]
    copies, at = [], 0
    for k, ref in enumerate(refs[:count]):
        copies.append(pltpu.make_async_copy(ref, held.at[pl.ds(at, ref.shape[0]), :], sems.at[k]))
        at += ref.shape[0]
    for copy in copies:
        copy.start()
    start = 0
    for copy, parts in zip(copies, layout, strict=True):
        copy.wait()
        for role, slot, rows in parts:
            at = pl.multiple_of(idx_ref[PLACES + slot] * rows, rows)
            outs[role][pl.ds(at, rows), :] = held[start : start + rows, :].astype(BF16)
            start += rows


def collected(idx, pieces, name):
    rows = sum(part[2] for _, parts in pieces for part in parts)
    depth = pieces[0][0].shape[1]
    shape = jax.ShapeDtypeStruct((rows // 3, depth), BF16)
    kernel = functools.partial(collect_kernel, layout=[parts for _, parts in pieces])
    scratch = [pltpu.VMEM((rows, depth), F32), pltpu.SemaphoreType.DMA((len(pieces),))]
    return list(resident(kernel, (shape,) * 3, (idx, *[array for array, _ in pieces]), name, scratch, anywhere=len(pieces)))


def forward_kernel(idx_ref, *refs, roles, first):
    xs = refs[:roles]
    w_ref, scale_ref, decay_ref, retain_ref, enter_ref = refs[roles : roles + 5]
    outs = refs[roles + 5 : -2]
    drive, state = refs[-2:]
    decays = decay_tiles(decay_ref)
    count = len(decays)
    rows_all = drive.shape[0]
    steps = rows_all // SEG
    for role in range(roles):
        start_ref, low_ref = outs[2 * role : 2 * role + 2]
        block = idx_ref[BLOCKS + first + role]
        base = (first + role) * rows_all
        drive[...] = nn(xs[role][...], w_ref[...]) * scale_ref[...]
        end, rate = scan_ends(drive, retain_ref, base, decays, False)
        start, _ = seg_starts(end, rate, enter_ref[pl.ds(block, 1), :], False)
        start_ref[...] = start

        def lap(j, before, base=base):
            at = pl.multiple_of(j * SEG, SEG)
            kept = retain_ref[pl.ds(pl.multiple_of(base + j * SEG, SEG), SEG), :]
            out = []
            for l in range(count):
                now = kept * decays[l] * before[l] + drive[pl.ds(at, SEG), lanes_of(l)]
                state[pl.ds(at, SEG), lanes_of(l)] = now
                out.append(now)
            return tuple(out)

        lax.fori_loop(0, steps, lap, tuple(start[:, lanes_of(l)] for l in range(count)), unroll=4)
        low_ref[...] = state[...].astype(BF16)


def backward_kernel(idx_ref, *refs, roles, parts, scaling, first):
    cs = refs[: roles * parts]
    v_ref, scale_ref, decay_ref, retain_ref, enter_ref = refs[roles * parts : roles * parts + 5]
    entering = refs[roles * parts + 5 : roles * parts + 5 + 2 * roles]
    outs = refs[roles * parts + 5 + 2 * roles : -3]
    scot, adjoint, track = refs[-3:]
    decays = decay_tiles(decay_ref)
    count = len(decays)
    rows_all = scot.shape[0]
    steps = rows_all // SEG
    width = v_ref.shape[1] // parts
    for role in range(roles):
        scaled_ref, grad_ref = outs[2 * role : 2 * role + 2]
        block = idx_ref[BLOCKS + first + role]
        base = (first + role) * rows_all
        if parts == 1:
            scot[...] = nt(cs[role][...], v_ref[...]) * scaling
        else:
            total = None
            for k in range(parts):
                cols = pl.ds(pl.multiple_of(idx_ref[SIDES + k] * width, width), width)
                part = nt(cs[parts * role + k][...], v_ref[:, cols])
                total = part if total is None else total + part
            scot[...] = total * scaling
        end, rate = scan_ends(scot, retain_ref, base, decays, True)
        start, _ = seg_starts(end, rate, enter_ref[pl.ds(block, 1), :], True)

        start_ref, low_ref = entering[2 * role : 2 * role + 2]
        track[0:SEG, :] = start_ref[...]
        track[SEG:, :] = low_ref[...].astype(F32)

        def lap(k, carry, base=base):
            at = (steps - 1 - k) * SEG
            rows = pl.ds(pl.multiple_of(at, SEG), SEG)
            kept = retain_ref[pl.ds(pl.multiple_of(base + at, SEG), SEG), :]
            out = []
            for l in range(count):
                follow, grad = carry[l]
                here = scot[rows, lanes_of(l)] + follow
                adjoint[rows, lanes_of(l)] = here
                part = kept * here
                out.append((part * decays[l], grad + part * track[rows, lanes_of(l)]))
            return tuple(out)

        begin = tuple((start[:, lanes_of(l)], jnp.zeros((SEG, 128), F32)) for l in range(count))
        done = lax.fori_loop(0, steps, lap, begin, unroll=4)
        scaled_ref[...] = (adjoint[...] * scale_ref[...]).astype(BF16)
        grad_ref[...] = jnp.sum(jnp.concatenate([d[1] for d in done], axis=1), axis=0, keepdims=True)


def forward_call(idx, first, xs, operands, name):
    channels = operands[1].shape[1]
    rows, roles = xs[0].shape[0], len(xs)
    shapes = (jax.ShapeDtypeStruct((SEG, channels), F32), jax.ShapeDtypeStruct((rows, channels), BF16)) * roles
    out = resident(
        functools.partial(forward_kernel, roles=roles, first=first), shapes, (idx, *xs, *operands), name,
        [pltpu.VMEM((rows, channels), F32)] * 2,
    )
    return list(out[::2]), list(out[1::2])


def backward_call(idx, first, cs, operands, starts, lows, scaling, name):
    channels = operands[1].shape[1]
    rows, roles = cs[0][0].shape[0], len(cs)
    kernel = functools.partial(backward_kernel, roles=roles, parts=len(cs[0]), scaling=scaling, first=first)
    shapes = (jax.ShapeDtypeStruct((rows, channels), BF16), jax.ShapeDtypeStruct((1, channels), F32)) * roles
    out = resident(
        kernel, shapes, (idx, *[part for c in cs for part in c], *operands, *[r for pair in zip(starts, lows, strict=True) for r in pair]), name,
        [pltpu.VMEM((rows, channels), F32)] * 2 + [pltpu.VMEM((SEG + rows, channels), F32)],
    )
    return list(out[::2]), list(out[1::2])


def grad_kernel(idx_ref, *refs, count, factor, which):
    features, values, sums, out_ref = refs[:count], refs[count : 2 * count], refs[2 * count : -1], refs[-1]
    width = out_ref.shape[0] - (SEG if sums else 0)
    at = pl.ds(pl.multiple_of(idx_ref[which] * width, width), width)
    total = tn(features[0][:, at], values[0][...])
    for k in range(1, count):
        total += tn(features[k][:, at], values[k][...])
    out_ref[0:width, :] = total * factor if factor is not None else total
    if sums:
        row = (sums[0][...] + sums[1][...]) + (sums[2][...] + sums[3][...])
        out_ref[width:, :] = jnp.broadcast_to(row, (SEG, row.shape[1]))


def grad_rows(idx, which, features, values, rows_out, factor, name, sums=()):
    channels = values[0].shape[1]
    if rows_out % 128:
        total = sum(
            tn(lax.dynamic_slice_in_dim(x, idx[which] * rows_out, rows_out, axis=1), v) for x, v in zip(features, values, strict=True)
        )
        total = total * factor if factor is not None else total
        if sums:
            row = (sums[0] + sums[1]) + (sums[2] + sums[3])
            total = jnp.concatenate([total, jnp.broadcast_to(row, (SEG, channels))], axis=0)
        return total
    return resident(
        functools.partial(grad_kernel, count=len(values), factor=factor, which=which),
        jax.ShapeDtypeStruct((rows_out + (SEG if sums else 0), channels), F32),
        (idx, *features, *values, *sums), name,
    )


def row_grad_kernel(idx_ref, a_ref, w_ref, keep_ref, give_ref):
    count, rows, width = keep_ref.shape
    a = nn(order(rows, True), a_ref[...]).astype(BF16)
    for k in range(count):
        for ref, flip in ((keep_ref, 0), (give_ref, 1)):
            at = (idx_ref[LANE] ^ (2 * k) ^ flip) * width
            ref[k] = nt(a, w_ref[pl.ds(pl.multiple_of(at, width), width), :])


def row_grad(idx, scaled, in_proj, parts):
    rows, channels = scaled.shape
    shape = jax.ShapeDtypeStruct((parts // 2, rows, in_proj.shape[0] // parts), F32)
    return resident(row_grad_kernel, (shape, shape), (idx, scaled, in_proj), "row_grad")


def after(x, *others):
    return lax.optimization_barrier((x, *others))[0]


class Order:
    def __init__(self):
        self.last = None

    def behind(self, x):
        return x if self.last is None else lax.optimization_barrier((x, self.last))[0]

    def step(self, *results):
        held = results if self.last is None else (*results, self.last)
        results = lax.optimization_barrier(held)[: len(results)]
        self.last = results[0]
        return results[0] if len(results) == 1 else results

    def send(self, x, axis, bit):
        return swap(self.behind(x), axis, bit)


def per_device(inputs, cotangent, in_proj, out_proj, decays, input_scale, retain):
    rows, depth = inputs.shape
    channels = in_proj.shape[1]
    devices, lanes = lax.axis_size("tm"), lax.axis_size("chan")
    scaling = 1.0 / math.sqrt(rows * devices)
    me, lane = lax.axis_index("tm"), lax.axis_index("chan")
    far = devices // 2
    groups = devices // 4
    steps = rows // SEG
    scale = input_scale[None, :]
    decay_row = decays[None, :]
    side = me // far

    half, quarter = rows // 2, rows // 4
    rows_out = depth // devices
    core = lane % 2
    idx = [core, lane, side, 1 - side]
    idx += [core, 1 - core, lane, lane ^ 2, lane ^ 1, lane ^ 3, 2 * core, 2 * core + 1, 2 - 2 * core, 3 - 2 * core]
    idx += [me, me ^ 1, me ^ far, me ^ far ^ 1, me]
    idx += [me ^ (2 * k) for k in range(groups)] + [(me % far) ^ (2 * k) for k in range(groups)]
    idx, inputs, cotangent = lax.optimization_barrier((jnp.stack(idx).astype(jnp.int32), inputs, cotangent))
    mine_near, mine_1, mine_2, mine_3, mine_4 = (
        [(0, 0, half)], [(1, 2, quarter)], [(1, 3, quarter)], [(2, 2, quarter)], [(2, 3, quarter)],
    )
    their_near, their_1, their_2, their_3, their_4 = (
        [(0, 1, half)], [(1, 4, quarter)], [(1, 5, quarter)], [(2, 4, quarter)], [(2, 5, quarter)],
    )

    line = Order()
    x_own, x_half, x_quarter = line.step(
        *prep(prep_inputs_kernel, idx, inputs, [((half, depth), F32), ((quarter, depth), F32)], "prep_inputs")
    )
    near_x = line.send(x_half, "tm", 1)
    away_x = line.send(x_quarter, "tm", far)
    part = ((quarter, depth // 2), F32)
    c_own, own_a, c_first_a, c_first_b, c_second_a, c_second_b, c_quarter_a, c_quarter_b = prep(
        prep_cotangent_kernel, idx, line.behind(cotangent),
        [((rows, depth // 2), BF16), part, part, part, part, part, part], "prep_cotangent",
    )
    table = resident(
        functools.partial(summary_kernel, scaling=scaling), jax.ShapeDtypeStruct((1, 4, channels), F32),
        (x_own, c_own, in_proj, out_proj, scale, decay_row, retain[None, :]), "summary",
        [pltpu.VMEM((rows, channels), F32)] * 2 + [pltpu.VMEM((rows, 128), F32)], scalars=0,
    )
    if groups == 2:
        table = jnp.concatenate([table] + [line.send(table, "tm", bit) for bit in (2, 3, 1)])
    else:
        for bit in reach(devices)[:-1]:
            table = jnp.concatenate([table, line.send(table, "tm", bit)])
    near_x, away_x, table = line.step(near_x, away_x, table)

    corner_x = line.send(away_x, "tm", 1)
    side_x = line.send(away_x, "chan", 2)
    away_a = line.send(c_quarter_a, "tm", far)
    table = jnp.concatenate([table, line.send(table, "tm", reach(devices)[-1])])
    enter_fwd, enter_bwd, retain_wide = carries(idx, table, rows)
    corner_x, side_x, away_a, enter_fwd = line.step(corner_x, side_x, away_a, enter_fwd)

    near_a1 = line.send(c_first_a, "tm", 1)
    corner_a = line.send(away_a, "tm", 1)
    corner_side_x = line.send(corner_x, "chan", 2)
    away_b = line.send(c_quarter_b, "tm", far)
    forward = (in_proj, scale, decay_row, retain_wide, enter_fwd)
    backward = (out_proj, scale, decay_row, retain_wide, enter_bwd)
    starts, lows = forward_call(idx, 0, [x_own], forward, "forward_own")
    scaled, grads = backward_call(idx, 0, [[c_own]], backward, starts, lows, scaling, "backward_own")
    keep, give = row_grad(idx, scaled[0], in_proj, lanes)
    other_x = line.send(pack([near_x, away_x, side_x, corner_x], "pack_x"), "chan", 1)
    corner_side_x, corner_a, near_a1, away_b, give, other_x = line.step(corner_side_x, corner_a, near_a1, away_b, give, other_x)

    corner_b = line.send(away_b, "tm", 1)
    corner_side_a = line.send(corner_a, "chan", 2)
    side_a = line.send(away_a, "chan", 2)
    near_a2 = line.send(c_second_a, "tm", 1)
    last_x = line.send(corner_side_x, "chan", 1)
    xs = [x_own] + collected(idx, [
        (near_x, mine_near), (away_x, mine_1), (side_x, mine_2), (corner_x, mine_3), (corner_side_x, mine_4),
        (other_x, their_near + their_1 + their_2 + their_3), (last_x, their_4),
    ], "collect_x")
    more, more_low = forward_call(idx, 1, xs[1:], forward, "forward_group")
    starts, lows = starts + more, lows + more_low
    corner_side_a, side_a, corner_b, near_a2, lows[1] = line.step(corner_side_a, side_a, corner_b, near_a2, lows[1])

    side_b = line.send(away_b, "chan", 2)
    near_b1 = line.send(c_first_b, "tm", 1)
    other_a = line.send(pack([near_a1, near_a2, away_a, side_a, corner_a, corner_side_a], "pack_a"), "chan", 1)
    ca = [own_a] + collected(idx, [
        (near_a1, [(0, 6, quarter)]), (near_a2, [(0, 7, quarter)]),
        (away_a, mine_1), (side_a, mine_2), (corner_a, mine_3), (corner_side_a, mine_4),
        (other_a, [(0, 8, quarter), (0, 9, quarter)] + their_1 + their_2 + their_3 + their_4),
    ], "collect_a")

    def shares(first, features, values, factor, name, sums=()):
        return [grad_rows(idx, first + k, features, values, rows_out, factor, name, sums) for k in range(1, groups)]

    out_given = shares(ROWS + groups, ca, lows, scaling, "out_grad")
    out_given[0], side_b, near_b1 = line.step(out_given[0], side_b, near_b1)

    out_got = [line.send(part, "tm", 2 * (k + 1)) for k, part in enumerate(out_given)]
    near_b2 = line.send(c_second_b, "tm", 1)
    corner_side_b = line.send(corner_b, "chan", 2)
    near_b1_other = line.send(near_b1, "chan", 1)
    away_b_other = line.send(away_b, "chan", 1)
    near_b2, corner_side_b, near_b1_other, away_b_other = line.step(near_b2, corner_side_b, near_b1_other, away_b_other)

    near_b2_other = line.send(near_b2, "chan", 1)
    side_b_other = line.send(side_b, "chan", 1)
    corner_b_other = line.send(corner_b, "chan", 1)
    last_b = line.send(corner_side_b, "chan", 1)
    cb = collected(idx, [
        (near_b1, [(0, 6, quarter)]), (near_b2, [(0, 7, quarter)]),
        (away_b, mine_1), (side_b, mine_2), (corner_b, mine_3), (corner_side_b, mine_4),
        (near_b1_other, [(0, 8, quarter)]), (near_b2_other, [(0, 9, quarter)]),
        (away_b_other, their_1), (side_b_other, their_2), (corner_b_other, their_3), (last_b, their_4),
    ], "collect_b")
    cs = [list(pair) for pair in zip(ca[1:], cb, strict=True)]
    more, more_grads = backward_call(idx, 1, cs, backward, starts[1:], lows[1:], scaling, "backward_group")
    scaled, grads = scaled + more, grads + more_grads
    in_given = shares(ROWS, xs, scaled, None, "in_grad", grads)
    in_given[0] = line.step(in_given[0])
    in_got = [line.send(part, "tm", 2 * (k + 1)) for k, part in enumerate(in_given)]
    out_got[0] = line.step(out_got[0])
    parts = keep + line.send(give, "chan", 1)
    columns = parts[0] + line.send(parts[1], "chan", 2)
    input_grad = columns.astype(BF16)
    in_got[0] = after(in_got[0], input_grad)

    out_proj_grad = sum(out_got, grad_rows(idx, ROWS + groups, [line.behind(ca[0]), *ca[1:]], lows, rows_out, scaling, "out_grad"))
    in_mine = grad_rows(idx, ROWS, [line.behind(xs[0]), *xs[1:]], scaled, rows_out, None, "in_grad", grads)
    in_proj_grad = sum((part[:rows_out] for part in in_got), in_mine[:rows_out])
    decay_grad = sum((part[rows_out] for part in in_got), in_mine[rows_out])
    if groups > 2:
        decay_grad = in_mine[rows_out]
        bit = 2
        while bit < far:
            decay_grad += swap(decay_grad, "tm", bit)
            bit *= 2
    return (in_proj_grad, out_proj_grad, decay_grad, input_grad)


def solution(mesh):
    return jax.shard_map(
        per_device,
        mesh=mesh,
        in_specs=(
            P("tm", None),
            P("tm", None),
            P(None, "chan"),
            P("chan", None),
            P("chan"),
            P("chan"),
            P("tm"),
        ),
        out_specs=(P("tm", "chan"), P("tm", "chan"), P("chan"), P("tm", "chan")),
        check_vma=False,
    )
```

```python
import functools
import math

import jax
import jax.numpy as jnp
from jax import lax
from jax.experimental import pallas as pl
from jax.experimental.pallas import tpu as pltpu
from jax.sharding import PartitionSpec as P

F32 = jnp.float32
BF16 = jnp.bfloat16
SEG = 8
CORE, LANE, SIDES, PLACES, BLOCKS, SELF, ROWS = 0, 1, 2, 4, 14, 18, 19
VMEM_LIMIT = 12 * 1024 * 1024


def swap(x, axis, bit):
    n = lax.axis_size(axis)
    return lax.ppermute(x, axis, [(k, k ^ bit) for k in range(n)])


def nn(a, b):
    return lax.dot_general(a, b, (((1,), (0,)), ((), ())), preferred_element_type=F32)


def nt(a, b):
    return lax.dot_general(a, b, (((1,), (1,)), ((), ())), preferred_element_type=F32)


def tn(a, b):
    return lax.dot_general(a, b, (((0,), (0,)), ((), ())), preferred_element_type=F32)


def order_of(rows, transpose=False):
    steps = rows // SEG
    r = lax.broadcasted_iota(jnp.int32, (rows, rows), 1 if transpose else 0)
    t = lax.broadcasted_iota(jnp.int32, (rows, rows), 0 if transpose else 1)
    return (r % SEG) * steps + r // SEG == t


def order(rows, transpose=False):
    return order_of(rows, transpose).astype(F32).astype(BF16)


VMEM = pl.BlockSpec(memory_space=pltpu.VMEM)
SMEM = pl.BlockSpec(memory_space=pltpu.SMEM)


ANY = pl.BlockSpec(memory_space=pl.ANY)


def resident(kernel, out_shape, operands, name, scratch=(), scalars=1, anywhere=0):
    return pl.pallas_call(
        kernel,
        out_shape=out_shape,
        in_specs=[SMEM] * scalars + [VMEM] * (len(operands) - scalars - anywhere) + [ANY] * anywhere,
        out_specs=jax.tree.map(lambda _: VMEM, out_shape),
        scratch_shapes=scratch,
        compiler_params=pltpu.CompilerParams(vmem_limit_bytes=VMEM_LIMIT),
        cost_estimate=pl.CostEstimate(flops=0, transcendentals=0, bytes_accessed=0),
        name=name,
    )(*operands)


def ordered_rows(x_ref, p_ref, full):
    full[...] = nn(order(x_ref.shape[0]), x_ref[...])
    p_ref[...] = full[...].astype(BF16)


def prep_inputs_kernel(idx_ref, x_ref, p_ref, half_ref, quarter_ref, full):
    ordered_rows(x_ref, p_ref, full)
    half, quarter = half_ref.shape[0], quarter_ref.shape[0]
    half_ref[...] = full[pl.ds(pl.multiple_of(idx_ref[CORE] * half, half), half), :]
    quarter_ref[...] = full[pl.ds(pl.multiple_of(idx_ref[LANE] * quarter, quarter), quarter), :]


def prep_cotangent_kernel(idx_ref, x_ref, p_ref, own_a_ref, first_a_ref, second_a_ref, half_b_ref, away_a_ref, away_b_ref, full):
    ordered_rows(x_ref, p_ref, full)
    quarter, width = first_a_ref.shape
    cols = [pl.ds(pl.multiple_of(idx_ref[SIDES + k] * width, width), width) for k in range(2)]
    first = pl.ds(pl.multiple_of(idx_ref[CORE] * 2 * quarter, quarter), quarter)
    second = pl.ds(pl.multiple_of(idx_ref[CORE] * 2 * quarter + quarter, quarter), quarter)
    away = pl.ds(pl.multiple_of(idx_ref[LANE] * quarter, quarter), quarter)
    own_a_ref[...] = full[:, cols[0]].astype(BF16)
    first_a_ref[...] = full[first, cols[0]]
    second_a_ref[...] = full[second, cols[0]]
    half_b_ref[...] = full[pl.ds(pl.multiple_of(idx_ref[CORE] * 2 * quarter, quarter), 2 * quarter), cols[1]]
    away_a_ref[...] = full[away, cols[1]]
    away_b_ref[...] = full[away, cols[0]]


def prep(kernel, idx, x, shapes, name):
    rows, depth = x.shape
    shapes = [jax.ShapeDtypeStruct(shape, kind) for shape, kind in shapes]
    return resident(kernel, (jax.ShapeDtypeStruct((rows, depth), BF16), *shapes), (idx, x), name, [pltpu.VMEM((rows, depth), F32)])


def pack_kernel(*refs):
    *pieces, out_ref, sems = refs
    copies, at = [], 0
    for k, ref in enumerate(pieces):
        copies.append(pltpu.make_async_copy(ref, out_ref.at[pl.ds(at, ref.shape[0]), :], sems.at[k]))
        at += ref.shape[0]
    for copy in copies:
        copy.start()
    for copy in copies:
        copy.wait()


def pack(pieces, name):
    shape = jax.ShapeDtypeStruct((sum(p.shape[0] for p in pieces), pieces[0].shape[1]), F32)
    return resident(pack_kernel, shape, tuple(pieces), name, [pltpu.SemaphoreType.DMA((len(pieces),))], scalars=0, anywhere=len(pieces))


def lanes_of(l):
    return slice(128 * l, 128 * (l + 1))


def scan_ends(src, retain_ref, base, decays, reverse):
    count, steps = src.shape[1] // 128, src.shape[0] // SEG

    def lap(k, carry):
        j = steps - 1 - k if reverse else k
        rows = pl.ds(pl.multiple_of(j * SEG, SEG), SEG)
        kept = retain_ref[pl.ds(pl.multiple_of(base + j * SEG, SEG), SEG), :]
        out = []
        for l in range(count):
            end, rate = carry[l]
            factor = kept * decays[l]
            value = src[rows, lanes_of(l)]
            end = factor * (value + end) if reverse else factor * end + value
            out.append((end, factor * rate))
        return tuple(out)

    start = tuple((jnp.zeros((SEG, 128), F32), jnp.ones((SEG, 128), F32)) for _ in range(count))
    ends = lax.fori_loop(0, steps, lap, start, unroll=4)
    return jnp.concatenate([e[0] for e in ends], axis=1), jnp.concatenate([e[1] for e in ends], axis=1)


def seg_starts(end, rate, entering, reverse):
    now = entering
    starts = [None] * SEG
    for k in range(SEG):
        s = SEG - 1 - k if reverse else k
        starts[s] = now
        now = end[s : s + 1] + rate[s : s + 1] * now
    return jnp.concatenate(starts, axis=0), now


def decay_tiles(decay_ref):
    width = decay_ref.shape[1]
    full = jnp.broadcast_to(decay_ref[...], (SEG, width))
    return [full[:, lanes_of(l)] for l in range(width // 128)]


def spread_rows(row, out_ref, at):
    rows = row.shape[1]
    column = jnp.sum(jnp.where(order_of(rows), row, 0.0), axis=1, keepdims=True)
    out_ref[at : at + rows, :] = jnp.broadcast_to(column, (rows, 128))


def summary_kernel(x_ref, c_ref, w_ref, v_ref, scale_ref, decay_ref, kept_ref, out_ref, drive, scot, retain_ref, *, scaling):
    decays = decay_tiles(decay_ref)
    spread_rows(kept_ref[...], retain_ref, 0)
    drive[...] = nn(x_ref[...], w_ref[...]) * scale_ref[...]
    scot[...] = nt(c_ref[...], v_ref[...]) * scaling
    zero = jnp.zeros(decay_ref.shape, F32)
    end, rate = scan_ends(drive, retain_ref, 0, decays, False)
    _, forward = seg_starts(end, rate, zero, False)
    back, _ = scan_ends(scot, retain_ref, 0, decays, True)
    _, backward = seg_starts(back, rate, zero, True)
    total = rate[0:1]
    for s in range(1, SEG):
        total = total * rate[s : s + 1]
    rest = zero.shape[1] - kept_ref.shape[1]
    kept = jnp.concatenate([kept_ref[...], zero[:, :rest]], axis=1) if rest else kept_ref[...]
    out_ref[0] = jnp.concatenate([total, forward, backward, kept], axis=0)


def carries_kernel(idx_ref, sum_ref, fwd_ref, bwd_ref, retain_ref):
    blocks = sum_ref.shape[0]
    far = blocks // 2
    rows = retain_ref.shape[0] // 4

    def row(away):
        top = away // far
        low = (away % 2) ^ top
        middle = ((away // 2) % (far // 2)) ^ low
        return sum_ref[middle + (far // 2) * low + far * top]

    for role, away in enumerate((0, 1, far, far + 1)):
        spread_rows(row(away)[3:4, :rows], retain_ref, role * rows)
    now = jnp.zeros_like(fwd_ref[0:1, :])
    for b in range(blocks):
        fwd_ref[b : b + 1, :] = now
        ends = row(idx_ref[SELF] ^ b)
        now = ends[1:2] + ends[0:1] * now
    now = jnp.zeros_like(now)
    for b in range(blocks - 1, -1, -1):
        bwd_ref[b : b + 1, :] = now
        ends = row(idx_ref[SELF] ^ b)
        now = ends[2:3] + ends[0:1] * now


def carries(idx, table, rows):
    shape = jax.ShapeDtypeStruct((table.shape[0], table.shape[2]), F32)
    return resident(carries_kernel, (shape, shape, jax.ShapeDtypeStruct((4 * rows, 128), F32)), (idx, table), "carries")


def reach(devices):
    return [1 << k for k in range(1, devices.bit_length() - 2)] + [3, devices // 2 + 1]


def collect_kernel(idx_ref, *refs, layout):
    count = len(layout)
    outs = refs[count : count + 3]
    held, sems = refs[count + 3], refs[count + 4]
    copies, at = [], 0
    for k, ref in enumerate(refs[:count]):
        copies.append(pltpu.make_async_copy(ref, held.at[pl.ds(at, ref.shape[0]), :], sems.at[k]))
        at += ref.shape[0]
    for copy in copies:
        copy.start()
    start = 0
    for copy, parts in zip(copies, layout, strict=True):
        copy.wait()
        for role, slot, rows in parts:
            at = pl.multiple_of(idx_ref[PLACES + slot] * rows, rows)
            outs[role][pl.ds(at, rows), :] = held[start : start + rows, :].astype(BF16)
            start += rows


def collected(idx, pieces, name):
    rows = sum(part[2] for _, parts in pieces for part in parts)
    depth = pieces[0][0].shape[1]
    shape = jax.ShapeDtypeStruct((rows // 3, depth), BF16)
    kernel = functools.partial(collect_kernel, layout=[parts for _, parts in pieces])
    scratch = [pltpu.VMEM((rows, depth), F32), pltpu.SemaphoreType.DMA((len(pieces),))]
    return list(resident(kernel, (shape,) * 3, (idx, *[array for array, _ in pieces]), name, scratch, anywhere=len(pieces)))


def forward_kernel(idx_ref, *refs, roles, first):
    xs = refs[:roles]
    w_ref, scale_ref, decay_ref, retain_ref, enter_ref = refs[roles : roles + 5]
    outs = refs[roles + 5 : -2]
    drive, state = refs[-2:]
    decays = decay_tiles(decay_ref)
    count = len(decays)
    rows_all = drive.shape[0]
    steps = rows_all // SEG
    for role in range(roles):
        start_ref, low_ref = outs[2 * role : 2 * role + 2]
        block = idx_ref[BLOCKS + first + role]
        base = (first + role) * rows_all
        drive[...] = nn(xs[role][...], w_ref[...]) * scale_ref[...]
        end, rate = scan_ends(drive, retain_ref, base, decays, False)
        start, _ = seg_starts(end, rate, enter_ref[pl.ds(block, 1), :], False)
        start_ref[...] = start

        def lap(j, before, base=base):
            at = pl.multiple_of(j * SEG, SEG)
            kept = retain_ref[pl.ds(pl.multiple_of(base + j * SEG, SEG), SEG), :]
            out = []
            for l in range(count):
                now = kept * decays[l] * before[l] + drive[pl.ds(at, SEG), lanes_of(l)]
                state[pl.ds(at, SEG), lanes_of(l)] = now
                out.append(now)
            return tuple(out)

        lax.fori_loop(0, steps, lap, tuple(start[:, lanes_of(l)] for l in range(count)), unroll=4)
        low_ref[...] = state[...].astype(BF16)


def backward_kernel(idx_ref, *refs, roles, parts, scaling, first):
    cs = refs[: roles * parts]
    v_ref, scale_ref, decay_ref, retain_ref, enter_ref = refs[roles * parts : roles * parts + 5]
    entering = refs[roles * parts + 5 : roles * parts + 5 + 2 * roles]
    outs = refs[roles * parts + 5 + 2 * roles : -3]
    scot, adjoint, track = refs[-3:]
    decays = decay_tiles(decay_ref)
    count = len(decays)
    rows_all = scot.shape[0]
    steps = rows_all // SEG
    width = v_ref.shape[1] // parts
    for role in range(roles):
        scaled_ref, grad_ref = outs[2 * role : 2 * role + 2]
        block = idx_ref[BLOCKS + first + role]
        base = (first + role) * rows_all
        if parts == 1:
            scot[...] = nt(cs[role][...], v_ref[...]) * scaling
        else:
            total = None
            for k in range(parts):
                cols = pl.ds(pl.multiple_of(idx_ref[SIDES + k] * width, width), width)
                part = nt(cs[parts * role + k][...], v_ref[:, cols])
                total = part if total is None else total + part
            scot[...] = total * scaling
        end, rate = scan_ends(scot, retain_ref, base, decays, True)
        start, _ = seg_starts(end, rate, enter_ref[pl.ds(block, 1), :], True)

        start_ref, low_ref = entering[2 * role : 2 * role + 2]
        track[0:SEG, :] = start_ref[...]
        track[SEG:, :] = low_ref[...].astype(F32)

        def lap(k, carry, base=base):
            at = (steps - 1 - k) * SEG
            rows = pl.ds(pl.multiple_of(at, SEG), SEG)
            kept = retain_ref[pl.ds(pl.multiple_of(base + at, SEG), SEG), :]
            out = []
            for l in range(count):
                follow, grad = carry[l]
                here = scot[rows, lanes_of(l)] + follow
                adjoint[rows, lanes_of(l)] = here
                part = kept * here
                out.append((part * decays[l], grad + part * track[rows, lanes_of(l)]))
            return tuple(out)

        begin = tuple((start[:, lanes_of(l)], jnp.zeros((SEG, 128), F32)) for l in range(count))
        done = lax.fori_loop(0, steps, lap, begin, unroll=4)
        scaled_ref[...] = (adjoint[...] * scale_ref[...]).astype(BF16)
        grad_ref[...] = jnp.sum(jnp.concatenate([d[1] for d in done], axis=1), axis=0, keepdims=True)


def forward_call(idx, first, xs, operands, name):
    channels = operands[1].shape[1]
    rows, roles = xs[0].shape[0], len(xs)
    shapes = (jax.ShapeDtypeStruct((SEG, channels), F32), jax.ShapeDtypeStruct((rows, channels), BF16)) * roles
    out = resident(
        functools.partial(forward_kernel, roles=roles, first=first), shapes, (idx, *xs, *operands), name,
        [pltpu.VMEM((rows, channels), F32)] * 2,
    )
    return list(out[::2]), list(out[1::2])


def backward_call(idx, first, cs, operands, starts, lows, scaling, name):
    channels = operands[1].shape[1]
    rows, roles = cs[0][0].shape[0], len(cs)
    kernel = functools.partial(backward_kernel, roles=roles, parts=len(cs[0]), scaling=scaling, first=first)
    shapes = (jax.ShapeDtypeStruct((rows, channels), BF16), jax.ShapeDtypeStruct((1, channels), F32)) * roles
    out = resident(
        kernel, shapes, (idx, *[part for c in cs for part in c], *operands, *[r for pair in zip(starts, lows, strict=True) for r in pair]), name,
        [pltpu.VMEM((rows, channels), F32)] * 2 + [pltpu.VMEM((SEG + rows, channels), F32)],
    )
    return list(out[::2]), list(out[1::2])


def grad_kernel(idx_ref, *refs, count, factor, which):
    features, values, sums, out_ref = refs[:count], refs[count : 2 * count], refs[2 * count : -1], refs[-1]
    width = out_ref.shape[0] - (SEG if sums else 0)
    at = pl.ds(pl.multiple_of(idx_ref[which] * width, width), width)
    total = tn(features[0][:, at], values[0][...])
    for k in range(1, count):
        total += tn(features[k][:, at], values[k][...])
    out_ref[0:width, :] = total * factor if factor is not None else total
    if sums:
        row = (sums[0][...] + sums[1][...]) + (sums[2][...] + sums[3][...])
        out_ref[width:, :] = jnp.broadcast_to(row, (SEG, row.shape[1]))


def grad_rows(idx, which, features, values, rows_out, factor, name, sums=()):
    channels = values[0].shape[1]
    if rows_out % 128:
        total = sum(
            tn(lax.dynamic_slice_in_dim(x, idx[which] * rows_out, rows_out, axis=1), v) for x, v in zip(features, values, strict=True)
        )
        total = total * factor if factor is not None else total
        if sums:
            row = (sums[0] + sums[1]) + (sums[2] + sums[3])
            total = jnp.concatenate([total, jnp.broadcast_to(row, (SEG, channels))], axis=0)
        return total
    return resident(
        functools.partial(grad_kernel, count=len(values), factor=factor, which=which),
        jax.ShapeDtypeStruct((rows_out + (SEG if sums else 0), channels), F32),
        (idx, *features, *values, *sums), name,
    )


def row_grad_kernel(idx_ref, a_ref, w_ref, keep_ref, give_ref):
    count, rows, width = keep_ref.shape
    a = nn(order(rows, True), a_ref[...]).astype(BF16)
    for k in range(count):
        for ref, flip in ((keep_ref, 0), (give_ref, 1)):
            at = (idx_ref[LANE] ^ (2 * k) ^ flip) * width
            ref[k] = nt(a, w_ref[pl.ds(pl.multiple_of(at, width), width), :])


def row_grad(idx, scaled, in_proj, parts):
    rows, channels = scaled.shape
    shape = jax.ShapeDtypeStruct((parts // 2, rows, in_proj.shape[0] // parts), F32)
    return resident(row_grad_kernel, (shape, shape), (idx, scaled, in_proj), "row_grad")


def after(x, *others):
    return lax.optimization_barrier((x, *others))[0]


class Order:
    def __init__(self):
        self.last = None

    def behind(self, x):
        return x if self.last is None else lax.optimization_barrier((x, self.last))[0]

    def step(self, *results):
        held = results if self.last is None else (*results, self.last)
        results = lax.optimization_barrier(held)[: len(results)]
        self.last = results[0]
        return results[0] if len(results) == 1 else results

    def send(self, x, axis, bit):
        return swap(self.behind(x), axis, bit)


def per_device(inputs, cotangent, in_proj, out_proj, decays, input_scale, retain):
    rows, depth = inputs.shape
    channels = in_proj.shape[1]
    devices, lanes = lax.axis_size("tm"), lax.axis_size("chan")
    scaling = 1.0 / math.sqrt(rows * devices)
    me, lane = lax.axis_index("tm"), lax.axis_index("chan")
    far = devices // 2
    groups = devices // 4
    steps = rows // SEG
    scale = input_scale[None, :]
    decay_row = decays[None, :]
    side = me // far

    half, quarter = rows // 2, rows // 4
    rows_out = depth // devices
    core = lane % 2
    idx = [core, lane, side, 1 - side]
    idx += [core, 1 - core, lane, lane ^ 2, lane ^ 1, lane ^ 3, 2 * core, 2 * core + 1, 2 - 2 * core, 3 - 2 * core]
    idx += [me, me ^ 1, me ^ far, me ^ far ^ 1, me]
    idx += [me ^ (2 * k) for k in range(groups)] + [(me % far) ^ (2 * k) for k in range(groups)]
    idx, inputs, cotangent = lax.optimization_barrier((jnp.stack(idx).astype(jnp.int32), inputs, cotangent))
    mine_near, mine_1, mine_2, mine_3, mine_4 = (
        [(0, 0, half)], [(1, 2, quarter)], [(1, 3, quarter)], [(2, 2, quarter)], [(2, 3, quarter)],
    )
    their_near, their_1, their_2, their_3, their_4 = (
        [(0, 1, half)], [(1, 4, quarter)], [(1, 5, quarter)], [(2, 4, quarter)], [(2, 5, quarter)],
    )

    line = Order()
    x_own, x_half, x_quarter = line.step(
        *prep(prep_inputs_kernel, idx, inputs, [((half, depth), F32), ((quarter, depth), F32)], "prep_inputs")
    )
    near_x = line.send(x_half, "tm", 1)
    away_x = line.send(x_quarter, "tm", far)
    part = ((quarter, depth // 2), F32)
    c_own, own_a, c_first_a, c_second_a, c_half_b, c_quarter_a, c_quarter_b = prep(
        prep_cotangent_kernel, idx, line.behind(cotangent),
        [((rows, depth // 2), BF16), part, part, ((half, depth // 2), F32), part, part], "prep_cotangent",
    )
    table = resident(
        functools.partial(summary_kernel, scaling=scaling), jax.ShapeDtypeStruct((1, 4, channels), F32),
        (x_own, c_own, in_proj, out_proj, scale, decay_row, retain[None, :]), "summary",
        [pltpu.VMEM((rows, channels), F32)] * 2 + [pltpu.VMEM((rows, 128), F32)], scalars=0,
    )
    if groups == 2:
        table = jnp.concatenate([table] + [line.send(table, "tm", bit) for bit in (2, 3, 1)])
    else:
        for bit in reach(devices)[:-1]:
            table = jnp.concatenate([table, line.send(table, "tm", bit)])
    near_x, away_x, table = line.step(near_x, away_x, table)

    corner_x = line.send(away_x, "tm", 1)
    side_x = line.send(away_x, "chan", 2)
    away_a = line.send(c_quarter_a, "tm", far)
    table = jnp.concatenate([table, line.send(table, "tm", reach(devices)[-1])])
    enter_fwd, enter_bwd, retain_wide = carries(idx, table, rows)
    corner_x, side_x, away_a, enter_fwd = line.step(corner_x, side_x, away_a, enter_fwd)

    near_a1 = line.send(c_first_a, "tm", 1)
    corner_a = line.send(away_a, "tm", 1)
    corner_side_x = line.send(corner_x, "chan", 2)
    away_b = line.send(c_quarter_b, "tm", far)
    forward = (in_proj, scale, decay_row, retain_wide, enter_fwd)
    backward = (out_proj, scale, decay_row, retain_wide, enter_bwd)
    starts, lows = forward_call(idx, 0, [x_own], forward, "forward_own")
    scaled, grads = backward_call(idx, 0, [[c_own]], backward, starts, lows, scaling, "backward_own")
    keep, give = row_grad(idx, scaled[0], in_proj, lanes)
    other_x = line.send(pack([near_x, away_x, side_x, corner_x], "pack_x"), "chan", 1)
    corner_side_x, corner_a, near_a1, away_b, give, other_x = line.step(corner_side_x, corner_a, near_a1, away_b, give, other_x)

    corner_b = line.send(away_b, "tm", 1)
    corner_side_a = line.send(corner_a, "chan", 2)
    side_a = line.send(away_a, "chan", 2)
    near_a2 = line.send(c_second_a, "tm", 1)
    last_x = line.send(corner_side_x, "chan", 1)
    xs = [x_own] + collected(idx, [
        (near_x, mine_near), (away_x, mine_1), (side_x, mine_2), (corner_x, mine_3), (corner_side_x, mine_4),
        (other_x, their_near + their_1 + their_2 + their_3), (last_x, their_4),
    ], "collect_x")
    more, more_low = forward_call(idx, 1, xs[1:], forward, "forward_group")
    starts, lows = starts + more, lows + more_low
    corner_side_a, side_a, corner_b, near_a2, lows[1] = line.step(corner_side_a, side_a, corner_b, near_a2, lows[1])

    far_b = pack([line.behind(away_b), corner_b], "pack_b")
    side_b = line.send(far_b, "chan", 2)
    near_b = line.send(c_half_b, "tm", 1)
    other_a = line.send(pack([near_a1, near_a2, away_a, side_a, corner_a, corner_side_a], "pack_a"), "chan", 1)
    ca = [own_a] + collected(idx, [
        (near_a1, [(0, 6, quarter)]), (near_a2, [(0, 7, quarter)]),
        (away_a, mine_1), (side_a, mine_2), (corner_a, mine_3), (corner_side_a, mine_4),
        (other_a, [(0, 8, quarter), (0, 9, quarter)] + their_1 + their_2 + their_3 + their_4),
    ], "collect_a")

    def shares(first, features, values, factor, name, sums=()):
        return [grad_rows(idx, first + k, features, values, rows_out, factor, name, sums) for k in range(1, groups)]

    out_given = shares(ROWS + groups, ca, lows, scaling, "out_grad")
    out_given[0] = line.step(out_given[0])

    out_got = [line.send(part, "tm", 2 * (k + 1)) for k, part in enumerate(out_given)]
    near_b, side_b = line.step(near_b, side_b)

    near_b_other = line.send(near_b, "chan", 1)
    far_b_other = line.send(far_b, "chan", 1)
    side_b_other = line.send(side_b, "chan", 1)
    cb = collected(idx, [
        (near_b, mine_near), (far_b, mine_1 + mine_3), (side_b, mine_2 + mine_4),
        (near_b_other, their_near), (far_b_other, their_1 + their_3), (side_b_other, their_2 + their_4),
    ], "collect_b")
    cs = [list(pair) for pair in zip(ca[1:], cb, strict=True)]
    more, more_grads = backward_call(idx, 1, cs, backward, starts[1:], lows[1:], scaling, "backward_group")
    scaled, grads = scaled + more, grads + more_grads
    in_given = shares(ROWS, xs, scaled, None, "in_grad", grads)
    in_given[0] = line.step(in_given[0])
    in_got = [line.send(part, "tm", 2 * (k + 1)) for k, part in enumerate(in_given)]
    out_got[0] = line.step(out_got[0])
    parts = keep + line.send(give, "chan", 1)
    columns = parts[0] + line.send(parts[1], "chan", 2)
    input_grad = columns.astype(BF16)
    in_got[0] = after(in_got[0], input_grad)

    out_proj_grad = sum(out_got, grad_rows(idx, ROWS + groups, [line.behind(ca[0]), *ca[1:]], lows, rows_out, scaling, "out_grad"))
    in_mine = grad_rows(idx, ROWS, [line.behind(xs[0]), *xs[1:]], scaled, rows_out, None, "in_grad", grads)
    in_proj_grad = sum((part[:rows_out] for part in in_got), in_mine[:rows_out])
    decay_grad = sum((part[rows_out] for part in in_got), in_mine[rows_out])
    if groups > 2:
        decay_grad = in_mine[rows_out]
        bit = 2
        while bit < far:
            decay_grad += swap(decay_grad, "tm", bit)
            bit *= 2
    return (in_proj_grad, out_proj_grad, decay_grad, input_grad)


def solution(mesh):
    return jax.shard_map(
        per_device,
        mesh=mesh,
        in_specs=(
            P("tm", None),
            P("tm", None),
            P(None, "chan"),
            P("chan", None),
            P("chan"),
            P("chan"),
            P("tm"),
        ),
        out_specs=(P("tm", "chan"), P("tm", "chan"), P("chan"), P("tm", "chan")),
        check_vma=False,
    )
```

```python
import functools
import math

import jax
import jax.numpy as jnp
from jax import lax
from jax.experimental import pallas as pl
from jax.experimental.pallas import tpu as pltpu
from jax.sharding import PartitionSpec as P

F32 = jnp.float32
BF16 = jnp.bfloat16
SEG = 8
CORE, LANE, SIDES, PLACES, BLOCKS, SELF, ROWS = 0, 1, 2, 4, 14, 18, 19
VMEM_LIMIT = 12 * 1024 * 1024


def swap(x, axis, bit):
    n = lax.axis_size(axis)
    return lax.ppermute(x, axis, [(k, k ^ bit) for k in range(n)])


def nn(a, b):
    return lax.dot_general(a, b, (((1,), (0,)), ((), ())), preferred_element_type=F32)


def nt(a, b):
    return lax.dot_general(a, b, (((1,), (1,)), ((), ())), preferred_element_type=F32)


def tn(a, b):
    return lax.dot_general(a, b, (((0,), (0,)), ((), ())), preferred_element_type=F32)


def order_of(rows, transpose=False):
    steps = rows // SEG
    r = lax.broadcasted_iota(jnp.int32, (rows, rows), 1 if transpose else 0)
    t = lax.broadcasted_iota(jnp.int32, (rows, rows), 0 if transpose else 1)
    return (r % SEG) * steps + r // SEG == t


def order(rows, transpose=False):
    return order_of(rows, transpose).astype(F32).astype(BF16)


VMEM = pl.BlockSpec(memory_space=pltpu.VMEM)
SMEM = pl.BlockSpec(memory_space=pltpu.SMEM)


ANY = pl.BlockSpec(memory_space=pl.ANY)


def resident(kernel, out_shape, operands, name, scratch=(), scalars=1, anywhere=0):
    return pl.pallas_call(
        kernel,
        out_shape=out_shape,
        in_specs=[SMEM] * scalars + [VMEM] * (len(operands) - scalars - anywhere) + [ANY] * anywhere,
        out_specs=jax.tree.map(lambda _: VMEM, out_shape),
        scratch_shapes=scratch,
        compiler_params=pltpu.CompilerParams(vmem_limit_bytes=VMEM_LIMIT),
        cost_estimate=pl.CostEstimate(flops=0, transcendentals=0, bytes_accessed=0),
        name=name,
    )(*operands)


def ordered_rows(x_ref, p_ref, full):
    full[...] = nn(order(x_ref.shape[0]), x_ref[...])
    p_ref[...] = full[...].astype(BF16)


def prep_inputs_kernel(idx_ref, x_ref, p_ref, half_ref, quarter_ref, full):
    ordered_rows(x_ref, p_ref, full)
    half, quarter = half_ref.shape[0], quarter_ref.shape[0]
    half_ref[...] = full[pl.ds(pl.multiple_of(idx_ref[CORE] * half, half), half), :]
    quarter_ref[...] = full[pl.ds(pl.multiple_of(idx_ref[LANE] * quarter, quarter), quarter), :]


def prep_cotangent_kernel(idx_ref, x_ref, p_ref, own_a_ref, first_a_ref, second_a_ref, half_b_ref, away_a_ref, away_b_ref, full):
    ordered_rows(x_ref, p_ref, full)
    quarter, width = first_a_ref.shape
    cols = [pl.ds(pl.multiple_of(idx_ref[SIDES + k] * width, width), width) for k in range(2)]
    first = pl.ds(pl.multiple_of(idx_ref[CORE] * 2 * quarter, quarter), quarter)
    second = pl.ds(pl.multiple_of(idx_ref[CORE] * 2 * quarter + quarter, quarter), quarter)
    away = pl.ds(pl.multiple_of(idx_ref[LANE] * quarter, quarter), quarter)
    own_a_ref[...] = full[:, cols[0]].astype(BF16)
    first_a_ref[...] = full[first, cols[0]]
    second_a_ref[...] = full[second, cols[0]]
    half_b_ref[...] = full[pl.ds(pl.multiple_of(idx_ref[CORE] * 2 * quarter, quarter), 2 * quarter), cols[1]]
    away_a_ref[...] = full[away, cols[1]]
    away_b_ref[...] = full[away, cols[0]]


def prep(kernel, idx, x, shapes, name):
    rows, depth = x.shape
    shapes = [jax.ShapeDtypeStruct(shape, kind) for shape, kind in shapes]
    return resident(kernel, (jax.ShapeDtypeStruct((rows, depth), BF16), *shapes), (idx, x), name, [pltpu.VMEM((rows, depth), F32)])


def pack_kernel(*refs, spans):
    *pieces, out_ref, sems = refs
    copies, at = [], 0
    for k, (ref, (start, rows)) in enumerate(zip(pieces, spans, strict=True)):
        copies.append(pltpu.make_async_copy(ref.at[pl.ds(start, rows), :], out_ref.at[pl.ds(at, rows), :], sems.at[k]))
        at += rows
    for copy in copies:
        copy.start()
    for copy in copies:
        copy.wait()


def pack(pieces, name):
    pieces = [p if isinstance(p, tuple) else (p, 0, p.shape[0]) for p in pieces]
    shape = jax.ShapeDtypeStruct((sum(p[2] for p in pieces), pieces[0][0].shape[1]), F32)
    kernel = functools.partial(pack_kernel, spans=[p[1:] for p in pieces])
    arrays = tuple(p[0] for p in pieces)
    return resident(kernel, shape, arrays, name, [pltpu.SemaphoreType.DMA((len(pieces),))], scalars=0, anywhere=len(pieces))


def lanes_of(l):
    return slice(128 * l, 128 * (l + 1))


def scan_ends(src, retain_ref, base, decays, reverse):
    count, steps = src.shape[1] // 128, src.shape[0] // SEG

    def lap(k, carry):
        j = steps - 1 - k if reverse else k
        rows = pl.ds(pl.multiple_of(j * SEG, SEG), SEG)
        kept = retain_ref[pl.ds(pl.multiple_of(base + j * SEG, SEG), SEG), :]
        out = []
        for l in range(count):
            end, rate = carry[l]
            factor = kept * decays[l]
            value = src[rows, lanes_of(l)]
            end = factor * (value + end) if reverse else factor * end + value
            out.append((end, factor * rate))
        return tuple(out)

    start = tuple((jnp.zeros((SEG, 128), F32), jnp.ones((SEG, 128), F32)) for _ in range(count))
    ends = lax.fori_loop(0, steps, lap, start, unroll=4)
    return jnp.concatenate([e[0] for e in ends], axis=1), jnp.concatenate([e[1] for e in ends], axis=1)


def seg_starts(end, rate, entering, reverse):
    now = entering
    starts = [None] * SEG
    for k in range(SEG):
        s = SEG - 1 - k if reverse else k
        starts[s] = now
        now = end[s : s + 1] + rate[s : s + 1] * now
    return jnp.concatenate(starts, axis=0), now


def decay_tiles(decay_ref):
    width = decay_ref.shape[1]
    full = jnp.broadcast_to(decay_ref[...], (SEG, width))
    return [full[:, lanes_of(l)] for l in range(width // 128)]


def spread_rows(row, out_ref, at):
    rows = row.shape[1]
    column = jnp.sum(jnp.where(order_of(rows), row, 0.0), axis=1, keepdims=True)
    out_ref[at : at + rows, :] = jnp.broadcast_to(column, (rows, 128))


def summary_kernel(x_ref, c_ref, w_ref, v_ref, scale_ref, decay_ref, kept_ref, out_ref, drive, scot, retain_ref, *, scaling):
    decays = decay_tiles(decay_ref)
    spread_rows(kept_ref[...], retain_ref, 0)
    drive[...] = nn(x_ref[...], w_ref[...]) * scale_ref[...]
    scot[...] = nt(c_ref[...], v_ref[...]) * scaling
    zero = jnp.zeros(decay_ref.shape, F32)
    end, rate = scan_ends(drive, retain_ref, 0, decays, False)
    _, forward = seg_starts(end, rate, zero, False)
    back, _ = scan_ends(scot, retain_ref, 0, decays, True)
    _, backward = seg_starts(back, rate, zero, True)
    total = rate[0:1]
    for s in range(1, SEG):
        total = total * rate[s : s + 1]
    rest = zero.shape[1] - kept_ref.shape[1]
    kept = jnp.concatenate([kept_ref[...], zero[:, :rest]], axis=1) if rest else kept_ref[...]
    out_ref[0] = jnp.concatenate([total, forward, backward, kept], axis=0)


def carries_kernel(idx_ref, sum_ref, fwd_ref, bwd_ref, retain_ref):
    blocks = sum_ref.shape[0]
    far = blocks // 2
    rows = retain_ref.shape[0] // 4

    def row(away):
        return sum_ref[(away % 2) * far + away // 2]

    for role, away in enumerate((0, 1, far, far + 1)):
        spread_rows(row(away)[3:4, :rows], retain_ref, role * rows)
    now = jnp.zeros_like(fwd_ref[0:1, :])
    for b in range(blocks):
        fwd_ref[b : b + 1, :] = now
        ends = row(idx_ref[SELF] ^ b)
        now = ends[1:2] + ends[0:1] * now
    now = jnp.zeros_like(now)
    for b in range(blocks - 1, -1, -1):
        bwd_ref[b : b + 1, :] = now
        ends = row(idx_ref[SELF] ^ b)
        now = ends[2:3] + ends[0:1] * now


def carries(idx, table, rows):
    shape = jax.ShapeDtypeStruct((table.shape[0], table.shape[2]), F32)
    return resident(carries_kernel, (shape, shape, jax.ShapeDtypeStruct((4 * rows, 128), F32)), (idx, table), "carries")


def reach(devices):
    return [1 << k for k in range(1, devices.bit_length() - 1)] + [1]


def collect_kernel(idx_ref, *refs, layout):
    count = len(layout)
    outs = refs[count : count + 3]
    held, sems = refs[count + 3], refs[count + 4]
    copies, at = [], 0
    for k, ref in enumerate(refs[:count]):
        copies.append(pltpu.make_async_copy(ref, held.at[pl.ds(at, ref.shape[0]), :], sems.at[k]))
        at += ref.shape[0]
    for copy in copies:
        copy.start()
    start = 0
    for copy, parts in zip(copies, layout, strict=True):
        copy.wait()
        for role, slot, rows in parts:
            at = pl.multiple_of(idx_ref[PLACES + slot] * rows, rows)
            outs[role][pl.ds(at, rows), :] = held[start : start + rows, :].astype(BF16)
            start += rows


def collected(idx, pieces, name):
    rows = sum(part[2] for _, parts in pieces for part in parts)
    depth = pieces[0][0].shape[1]
    shape = jax.ShapeDtypeStruct((rows // 3, depth), BF16)
    kernel = functools.partial(collect_kernel, layout=[parts for _, parts in pieces])
    scratch = [pltpu.VMEM((rows, depth), F32), pltpu.SemaphoreType.DMA((len(pieces),))]
    return list(resident(kernel, (shape,) * 3, (idx, *[array for array, _ in pieces]), name, scratch, anywhere=len(pieces)))


def forward_kernel(idx_ref, *refs, roles, first):
    xs = refs[:roles]
    w_ref, scale_ref, decay_ref, retain_ref, enter_ref = refs[roles : roles + 5]
    outs = refs[roles + 5 : -2]
    drive, state = refs[-2:]
    decays = decay_tiles(decay_ref)
    count = len(decays)
    rows_all = drive.shape[0]
    steps = rows_all // SEG
    for role in range(roles):
        start_ref, low_ref = outs[2 * role : 2 * role + 2]
        block = idx_ref[BLOCKS + first + role]
        base = (first + role) * rows_all
        drive[...] = nn(xs[role][...], w_ref[...]) * scale_ref[...]
        end, rate = scan_ends(drive, retain_ref, base, decays, False)
        start, _ = seg_starts(end, rate, enter_ref[pl.ds(block, 1), :], False)
        start_ref[...] = start

        def lap(j, before, base=base):
            at = pl.multiple_of(j * SEG, SEG)
            kept = retain_ref[pl.ds(pl.multiple_of(base + j * SEG, SEG), SEG), :]
            out = []
            for l in range(count):
                now = kept * decays[l] * before[l] + drive[pl.ds(at, SEG), lanes_of(l)]
                state[pl.ds(at, SEG), lanes_of(l)] = now
                out.append(now)
            return tuple(out)

        lax.fori_loop(0, steps, lap, tuple(start[:, lanes_of(l)] for l in range(count)), unroll=4)
        low_ref[...] = state[...].astype(BF16)


def backward_kernel(idx_ref, *refs, roles, parts, scaling, first):
    cs = refs[: roles * parts]
    v_ref, scale_ref, decay_ref, retain_ref, enter_ref = refs[roles * parts : roles * parts + 5]
    entering = refs[roles * parts + 5 : roles * parts + 5 + 2 * roles]
    outs = refs[roles * parts + 5 + 2 * roles : -3]
    scot, adjoint, track = refs[-3:]
    decays = decay_tiles(decay_ref)
    count = len(decays)
    rows_all = scot.shape[0]
    steps = rows_all // SEG
    width = v_ref.shape[1] // parts
    for role in range(roles):
        scaled_ref, grad_ref = outs[2 * role : 2 * role + 2]
        block = idx_ref[BLOCKS + first + role]
        base = (first + role) * rows_all
        if parts == 1:
            scot[...] = nt(cs[role][...], v_ref[...]) * scaling
        else:
            total = None
            for k in range(parts):
                cols = pl.ds(pl.multiple_of(idx_ref[SIDES + k] * width, width), width)
                part = nt(cs[parts * role + k][...], v_ref[:, cols])
                total = part if total is None else total + part
            scot[...] = total * scaling
        end, rate = scan_ends(scot, retain_ref, base, decays, True)
        start, _ = seg_starts(end, rate, enter_ref[pl.ds(block, 1), :], True)

        start_ref, low_ref = entering[2 * role : 2 * role + 2]
        track[0:SEG, :] = start_ref[...]
        track[SEG:, :] = low_ref[...].astype(F32)

        def lap(k, carry, base=base):
            at = (steps - 1 - k) * SEG
            rows = pl.ds(pl.multiple_of(at, SEG), SEG)
            kept = retain_ref[pl.ds(pl.multiple_of(base + at, SEG), SEG), :]
            out = []
            for l in range(count):
                follow, grad = carry[l]
                here = scot[rows, lanes_of(l)] + follow
                adjoint[rows, lanes_of(l)] = here
                part = kept * here
                out.append((part * decays[l], grad + part * track[rows, lanes_of(l)]))
            return tuple(out)

        begin = tuple((start[:, lanes_of(l)], jnp.zeros((SEG, 128), F32)) for l in range(count))
        done = lax.fori_loop(0, steps, lap, begin, unroll=4)
        scaled_ref[...] = (adjoint[...] * scale_ref[...]).astype(BF16)
        grad_ref[...] = jnp.sum(jnp.concatenate([d[1] for d in done], axis=1), axis=0, keepdims=True)


def forward_call(idx, first, xs, operands, name):
    channels = operands[1].shape[1]
    rows, roles = xs[0].shape[0], len(xs)
    shapes = (jax.ShapeDtypeStruct((SEG, channels), F32), jax.ShapeDtypeStruct((rows, channels), BF16)) * roles
    out = resident(
        functools.partial(forward_kernel, roles=roles, first=first), shapes, (idx, *xs, *operands), name,
        [pltpu.VMEM((rows, channels), F32)] * 2,
    )
    return list(out[::2]), list(out[1::2])


def backward_call(idx, first, cs, operands, starts, lows, scaling, name):
    channels = operands[1].shape[1]
    rows, roles = cs[0][0].shape[0], len(cs)
    kernel = functools.partial(backward_kernel, roles=roles, parts=len(cs[0]), scaling=scaling, first=first)
    shapes = (jax.ShapeDtypeStruct((rows, channels), BF16), jax.ShapeDtypeStruct((1, channels), F32)) * roles
    out = resident(
        kernel, shapes, (idx, *[part for c in cs for part in c], *operands, *[r for pair in zip(starts, lows, strict=True) for r in pair]), name,
        [pltpu.VMEM((rows, channels), F32)] * 2 + [pltpu.VMEM((SEG + rows, channels), F32)],
    )
    return list(out[::2]), list(out[1::2])


def grad_kernel(idx_ref, *refs, count, factor, which):
    features, values, sums, out_ref = refs[:count], refs[count : 2 * count], refs[2 * count : -1], refs[-1]
    width = out_ref.shape[0] - (SEG if sums else 0)
    at = pl.ds(pl.multiple_of(idx_ref[which] * width, width), width)
    total = tn(features[0][:, at], values[0][...])
    for k in range(1, count):
        total += tn(features[k][:, at], values[k][...])
    out_ref[0:width, :] = total * factor if factor is not None else total
    if sums:
        row = (sums[0][...] + sums[1][...]) + (sums[2][...] + sums[3][...])
        out_ref[width:, :] = jnp.broadcast_to(row, (SEG, row.shape[1]))


def grad_rows(idx, which, features, values, rows_out, factor, name, sums=()):
    channels = values[0].shape[1]
    if rows_out % 128:
        total = sum(
            tn(lax.dynamic_slice_in_dim(x, idx[which] * rows_out, rows_out, axis=1), v) for x, v in zip(features, values, strict=True)
        )
        total = total * factor if factor is not None else total
        if sums:
            row = (sums[0] + sums[1]) + (sums[2] + sums[3])
            total = jnp.concatenate([total, jnp.broadcast_to(row, (SEG, channels))], axis=0)
        return total
    return resident(
        functools.partial(grad_kernel, count=len(values), factor=factor, which=which),
        jax.ShapeDtypeStruct((rows_out + (SEG if sums else 0), channels), F32),
        (idx, *features, *values, *sums), name,
    )


def row_grad_kernel(idx_ref, a_ref, w_ref, keep_ref, give_ref):
    count, rows, width = keep_ref.shape
    a = nn(order(rows, True), a_ref[...]).astype(BF16)
    for k in range(count):
        for ref, flip in ((keep_ref, 0), (give_ref, 1)):
            at = (idx_ref[LANE] ^ (2 * k) ^ flip) * width
            ref[k] = nt(a, w_ref[pl.ds(pl.multiple_of(at, width), width), :])


def row_grad(idx, scaled, in_proj, parts):
    rows, channels = scaled.shape
    shape = jax.ShapeDtypeStruct((parts // 2, rows, in_proj.shape[0] // parts), F32)
    return resident(row_grad_kernel, (shape, shape), (idx, scaled, in_proj), "row_grad")


def after(x, *others):
    return lax.optimization_barrier((x, *others))[0]


class Order:
    def __init__(self):
        self.last = None

    def behind(self, x):
        return x if self.last is None else lax.optimization_barrier((x, self.last))[0]

    def step(self, *results):
        held = results if self.last is None else (*results, self.last)
        results = lax.optimization_barrier(held)[: len(results)]
        self.last = results[0]
        return results[0] if len(results) == 1 else results

    def send(self, x, axis, bit):
        return swap(self.behind(x), axis, bit)


def per_device(inputs, cotangent, in_proj, out_proj, decays, input_scale, retain):
    rows, depth = inputs.shape
    channels = in_proj.shape[1]
    devices, lanes = lax.axis_size("tm"), lax.axis_size("chan")
    scaling = 1.0 / math.sqrt(rows * devices)
    me, lane = lax.axis_index("tm"), lax.axis_index("chan")
    far = devices // 2
    groups = devices // 4
    steps = rows // SEG
    scale = input_scale[None, :]
    decay_row = decays[None, :]
    side = me // far

    half, quarter = rows // 2, rows // 4
    rows_out = depth // devices
    core = lane % 2
    idx = [core, lane, side, 1 - side]
    idx += [core, 1 - core, lane, lane ^ 2, lane ^ 1, lane ^ 3, 2 * core, 2 * core + 1, 2 - 2 * core, 3 - 2 * core]
    idx += [me, me ^ 1, me ^ far, me ^ far ^ 1, me]
    idx += [me ^ (2 * k) for k in range(groups)] + [(me % far) ^ (2 * k) for k in range(groups)]
    idx, inputs, cotangent = lax.optimization_barrier((jnp.stack(idx).astype(jnp.int32), inputs, cotangent))
    mine_near, mine_1, mine_2, mine_3, mine_4 = (
        [(0, 0, half)], [(1, 2, quarter)], [(1, 3, quarter)], [(2, 2, quarter)], [(2, 3, quarter)],
    )
    their_near, their_1, their_2, their_3, their_4 = (
        [(0, 1, half)], [(1, 4, quarter)], [(1, 5, quarter)], [(2, 4, quarter)], [(2, 5, quarter)],
    )

    line = Order()
    x_own, x_half, x_quarter = line.step(
        *prep(prep_inputs_kernel, idx, inputs, [((half, depth), F32), ((quarter, depth), F32)], "prep_inputs")
    )
    near_x = line.send(x_half, "tm", 1)
    away_x = line.send(x_quarter, "tm", far)
    part = ((quarter, depth // 2), F32)
    c_own, own_a, c_first_a, c_second_a, c_half_b, c_quarter_a, c_quarter_b = prep(
        prep_cotangent_kernel, idx, line.behind(cotangent),
        [((rows, depth // 2), BF16), part, part, ((half, depth // 2), F32), part, part], "prep_cotangent",
    )
    table = resident(
        functools.partial(summary_kernel, scaling=scaling), jax.ShapeDtypeStruct((1, 4, channels), F32),
        (x_own, c_own, in_proj, out_proj, scale, decay_row, retain[None, :]), "summary",
        [pltpu.VMEM((rows, channels), F32)] * 2 + [pltpu.VMEM((rows, 128), F32)], scalars=0,
    )
    if groups == 2:
        table = jnp.concatenate([table] + [line.send(table, "tm", bit) for bit in (2, 4, 6)])
    else:
        for bit in reach(devices)[:-1]:
            table = jnp.concatenate([table, line.send(table, "tm", bit)])
    near_x, away_x, table = line.step(near_x, away_x, table)

    corner_x = line.send(away_x, "tm", 1)
    side_x = line.send(away_x, "chan", 2)
    away_a = line.send(c_quarter_a, "tm", far)
    table = jnp.concatenate([table, line.send(table, "tm", reach(devices)[-1])])
    enter_fwd, enter_bwd, retain_wide = carries(idx, table, rows)
    corner_x, side_x, away_a, enter_fwd = line.step(corner_x, side_x, away_a, enter_fwd)

    mixed_a = line.send(pack([c_first_a, line.behind(away_a)], "pack_mixed"), "tm", 1)
    corner_side_x = line.send(corner_x, "chan", 2)
    away_b = line.send(c_quarter_b, "tm", far)
    forward = (in_proj, scale, decay_row, retain_wide, enter_fwd)
    backward = (out_proj, scale, decay_row, retain_wide, enter_bwd)
    starts, lows = forward_call(idx, 0, [x_own], forward, "forward_own")
    scaled, grads = backward_call(idx, 0, [[c_own]], backward, starts, lows, scaling, "backward_own")
    keep, give = row_grad(idx, scaled[0], in_proj, lanes)
    other_x = line.send(pack([near_x, away_x, side_x, corner_x], "pack_x"), "chan", 1)
    corner_side_x, mixed_a, away_b, give, other_x = line.step(corner_side_x, mixed_a, away_b, give, other_x)

    mixed_b = line.send(pack([c_second_a, line.behind(away_b)], "pack_mixed"), "tm", 1)
    far_a = pack([line.behind(away_a), (mixed_a, quarter, quarter)], "pack_far")
    side_a = line.send(far_a, "chan", 2)
    last_x = line.send(corner_side_x, "chan", 1)
    xs = [x_own] + collected(idx, [
        (near_x, mine_near), (away_x, mine_1), (side_x, mine_2), (corner_x, mine_3), (corner_side_x, mine_4),
        (other_x, their_near + their_1 + their_2 + their_3), (last_x, their_4),
    ], "collect_x")
    more, more_low = forward_call(idx, 1, xs[1:], forward, "forward_group")
    starts, lows = starts + more, lows + more_low
    side_a, mixed_b, lows[1] = line.step(side_a, mixed_b, lows[1])

    far_b = pack([line.behind(away_b), (mixed_b, quarter, quarter)], "pack_far")
    side_b = line.send(far_b, "chan", 2)
    near_b = line.send(c_half_b, "tm", 1)
    rest_a = pack([(mixed_a, 0, quarter), (mixed_b, 0, quarter), side_a], "pack_rest")
    far_a_other = line.send(far_a, "chan", 1)
    rest_a_other = line.send(rest_a, "chan", 1)
    ca = [own_a] + collected(idx, [
        (far_a, mine_1 + mine_3), (rest_a, [(0, 6, quarter), (0, 7, quarter)] + mine_2 + mine_4),
        (far_a_other, their_1 + their_3), (rest_a_other, [(0, 8, quarter), (0, 9, quarter)] + their_2 + their_4),
    ], "collect_a")

    def shares(first, features, values, factor, name, sums=()):
        return [grad_rows(idx, first + k, features, values, rows_out, factor, name, sums) for k in range(1, groups)]

    out_given = shares(ROWS + groups, ca, lows, scaling, "out_grad")
    out_given[0] = line.step(out_given[0])

    out_got = [line.send(part, "tm", 2 * (k + 1)) for k, part in enumerate(out_given)]
    near_b, side_b = line.step(near_b, side_b)

    near_b_other = line.send(near_b, "chan", 1)
    far_b_other = line.send(far_b, "chan", 1)
    side_b_other = line.send(side_b, "chan", 1)
    cb = collected(idx, [
        (near_b, mine_near), (far_b, mine_1 + mine_3), (side_b, mine_2 + mine_4),
        (near_b_other, their_near), (far_b_other, their_1 + their_3), (side_b_other, their_2 + their_4),
    ], "collect_b")
    cs = [list(pair) for pair in zip(ca[1:], cb, strict=True)]
    more, more_grads = backward_call(idx, 1, cs, backward, starts[1:], lows[1:], scaling, "backward_group")
    scaled, grads = scaled + more, grads + more_grads
    in_given = shares(ROWS, xs, scaled, None, "in_grad", grads)
    in_given[0] = line.step(in_given[0])
    in_got = [line.send(part, "tm", 2 * (k + 1)) for k, part in enumerate(in_given)]
    out_got[0] = line.step(out_got[0])
    parts = keep + line.send(give, "chan", 1)
    columns = parts[0] + line.send(parts[1], "chan", 2)
    input_grad = columns.astype(BF16)
    in_got[0] = after(in_got[0], input_grad)

    out_proj_grad = sum(out_got, grad_rows(idx, ROWS + groups, [line.behind(ca[0]), *ca[1:]], lows, rows_out, scaling, "out_grad"))
    in_mine = grad_rows(idx, ROWS, [line.behind(xs[0]), *xs[1:]], scaled, rows_out, None, "in_grad", grads)
    in_proj_grad = sum((part[:rows_out] for part in in_got), in_mine[:rows_out])
    decay_grad = sum((part[rows_out] for part in in_got), in_mine[rows_out])
    if groups > 2:
        decay_grad = in_mine[rows_out]
        bit = 2
        while bit < far:
            decay_grad += swap(decay_grad, "tm", bit)
            bit *= 2
    return (in_proj_grad, out_proj_grad, decay_grad, input_grad)


def solution(mesh):
    return jax.shard_map(
        per_device,
        mesh=mesh,
        in_specs=(
            P("tm", None),
            P("tm", None),
            P(None, "chan"),
            P("chan", None),
            P("chan"),
            P("chan"),
            P("tm"),
        ),
        out_specs=(P("tm", "chan"), P("tm", "chan"), P("chan"), P("tm", "chan")),
        check_vma=False,
    )
```

```python
import functools
import math

import jax
import jax.numpy as jnp
from jax import lax
from jax.experimental import pallas as pl
from jax.experimental.pallas import tpu as pltpu
from jax.sharding import PartitionSpec as P

F32 = jnp.float32
BF16 = jnp.bfloat16
SEG = 8
CORE, LANE, SIDES, PLACES, BLOCKS, SELF, ROWS = 0, 1, 2, 4, 14, 18, 19
VMEM_LIMIT = 12 * 1024 * 1024


def swap(x, axis, bit):
    n = lax.axis_size(axis)
    return lax.ppermute(x, axis, [(k, k ^ bit) for k in range(n)])


def nn(a, b):
    return lax.dot_general(a, b, (((1,), (0,)), ((), ())), preferred_element_type=F32)


def nt(a, b):
    return lax.dot_general(a, b, (((1,), (1,)), ((), ())), preferred_element_type=F32)


def tn(a, b):
    return lax.dot_general(a, b, (((0,), (0,)), ((), ())), preferred_element_type=F32)


def order_of(rows, transpose=False):
    steps = rows // SEG
    r = lax.broadcasted_iota(jnp.int32, (rows, rows), 1 if transpose else 0)
    t = lax.broadcasted_iota(jnp.int32, (rows, rows), 0 if transpose else 1)
    return (r % SEG) * steps + r // SEG == t


def order(rows, transpose=False):
    return order_of(rows, transpose).astype(F32).astype(BF16)


VMEM = pl.BlockSpec(memory_space=pltpu.VMEM)
SMEM = pl.BlockSpec(memory_space=pltpu.SMEM)


ANY = pl.BlockSpec(memory_space=pl.ANY)


def resident(kernel, out_shape, operands, name, scratch=(), scalars=1, anywhere=0):
    return pl.pallas_call(
        kernel,
        out_shape=out_shape,
        in_specs=[SMEM] * scalars + [VMEM] * (len(operands) - scalars - anywhere) + [ANY] * anywhere,
        out_specs=jax.tree.map(lambda _: VMEM, out_shape),
        scratch_shapes=scratch,
        compiler_params=pltpu.CompilerParams(vmem_limit_bytes=VMEM_LIMIT),
        cost_estimate=pl.CostEstimate(flops=0, transcendentals=0, bytes_accessed=0),
        name=name,
    )(*operands)


def ordered_rows(x_ref, p_ref, full):
    full[...] = nn(order(x_ref.shape[0]), x_ref[...])
    p_ref[...] = full[...].astype(BF16)


def prep_inputs_kernel(idx_ref, x_ref, p_ref, half_ref, quarter_ref, full):
    ordered_rows(x_ref, p_ref, full)
    half, quarter = half_ref.shape[0], quarter_ref.shape[0]
    half_ref[...] = full[pl.ds(pl.multiple_of(idx_ref[CORE] * half, half), half), :]
    quarter_ref[...] = full[pl.ds(pl.multiple_of(idx_ref[LANE] * quarter, quarter), quarter), :]


def prep_cotangent_kernel(idx_ref, x_ref, p_ref, own_a_ref, first_a_ref, second_a_ref, half_b_ref, away_a_ref, away_b_ref, full):
    ordered_rows(x_ref, p_ref, full)
    quarter, width = first_a_ref.shape
    cols = [pl.ds(pl.multiple_of(idx_ref[SIDES + k] * width, width), width) for k in range(2)]
    first = pl.ds(pl.multiple_of(idx_ref[CORE] * 2 * quarter, quarter), quarter)
    second = pl.ds(pl.multiple_of(idx_ref[CORE] * 2 * quarter + quarter, quarter), quarter)
    away = pl.ds(pl.multiple_of(idx_ref[LANE] * quarter, quarter), quarter)
    own_a_ref[...] = full[:, cols[0]].astype(BF16)
    first_a_ref[...] = full[first, cols[0]]
    second_a_ref[...] = full[second, cols[0]]
    half_b_ref[...] = full[pl.ds(pl.multiple_of(idx_ref[CORE] * 2 * quarter, quarter), 2 * quarter), cols[1]]
    away_a_ref[...] = full[away, cols[1]]
    away_b_ref[...] = full[away, cols[0]]


def prep(kernel, idx, x, shapes, name):
    rows, depth = x.shape
    shapes = [jax.ShapeDtypeStruct(shape, kind) for shape, kind in shapes]
    return resident(kernel, (jax.ShapeDtypeStruct((rows, depth), BF16), *shapes), (idx, x), name, [pltpu.VMEM((rows, depth), F32)])


def pack_kernel(*refs, spans):
    *pieces, out_ref, sems = refs
    copies, at = [], 0
    for k, (ref, (start, rows)) in enumerate(zip(pieces, spans, strict=True)):
        copies.append(pltpu.make_async_copy(ref.at[pl.ds(start, rows), :], out_ref.at[pl.ds(at, rows), :], sems.at[k]))
        at += rows
    for copy in copies:
        copy.start()
    for copy in copies:
        copy.wait()


def pack(pieces, name):
    pieces = [p if isinstance(p, tuple) else (p, 0, p.shape[0]) for p in pieces]
    shape = jax.ShapeDtypeStruct((sum(p[2] for p in pieces), pieces[0][0].shape[1]), F32)
    kernel = functools.partial(pack_kernel, spans=[p[1:] for p in pieces])
    arrays = tuple(p[0] for p in pieces)
    return resident(kernel, shape, arrays, name, [pltpu.SemaphoreType.DMA((len(pieces),))], scalars=0, anywhere=len(pieces))


def lanes_of(l):
    return slice(128 * l, 128 * (l + 1))


def scan_ends(src, retain_ref, base, decays, reverse):
    count, steps = src.shape[1] // 128, src.shape[0] // SEG

    def lap(k, carry):
        j = steps - 1 - k if reverse else k
        rows = pl.ds(pl.multiple_of(j * SEG, SEG), SEG)
        kept = retain_ref[pl.ds(pl.multiple_of(base + j * SEG, SEG), SEG), :]
        out = []
        for l in range(count):
            end, rate = carry[l]
            factor = kept * decays[l]
            value = src[rows, lanes_of(l)]
            end = factor * (value + end) if reverse else factor * end + value
            out.append((end, factor * rate))
        return tuple(out)

    start = tuple((jnp.zeros((SEG, 128), F32), jnp.ones((SEG, 128), F32)) for _ in range(count))
    ends = lax.fori_loop(0, steps, lap, start, unroll=4)
    return jnp.concatenate([e[0] for e in ends], axis=1), jnp.concatenate([e[1] for e in ends], axis=1)


def seg_starts(end, rate, entering, reverse):
    now = entering
    starts = [None] * SEG
    for k in range(SEG):
        s = SEG - 1 - k if reverse else k
        starts[s] = now
        now = end[s : s + 1] + rate[s : s + 1] * now
    return jnp.concatenate(starts, axis=0), now


def decay_tiles(decay_ref):
    width = decay_ref.shape[1]
    full = jnp.broadcast_to(decay_ref[...], (SEG, width))
    return [full[:, lanes_of(l)] for l in range(width // 128)]


def spread_rows(row, out_ref, at):
    rows = row.shape[1]
    column = jnp.sum(jnp.where(order_of(rows), row, 0.0), axis=1, keepdims=True)
    out_ref[at : at + rows, :] = jnp.broadcast_to(column, (rows, 128))


def summary_kernel(x_ref, c_ref, w_ref, v_ref, scale_ref, decay_ref, kept_ref, out_ref, drive, scot, retain_ref, *, scaling):
    decays = decay_tiles(decay_ref)
    spread_rows(kept_ref[...], retain_ref, 0)
    drive[...] = nn(x_ref[...], w_ref[...]) * scale_ref[...]
    scot[...] = nt(c_ref[...], v_ref[...]) * scaling
    zero = jnp.zeros(decay_ref.shape, F32)
    end, rate = scan_ends(drive, retain_ref, 0, decays, False)
    _, forward = seg_starts(end, rate, zero, False)
    back, _ = scan_ends(scot, retain_ref, 0, decays, True)
    _, backward = seg_starts(back, rate, zero, True)
    total = rate[0:1]
    for s in range(1, SEG):
        total = total * rate[s : s + 1]
    rest = zero.shape[1] - kept_ref.shape[1]
    kept = jnp.concatenate([kept_ref[...], zero[:, :rest]], axis=1) if rest else kept_ref[...]
    out_ref[0] = jnp.concatenate([total, forward, backward, kept], axis=0)


def carries_kernel(idx_ref, sum_ref, fwd_ref, bwd_ref, retain_ref):
    blocks = sum_ref.shape[0]
    far = blocks // 2
    rows = retain_ref.shape[0] // 4

    def row(away):
        return sum_ref[(away % 2) * far + away // 2]

    for role, away in enumerate((0, 1, far, far + 1)):
        spread_rows(row(away)[3:4, :rows], retain_ref, role * rows)
    now = jnp.zeros_like(fwd_ref[0:1, :])
    for b in range(blocks):
        fwd_ref[b : b + 1, :] = now
        ends = row(idx_ref[SELF] ^ b)
        now = ends[1:2] + ends[0:1] * now
    now = jnp.zeros_like(now)
    for b in range(blocks - 1, -1, -1):
        bwd_ref[b : b + 1, :] = now
        ends = row(idx_ref[SELF] ^ b)
        now = ends[2:3] + ends[0:1] * now


def carries(idx, table, rows):
    shape = jax.ShapeDtypeStruct((table.shape[0], table.shape[2]), F32)
    return resident(carries_kernel, (shape, shape, jax.ShapeDtypeStruct((4 * rows, 128), F32)), (idx, table), "carries")


def reach(devices):
    return [1 << k for k in range(1, devices.bit_length() - 1)] + [1]


def collect_kernel(idx_ref, *refs, layout):
    count = len(layout)
    outs = refs[count : count + 3]
    held, sems = refs[count + 3], refs[count + 4]
    copies, at = [], 0
    for k, ref in enumerate(refs[:count]):
        copies.append(pltpu.make_async_copy(ref, held.at[pl.ds(at, ref.shape[0]), :], sems.at[k]))
        at += ref.shape[0]
    for copy in copies:
        copy.start()
    start = 0
    for copy, parts in zip(copies, layout, strict=True):
        copy.wait()
        for role, slot, rows in parts:
            at = pl.multiple_of(idx_ref[PLACES + slot] * rows, rows)
            outs[role][pl.ds(at, rows), :] = held[start : start + rows, :].astype(BF16)
            start += rows


def collected(idx, pieces, name):
    rows = sum(part[2] for _, parts in pieces for part in parts)
    depth = pieces[0][0].shape[1]
    shape = jax.ShapeDtypeStruct((rows // 3, depth), BF16)
    kernel = functools.partial(collect_kernel, layout=[parts for _, parts in pieces])
    scratch = [pltpu.VMEM((rows, depth), F32), pltpu.SemaphoreType.DMA((len(pieces),))]
    return list(resident(kernel, (shape,) * 3, (idx, *[array for array, _ in pieces]), name, scratch, anywhere=len(pieces)))


def forward_kernel(idx_ref, *refs, roles, first):
    xs = refs[:roles]
    w_ref, scale_ref, decay_ref, retain_ref, enter_ref = refs[roles : roles + 5]
    outs = refs[roles + 5 : -2]
    drive, state = refs[-2:]
    decays = decay_tiles(decay_ref)
    count = len(decays)
    rows_all = drive.shape[0]
    steps = rows_all // SEG
    for role in range(roles):
        start_ref, low_ref = outs[2 * role : 2 * role + 2]
        block = idx_ref[BLOCKS + first + role]
        base = (first + role) * rows_all
        drive[...] = nn(xs[role][...], w_ref[...]) * scale_ref[...]
        end, rate = scan_ends(drive, retain_ref, base, decays, False)
        start, _ = seg_starts(end, rate, enter_ref[pl.ds(block, 1), :], False)
        start_ref[...] = start

        def lap(j, before, base=base):
            at = pl.multiple_of(j * SEG, SEG)
            kept = retain_ref[pl.ds(pl.multiple_of(base + j * SEG, SEG), SEG), :]
            out = []
            for l in range(count):
                now = kept * decays[l] * before[l] + drive[pl.ds(at, SEG), lanes_of(l)]
                state[pl.ds(at, SEG), lanes_of(l)] = now
                out.append(now)
            return tuple(out)

        lax.fori_loop(0, steps, lap, tuple(start[:, lanes_of(l)] for l in range(count)), unroll=4)
        low_ref[...] = state[...].astype(BF16)


def backward_kernel(idx_ref, *refs, roles, parts, scaling, first):
    cs = refs[: roles * parts]
    v_ref, scale_ref, decay_ref, retain_ref, enter_ref = refs[roles * parts : roles * parts + 5]
    entering = refs[roles * parts + 5 : roles * parts + 5 + 2 * roles]
    outs = refs[roles * parts + 5 + 2 * roles : -3]
    scot, adjoint, track = refs[-3:]
    decays = decay_tiles(decay_ref)
    count = len(decays)
    rows_all = scot.shape[0]
    steps = rows_all // SEG
    width = v_ref.shape[1] // parts
    for role in range(roles):
        scaled_ref, grad_ref = outs[2 * role : 2 * role + 2]
        block = idx_ref[BLOCKS + first + role]
        base = (first + role) * rows_all
        if parts == 1:
            scot[...] = nt(cs[role][...], v_ref[...]) * scaling
        else:
            total = None
            for k in range(parts):
                cols = pl.ds(pl.multiple_of(idx_ref[SIDES + k] * width, width), width)
                part = nt(cs[parts * role + k][...], v_ref[:, cols])
                total = part if total is None else total + part
            scot[...] = total * scaling
        end, rate = scan_ends(scot, retain_ref, base, decays, True)
        start, _ = seg_starts(end, rate, enter_ref[pl.ds(block, 1), :], True)

        start_ref, low_ref = entering[2 * role : 2 * role + 2]
        track[0:SEG, :] = start_ref[...]
        track[SEG:, :] = low_ref[...].astype(F32)

        def lap(k, carry, base=base):
            at = (steps - 1 - k) * SEG
            rows = pl.ds(pl.multiple_of(at, SEG), SEG)
            kept = retain_ref[pl.ds(pl.multiple_of(base + at, SEG), SEG), :]
            out = []
            for l in range(count):
                follow, grad = carry[l]
                here = scot[rows, lanes_of(l)] + follow
                adjoint[rows, lanes_of(l)] = here
                part = kept * here
                out.append((part * decays[l], grad + part * track[rows, lanes_of(l)]))
            return tuple(out)

        begin = tuple((start[:, lanes_of(l)], jnp.zeros((SEG, 128), F32)) for l in range(count))
        done = lax.fori_loop(0, steps, lap, begin, unroll=4)
        scaled_ref[...] = (adjoint[...] * scale_ref[...]).astype(BF16)
        grad_ref[...] = jnp.sum(jnp.concatenate([d[1] for d in done], axis=1), axis=0, keepdims=True)


def forward_call(idx, first, xs, operands, name):
    channels = operands[1].shape[1]
    rows, roles = xs[0].shape[0], len(xs)
    shapes = (jax.ShapeDtypeStruct((SEG, channels), F32), jax.ShapeDtypeStruct((rows, channels), BF16)) * roles
    out = resident(
        functools.partial(forward_kernel, roles=roles, first=first), shapes, (idx, *xs, *operands), name,
        [pltpu.VMEM((rows, channels), F32)] * 2,
    )
    return list(out[::2]), list(out[1::2])


def backward_call(idx, first, cs, operands, starts, lows, scaling, name):
    channels = operands[1].shape[1]
    rows, roles = cs[0][0].shape[0], len(cs)
    kernel = functools.partial(backward_kernel, roles=roles, parts=len(cs[0]), scaling=scaling, first=first)
    shapes = (jax.ShapeDtypeStruct((rows, channels), BF16), jax.ShapeDtypeStruct((1, channels), F32)) * roles
    out = resident(
        kernel, shapes, (idx, *[part for c in cs for part in c], *operands, *[r for pair in zip(starts, lows, strict=True) for r in pair]), name,
        [pltpu.VMEM((rows, channels), F32)] * 2 + [pltpu.VMEM((SEG + rows, channels), F32)],
    )
    return list(out[::2]), list(out[1::2])


def grad_kernel(idx_ref, *refs, count, factor, which):
    features, values, sums, out_ref = refs[:count], refs[count : 2 * count], refs[2 * count : -1], refs[-1]
    width = out_ref.shape[0] - (SEG if sums else 0)
    at = pl.ds(pl.multiple_of(idx_ref[which] * width, width), width)
    total = tn(features[0][:, at], values[0][...])
    for k in range(1, count):
        total += tn(features[k][:, at], values[k][...])
    out_ref[0:width, :] = total * factor if factor is not None else total
    if sums:
        row = (sums[0][...] + sums[1][...]) + (sums[2][...] + sums[3][...])
        out_ref[width:, :] = jnp.broadcast_to(row, (SEG, row.shape[1]))


def grad_rows(idx, which, features, values, rows_out, factor, name, sums=()):
    channels = values[0].shape[1]
    if rows_out % 128:
        total = sum(
            tn(lax.dynamic_slice_in_dim(x, idx[which] * rows_out, rows_out, axis=1), v) for x, v in zip(features, values, strict=True)
        )
        total = total * factor if factor is not None else total
        if sums:
            row = (sums[0] + sums[1]) + (sums[2] + sums[3])
            total = jnp.concatenate([total, jnp.broadcast_to(row, (SEG, channels))], axis=0)
        return total
    return resident(
        functools.partial(grad_kernel, count=len(values), factor=factor, which=which),
        jax.ShapeDtypeStruct((rows_out + (SEG if sums else 0), channels), F32),
        (idx, *features, *values, *sums), name,
    )


def row_grad_kernel(idx_ref, a_ref, w_ref, keep_ref, give_ref):
    count, rows, width = keep_ref.shape
    a = nn(order(rows, True), a_ref[...]).astype(BF16)
    for k in range(count):
        for ref, flip in ((keep_ref, 0), (give_ref, 1)):
            at = (idx_ref[LANE] ^ (2 * k) ^ flip) * width
            ref[k] = nt(a, w_ref[pl.ds(pl.multiple_of(at, width), width), :])


def row_grad(idx, scaled, in_proj, parts):
    rows, channels = scaled.shape
    shape = jax.ShapeDtypeStruct((parts // 2, rows, in_proj.shape[0] // parts), F32)
    return resident(row_grad_kernel, (shape, shape), (idx, scaled, in_proj), "row_grad")


def after(x, *others):
    return lax.optimization_barrier((x, *others))[0]


class Order:
    def __init__(self):
        self.last = None

    def behind(self, x):
        return x if self.last is None else lax.optimization_barrier((x, self.last))[0]

    def step(self, *results):
        held = results if self.last is None else (*results, self.last)
        results = lax.optimization_barrier(held)[: len(results)]
        self.last = results[0]
        return results[0] if len(results) == 1 else results

    def send(self, x, axis, bit):
        return swap(self.behind(x), axis, bit)


def per_device(inputs, cotangent, in_proj, out_proj, decays, input_scale, retain):
    rows, depth = inputs.shape
    channels = in_proj.shape[1]
    devices, lanes = lax.axis_size("tm"), lax.axis_size("chan")
    scaling = 1.0 / math.sqrt(rows * devices)
    me, lane = lax.axis_index("tm"), lax.axis_index("chan")
    far = devices // 2
    groups = devices // 4
    steps = rows // SEG
    scale = input_scale[None, :]
    decay_row = decays[None, :]
    side = me // far

    half, quarter = rows // 2, rows // 4
    rows_out = depth // devices
    core = lane % 2
    idx = [core, lane, side, 1 - side]
    idx += [core, 1 - core, lane, lane ^ 2, lane ^ 1, lane ^ 3, 2 * core, 2 * core + 1, 2 - 2 * core, 3 - 2 * core]
    idx += [me, me ^ 1, me ^ far, me ^ far ^ 1, me]
    idx += [me ^ (2 * k) for k in range(groups)] + [(me % far) ^ (2 * k) for k in range(groups)]
    idx, inputs, cotangent = lax.optimization_barrier((jnp.stack(idx).astype(jnp.int32), inputs, cotangent))
    mine_near, mine_1, mine_2, mine_3, mine_4 = (
        [(0, 0, half)], [(1, 2, quarter)], [(1, 3, quarter)], [(2, 2, quarter)], [(2, 3, quarter)],
    )
    their_near, their_1, their_2, their_3, their_4 = (
        [(0, 1, half)], [(1, 4, quarter)], [(1, 5, quarter)], [(2, 4, quarter)], [(2, 5, quarter)],
    )

    line = Order()
    x_own, x_half, x_quarter = line.step(
        *prep(prep_inputs_kernel, idx, inputs, [((half, depth), F32), ((quarter, depth), F32)], "prep_inputs")
    )
    near_x = line.send(x_half, "tm", 1)
    away_x = line.send(x_quarter, "tm", far)
    part = ((quarter, depth // 2), F32)
    c_own, own_a, c_first_a, c_second_a, c_half_b, c_quarter_a, c_quarter_b = prep(
        prep_cotangent_kernel, idx, line.behind(cotangent),
        [((rows, depth // 2), BF16), part, part, ((half, depth // 2), F32), part, part], "prep_cotangent",
    )
    table = resident(
        functools.partial(summary_kernel, scaling=scaling), jax.ShapeDtypeStruct((1, 4, channels), F32),
        (x_own, c_own, in_proj, out_proj, scale, decay_row, retain[None, :]), "summary",
        [pltpu.VMEM((rows, channels), F32)] * 2 + [pltpu.VMEM((rows, 128), F32)], scalars=0,
    )
    if groups == 2:
        table = jnp.concatenate([table] + [line.send(table, "tm", bit) for bit in (2, 4, 6)])
    else:
        for bit in reach(devices)[:-1]:
            table = jnp.concatenate([table, line.send(table, "tm", bit)])
    near_x, away_x, table = line.step(near_x, away_x, table)

    corner_x = line.send(away_x, "tm", 1)
    side_x = line.send(away_x, "chan", 2)
    away_a = line.send(c_quarter_a, "tm", far)
    table = jnp.concatenate([table, line.send(table, "tm", reach(devices)[-1])])
    enter_fwd, enter_bwd, retain_wide = carries(idx, table, rows)
    corner_x, side_x, away_a, enter_fwd = line.step(corner_x, side_x, away_a, enter_fwd)

    mixed_a = line.send(pack([c_first_a, line.behind(away_a)], "pack_mixed"), "tm", 1)
    corner_side_x = line.send(corner_x, "chan", 2)
    away_b = line.send(c_quarter_b, "tm", far)
    forward = (in_proj, scale, decay_row, retain_wide, enter_fwd)
    backward = (out_proj, scale, decay_row, retain_wide, enter_bwd)
    starts, lows = forward_call(idx, 0, [x_own], forward, "forward_own")
    scaled, grads = backward_call(idx, 0, [[c_own]], backward, starts, lows, scaling, "backward_own")
    keep, give = row_grad(idx, scaled[0], in_proj, lanes)
    other_x = line.send(pack([near_x, away_x, side_x, corner_x], "pack_x"), "chan", 1)
    corner_side_x, mixed_a, away_b, give, other_x = line.step(corner_side_x, mixed_a, away_b, give, other_x)

    mixed_b = line.send(pack([c_second_a, line.behind(away_b)], "pack_mixed"), "tm", 1)
    far_a = pack([line.behind(away_a), (mixed_a, quarter, quarter)], "pack_far")
    side_a = line.send(far_a, "chan", 2)
    last_x = line.send(corner_side_x, "chan", 1)
    xs = [x_own] + collected(idx, [
        (near_x, mine_near), (away_x, mine_1), (side_x, mine_2), (corner_x, mine_3), (corner_side_x, mine_4),
        (other_x, their_near + their_1 + their_2 + their_3), (last_x, their_4),
    ], "collect_x")
    more, more_low = forward_call(idx, 1, xs[1:], forward, "forward_group")
    starts, lows = starts + more, lows + more_low
    side_a, mixed_b, lows[1] = line.step(side_a, mixed_b, lows[1])

    far_b = pack([line.behind(away_b), (mixed_b, quarter, quarter)], "pack_far")
    side_b = line.send(far_b, "chan", 2)
    near_b = line.send(c_half_b, "tm", 1)
    rest_a = pack([(mixed_a, 0, quarter), (mixed_b, 0, quarter), side_a], "pack_rest")
    far_a_other = line.send(far_a, "chan", 1)
    given = line.send(give, "chan", 1)
    rest_a_other = line.send(rest_a, "chan", 1)
    ca = [own_a] + collected(idx, [
        (far_a, mine_1 + mine_3), (rest_a, [(0, 6, quarter), (0, 7, quarter)] + mine_2 + mine_4),
        (far_a_other, their_1 + their_3), (rest_a_other, [(0, 8, quarter), (0, 9, quarter)] + their_2 + their_4),
    ], "collect_a")

    def shares(first, features, values, factor, name, sums=()):
        return [grad_rows(idx, first + k, features, values, rows_out, factor, name, sums) for k in range(1, groups)]

    out_given = shares(ROWS + groups, ca, lows, scaling, "out_grad")
    out_given[0], given = line.step(out_given[0], given)

    out_got = [line.send(part, "tm", 2 * (k + 1)) for k, part in enumerate(out_given)]
    near_b, side_b = line.step(near_b, side_b)

    near_b_other = line.send(near_b, "chan", 1)
    far_b_other = line.send(far_b, "chan", 1)
    side_b_other = line.send(side_b, "chan", 1)
    cb = collected(idx, [
        (near_b, mine_near), (far_b, mine_1 + mine_3), (side_b, mine_2 + mine_4),
        (near_b_other, their_near), (far_b_other, their_1 + their_3), (side_b_other, their_2 + their_4),
    ], "collect_b")
    cs = [list(pair) for pair in zip(ca[1:], cb, strict=True)]
    more, more_grads = backward_call(idx, 1, cs, backward, starts[1:], lows[1:], scaling, "backward_group")
    scaled, grads = scaled + more, grads + more_grads
    in_given = shares(ROWS, xs, scaled, None, "in_grad", grads)
    in_given[0] = line.step(in_given[0])
    in_got = [line.send(part, "tm", 2 * (k + 1)) for k, part in enumerate(in_given)]
    out_got[0] = line.step(out_got[0])
    parts = keep + given
    columns = parts[0] + line.send(parts[1], "chan", 2)
    input_grad = columns.astype(BF16)
    in_got[0] = after(in_got[0], input_grad)

    out_proj_grad = sum(out_got, grad_rows(idx, ROWS + groups, [line.behind(ca[0]), *ca[1:]], lows, rows_out, scaling, "out_grad"))
    in_mine = grad_rows(idx, ROWS, [line.behind(xs[0]), *xs[1:]], scaled, rows_out, None, "in_grad", grads)
    in_proj_grad = sum((part[:rows_out] for part in in_got), in_mine[:rows_out])
    decay_grad = sum((part[rows_out] for part in in_got), in_mine[rows_out])
    if groups > 2:
        decay_grad = in_mine[rows_out]
        bit = 2
        while bit < far:
            decay_grad += swap(decay_grad, "tm", bit)
            bit *= 2
    return (in_proj_grad, out_proj_grad, decay_grad, input_grad)


def solution(mesh):
    return jax.shard_map(
        per_device,
        mesh=mesh,
        in_specs=(
            P("tm", None),
            P("tm", None),
            P(None, "chan"),
            P("chan", None),
            P("chan"),
            P("chan"),
            P("tm"),
        ),
        out_specs=(P("tm", "chan"), P("tm", "chan"), P("chan"), P("tm", "chan")),
        check_vma=False,
    )
```
